32 devices in a mesh: dp: 8 (over y, x, core), seq: 4 (over z).
Axes of the slice: x: 2, y: 2, z: 4, core: 2. Of those that a mesh axis runs over, the one named last changes fastest.
Arguments:
- inputs: bfloat16 [16, 2048, 1024], P('dp', 'seq'), may hold values from -6 to 6
- cotangent: bfloat16 [16, 2048, 1024], P('dp', 'seq'), may hold values from -6 to 6
- segment_ids: int32 [16, 2048], P('dp'), may hold values from 0 to 21, as said below
- query_weight: bfloat16 [1024, 1024], P(('dp', 'seq')), may hold values from -0.1875 to 0.1875
- key_weight: bfloat16 [1024, 1024], P(('dp', 'seq')), may hold values from -0.1875 to 0.1875
- value_weight: bfloat16 [1024, 1024], P(('dp', 'seq')), may hold values from -0.1875 to 0.1875
- output_weight: bfloat16 [1024, 1024], P(('dp', 'seq')), may hold values from -0.1875 to 0.1875
- up_weight: bfloat16 [1024, 4096], P(('dp', 'seq')), may hold values from -0.1875 to 0.1875
- down_weight: bfloat16 [4096, 1024], P(('dp', 'seq')), may hold values from -0.09375 to 0.09375
- first_gain: float32 [1024], replicated, may hold values from 0.25 to 1.75
- first_shift: float32 [1024], replicated, may hold values from -1 to 1
- query_bias: float32 [1024], replicated, may hold values from -1 to 1
- value_bias: float32 [1024], replicated, may hold values from -1 to 1
- head_scale: float32 [16], replicated, may hold values from 0.3 to 3
- output_bias: float32 [1024], replicated, may hold values from -1 to 1
- post_gain: float32 [1024], replicated, may hold values from 0.25 to 1.75
- post_shift: float32 [1024], replicated, may hold values from -1 to 1
- second_gain: float32 [1024], replicated, may hold values from 0.25 to 1.75
- second_shift: float32 [1024], replicated, may hold values from -1 to 1
- up_bias: float32 [4096], replicated, may hold values from -1 to 1
- middle_gain: float32 [4096], replicated, may hold values from 0.25 to 1.75
- middle_shift: float32 [4096], replicated, may hold values from -1 to 1
- down_bias: float32 [1024], replicated, may hold values from -1 to 1
Outputs:
- layer_output: bfloat16 [16, 2048, 1024], P('dp', 'seq')
- input_grad: bfloat16 [16, 2048, 1024], P('dp', 'seq')
- query_weight_grad: float32 [1024, 1024], P(('dp', 'seq'))
- key_weight_grad: float32 [1024, 1024], P(('dp', 'seq'))
- value_weight_grad: float32 [1024, 1024], P(('dp', 'seq'))
- output_weight_grad: float32 [1024, 1024], P(('dp', 'seq'))
- up_weight_grad: float32 [1024, 4096], P(('dp', 'seq'))
- down_weight_grad: float32 [4096, 1024], P(('dp', 'seq'))
- first_gain_grad: float32 [1024], replicated
- first_shift_grad: float32 [1024], replicated
- query_bias_grad: float32 [1024], replicated
- value_bias_grad: float32 [1024], replicated
- head_scale_grad: float32 [16], replicated
- output_bias_grad: float32 [1024], replicated
- post_gain_grad: float32 [1024], replicated
- post_shift_grad: float32 [1024], replicated
- second_gain_grad: float32 [1024], replicated
- second_shift_grad: float32 [1024], replicated
- up_bias_grad: float32 [4096], replicated
- middle_gain_grad: float32 [4096], replicated
- middle_shift_grad: float32 [4096], replicated
- down_bias_grad: float32 [1024], replicated
The draws below stay inside these ranges and needn't reach their ends.
Inputs may be any that keep to these rules, and one draw needn't show every extreme that they name: `segment_ids`: along each sequence the ids start at 0 and never fall; each document (a run of equal ids) has 60 to 800 positions, except the last of a sequence, which the sequence's end may cut short; in each sequence the first or the second document has exactly 800 positions; the last sequence reaches the largest id.
All inputs are finite; a program needn't handle non-finite values.
Results may differ from the reference program's by a relative error of at most 0.014.
Values may be sent and summed in bfloat16 or wider, within the bound.
A program may use at most 184 MiB of HBM per device.

```python
import math
import jax
import jax.numpy as jnp
from jax import lax

D = 1024
H = 16
FF = 4096
DOC_MIN = 60
DOC_MAX = 800
SEQ_LEN = 2048
SEQS = 16


def draw_segment_ids(key, part):
    doc_count = SEQ_LEN // DOC_MIN + 1
    length_key, pick_key = jax.random.split(key)
    lengths = jax.random.randint(length_key, (SEQS, doc_count), DOC_MIN, DOC_MAX + 1)
    last_row = jnp.arange(SEQS)[:, None] == SEQS - 1
    lengths = jnp.where(last_row, DOC_MIN, lengths)
    chosen = jax.random.randint(pick_key, (SEQS, 1), 0, 2)
    lengths = jnp.where(jnp.arange(doc_count)[None, :] == chosen, DOC_MAX, lengths)
    doc_ends = jnp.cumsum(lengths, axis=1)
    positions = jnp.arange(SEQ_LEN)
    passed = (doc_ends[:, None, :] <= positions[None, :, None]).astype(jnp.int32)
    return jnp.sum(passed, axis=-1).astype(jnp.int32)


def shard_levels(own_key, dims, shards, smallest, largest):
    loudness = 1.0
    for dim, shards_of in shards:
        steps = jax.random.uniform(jax.random.fold_in(jax.random.fold_in(own_key, 6), dim), (shards_of,), jnp.float32, smallest / len(shards), largest / len(shards))
        loudness = loudness * jnp.repeat(jnp.exp(steps), dims[dim] // shards_of).reshape((-1,) + (1,) * (len(dims) - 1 - dim))
    return loudness


def bell_draw(stream_key, extent, scale, bound, cuts=(), dtype=jnp.bfloat16):
    result = jax.random.normal(stream_key, extent, jnp.float32) * scale
    if len(cuts) > 0:
        result = shard_levels(stream_key, extent, cuts, -0.22, 0.18) * result
    return jnp.clip(result, min=-bound, max=bound).astype(dtype)


def setup_inputs(seed: int = 0) -> dict:
    splits = jax.random.split(jax.random.key(seed), 24)
    return {
        "inputs": bell_draw(splits[0], (SEQS, SEQ_LEN, D), 1.0, 6.0, ((0, 8), (1, 4))),
        "cotangent": bell_draw(splits[1], (SEQS, SEQ_LEN, D), 1.0, 6.0, ((0, 8), (1, 4))),
        "segment_ids": draw_segment_ids(jax.random.fold_in(splits[23], 71), 0),
        "query_weight": bell_draw(splits[3], (D, D), D ** -0.5, 0.1875, ((0, 32),)),
        "key_weight": bell_draw(splits[4], (D, D), D ** -0.5, 0.1875, ((0, 32),)),
        "value_weight": bell_draw(splits[5], (D, D), D ** -0.5, 0.1875, ((0, 32),)),
        "output_weight": bell_draw(splits[6], (D, D), D ** -0.5, 0.1875, ((0, 32),)),
        "up_weight": bell_draw(splits[7], (D, FF), D ** -0.5, 0.1875, ((0, 32),)),
        "down_weight": bell_draw(splits[8], (FF, D), FF ** -0.5, 0.09375, ((0, 32),)),
        "first_gain": jnp.clip(1.0 + 0.15 * jax.random.normal(splits[9], (D,), jnp.float32), 0.25, 1.75),
        "first_shift": bell_draw(splits[10], (D,), 0.2, 1.0, (), jnp.float32),
        "query_bias": bell_draw(splits[11], (D,), 0.2, 1.0, (), jnp.float32),
        "value_bias": bell_draw(splits[12], (D,), 0.2, 1.0, (), jnp.float32),
        "head_scale": jnp.clip(jnp.exp(jax.random.uniform(splits[13], (H,), jnp.float32, math.log(0.3), math.log(3.0))), 0.3, 3.0),
        "output_bias": bell_draw(splits[14], (D,), 0.2, 1.0, (), jnp.float32),
        "post_gain": jnp.clip(1.0 + 0.15 * jax.random.normal(splits[15], (D,), jnp.float32), 0.25, 1.75),
        "post_shift": bell_draw(splits[16], (D,), 0.2, 1.0, (), jnp.float32),
        "second_gain": jnp.clip(1.0 + 0.15 * jax.random.normal(splits[17], (D,), jnp.float32), 0.25, 1.75),
        "second_shift": bell_draw(splits[18], (D,), 0.2, 1.0, (), jnp.float32),
        "up_bias": bell_draw(splits[19], (FF,), 0.2, 1.0, (), jnp.float32),
        "middle_gain": jnp.clip(1.0 + 0.15 * jax.random.normal(splits[20], (FF,), jnp.float32), 0.25, 1.75),
        "middle_shift": bell_draw(splits[21], (FF,), 0.2, 1.0, (), jnp.float32),
        "down_bias": bell_draw(splits[22], (D,), 0.2, 1.0, (), jnp.float32),
    }


EPSILON = 1e-05
MASKED = -1e+30
HIGHEST_ACCURACY = lax.Precision.HIGHEST

@jax.custom_vjp
def low(v):
    return lax.optimization_barrier(v.astype(jnp.bfloat16)).astype(jnp.float32)

@jax.custom_vjp
def low_back(v):
    return v

def low_keep(v):
    return (low(v), None)

def low_pass(kept, grad):
    return (grad,)

def back_keep(v):
    return (v, None)

def back_low(kept, grad):
    return (low(grad),)
low.defvjp(low_keep, low_pass)
low_back.defvjp(back_keep, back_low)

def layer_norm(values, gain_vec, shift_vec):
    row_mean = lax.optimization_barrier(jnp.mean(values, -1, keepdims=True))
    centred = values - row_mean
    spread = lax.optimization_barrier(jnp.mean(centred * centred, -1, keepdims=True))
    return centred * lax.rsqrt(spread + EPSILON) * gain_vec + shift_vec

def matmul(left_side, right_side):
    return jnp.einsum('...i,ij->...j', left_side, right_side, precision=HIGHEST_ACCURACY)

def split_heads(matrix, head_count):
    return matrix.reshape(matrix.shape[0], matrix.shape[1], head_count, -1).transpose(2, 0, 1, 3)

def attend_heads(query_rows, key_rows, value_rows, allowed):
    logit_scale_factor = query_rows.shape[-1] ** (-0.5)

    def attend(packed):
        single_query_head, single_key_head, single_value_head = packed
        score_matrix = jnp.einsum('hvw,hcw->hvc', single_query_head, single_key_head, precision=HIGHEST_ACCURACY) * logit_scale_factor
        score_matrix = low_back(jnp.where(allowed, score_matrix, MASKED))
        attention_probabilities = low(jax.nn.softmax(score_matrix, axis=-1))
        return jnp.einsum('guo,gon->gun', attention_probabilities, single_value_head, precision=HIGHEST_ACCURACY)
    return lax.map(jax.checkpoint(attend), (query_rows, key_rows, value_rows))

def layer(tokens, segments, attention_probabilities):
    query_weight, key_weight, value_weight, output_weight, up_weight, down_weight, first_gain, first_shift, query_bias, value_bias, head_scale, output_bias, post_gain, post_shift, second_gain, second_shift, up_bias, middle_gain, middle_shift, down_bias = attention_probabilities
    head_count = head_scale.shape[0]
    positions = jnp.arange(tokens.shape[1])
    causal = positions[None, :] <= positions[:, None]
    allowed = causal[None] & (segments[:, None, :] == segments[:, :, None])
    normed = low(layer_norm(tokens, first_gain, first_shift))
    query_rows = low(low_back(matmul(normed, query_weight) + query_bias))
    key_rows = low(low_back(matmul(normed, key_weight)))
    value_rows = low(low_back(matmul(normed, value_weight) + value_bias))
    attended = attend_heads(split_heads(query_rows, head_count), split_heads(key_rows, head_count), split_heads(value_rows, head_count), allowed)
    attended = low_back(attended)
    scaled = low(attended * head_scale[:, None, None, None])
    merged = scaled.transpose(1, 2, 0, 3).reshape(tokens.shape)
    branch = low_back(matmul(merged, output_weight) + output_bias)
    middle = tokens + layer_norm(branch, post_gain, post_shift)
    second = low(layer_norm(middle, second_gain, second_shift))
    upper_pre = low_back(matmul(second, up_weight) + up_bias)
    mixed_low = low(layer_norm(jax.nn.gelu(upper_pre, approximate=False), middle_gain, middle_shift))
    return middle + low_back(matmul(mixed_low, down_weight) + down_bias)

def reference(inputs, cotangent, segment_ids, query_weight, key_weight, value_weight, output_weight, up_weight, down_weight, first_gain, first_shift, query_bias, value_bias, head_scale, output_bias, post_gain, post_shift, second_gain, second_shift, up_bias, middle_gain, middle_shift, down_bias):
    params = tuple((tensor.astype(jnp.float32) for tensor in (query_weight, key_weight, value_weight, output_weight, up_weight, down_weight, first_gain, first_shift, query_bias, value_bias, head_scale, output_bias, post_gain, post_shift, second_gain, second_shift, up_bias, middle_gain, middle_shift, down_bias)))
    pair_count = SEQS // 2

    def one_pair(totals, packed):
        tokens_pair, grad_pair, segment_pair = packed

        def forward(tokens, attention_probabilities):
            return layer(tokens, segment_pair, attention_probabilities)
        output, pullback = jax.vjp(forward, tokens_pair.astype(jnp.float32), params)
        grad_tokens, grad_params = pullback(grad_pair.astype(jnp.float32))
        totals = jax.tree.map(jnp.add, totals, grad_params)
        return (totals, (output.astype(jnp.bfloat16), grad_tokens.astype(jnp.bfloat16)))
    zero_grads = tuple((jnp.zeros_like(tensor) for tensor in params))
    packed_in = (inputs.reshape(pair_count, 2, SEQ_LEN, D), cotangent.reshape(pair_count, 2, SEQ_LEN, D), segment_ids.reshape(pair_count, 2, SEQ_LEN))
    totals, (outputs, input_grads) = lax.scan(one_pair, zero_grads, packed_in)
    return (outputs.reshape(SEQS, SEQ_LEN, D), input_grads.reshape(SEQS, SEQ_LEN, D), totals[0], totals[1], totals[2], totals[3], totals[4], totals[5], totals[6], totals[7], totals[8], totals[9], totals[10], totals[11], totals[12], totals[13], totals[14], totals[15], totals[16], totals[17], totals[18], totals[19])
```

```python
import functools

import jax
import jax.numpy as jnp
from jax import lax
from jax.experimental import pallas as pl
from jax.experimental.pallas import tpu as pltpu
from jax.sharding import PartitionSpec as P

EPSILON = 1e-05
MASKED = -1e30
DOCUMENT_MAX = 800
BLOCK = 256
LANES = 256
BOTH = ("dp", "seq")


def dot_nn(a, b):
    return lax.dot_general(a, b, (((1,), (0,)), ((), ())), preferred_element_type=jnp.float32)


def dot_nt(a, b):
    return lax.dot_general(a, b, (((1,), (1,)), ((), ())), preferred_element_type=jnp.float32)


def dot_tn(a, b):
    return lax.dot_general(a, b, (((0,), (0,)), ((), ())), preferred_element_type=jnp.float32)


def moments(values):
    row_mean = jnp.mean(values, -1, keepdims=True)
    centred = values - row_mean
    spread = jnp.mean(centred * centred, -1, keepdims=True)
    scale = lax.rsqrt(spread + EPSILON)
    return centred * scale, scale


def norm_back(hat, scale, gain, grad):
    weighted = gain * grad
    first = jnp.mean(weighted, -1, keepdims=True)
    second = jnp.mean(weighted * hat, -1, keepdims=True)
    return scale * (weighted - first - hat * second)


def pick_lanes(block, head, width):
    lane = lax.broadcasted_iota(jnp.int32, block.shape, 1)
    inside = (lane >= head * width) & (lane < (head + 1) * width)
    return jnp.where(inside, block, jnp.zeros_like(block))


def key_blocks(rows, hops):
    blocks = []
    for block in range(rows // BLOCK):
        blocks.append((0, block * BLOCK, BLOCK, block * BLOCK))
    place = 0
    for hop, hop_rows in enumerate(hops):
        place -= hop_rows
        if hop_rows % BLOCK == 0:
            for block in reversed(range(hop_rows // BLOCK)):
                blocks.append((hop + 1, block * BLOCK, BLOCK, place + block * BLOCK))
        else:
            blocks.append((hop + 1, 0, hop_rows, place))
    return blocks


def mask_scores(scores, first_key, start_row, first_query, diagonal):
    place = first_key + lax.broadcasted_iota(jnp.int32, scores.shape, 0)
    ok = place >= start_row
    if diagonal:
        ok = ok & (place <= first_query + lax.broadcasted_iota(jnp.int32, scores.shape, 1))
    return jnp.where(ok, scores, MASKED)


def attend_kernel(pieces, hops, heads, width, factor, first_ref, scale_ref, q_ref, *refs):
    keys, values = refs[:pieces], refs[pieces : 2 * pieces]
    start_ref, out_ref, lse_ref, qh_ref, m_ref, l_ref, acc_ref = refs[2 * pieces :]
    sequence, group = pl.program_id(0), pl.program_id(1)
    rows = q_ref.shape[1]
    blocks = key_blocks(rows, hops)
    for qi in range(rows // BLOCK):
        first_query = qi * BLOCK
        first = first_ref[sequence, qi]
        start_row = start_ref[0, :, first_query : first_query + BLOCK]
        q_block = q_ref[0, first_query : first_query + BLOCK, :] * factor
        for head in range(heads):
            qh_ref[head] = pick_lanes(q_block, head, width)

        def body(piece, offset, count, place, fresh):
            key = keys[piece][0, offset : offset + count, :]
            value_t = values[piece][0, offset : offset + count, :].T
            for head in range(heads):
                scores = dot_nt(key, qh_ref[head])
                scores = mask_scores(scores, place, start_row, first_query, fresh)
                top = jnp.max(scores, 0, keepdims=True)
                lanes = slice(head * width, (head + 1) * width)
                if fresh:
                    weights = jnp.exp(scores - top)
                    l_ref[head : head + 1] = jnp.sum(weights, 0, keepdims=True)
                    acc_ref[lanes] = dot_nn(value_t[lanes], weights.astype(jnp.bfloat16))
                    m_ref[head : head + 1] = top
                else:
                    before = m_ref[head : head + 1]
                    top = jnp.maximum(before, top)
                    fade = jnp.exp(before - top)
                    weights = jnp.exp(scores - top)
                    l_ref[head : head + 1] = l_ref[head : head + 1] * fade + jnp.sum(weights, 0, keepdims=True)
                    acc_ref[lanes] = acc_ref[lanes] * fade + dot_nn(value_t[lanes], weights.astype(jnp.bfloat16))
                    m_ref[head : head + 1] = top

        body(*blocks[qi], True)
        for block in reversed(blocks[:qi]):
            pl.when(first < block[3] + block[2])(functools.partial(body, *block, False))
        for block in blocks[rows // BLOCK :]:
            pl.when(first < block[3] + block[2])(functools.partial(body, *block, False))
        total = l_ref[...]
        lse_ref[0, 0, :, first_query : first_query + BLOCK] = m_ref[...] + jnp.log(total)
        for head in range(heads):
            lanes = slice(head * width, (head + 1) * width)
            acc_ref[lanes] = acc_ref[lanes] * (scale_ref[group * heads + head] / total[head : head + 1])
        out_ref[0, first_query : first_query + BLOCK, :] = acc_ref[...].T.astype(jnp.bfloat16)


def attend(first, head_scale, query, keys, values, start, hops):
    sequences, rows, model = query.shape
    head_count = head_scale.shape[0]
    width = model // head_count
    heads = LANES // width
    groups = model // LANES
    pieces = len(keys)
    wide = lambda count: pl.BlockSpec((1, count, LANES), lambda s, g, *_: (s, 0, g))
    counts = [k.shape[1] for k in keys]
    kernel = functools.partial(attend_kernel, pieces, hops, heads, width, width ** (-0.5))
    return pl.pallas_call(
        kernel,
        grid_spec=pltpu.PrefetchScalarGridSpec(
            num_scalar_prefetch=2,
            grid=(sequences, groups),
            in_specs=[wide(rows)] + [wide(c) for c in counts] * 2
            + [pl.BlockSpec((1, 1, rows), lambda s, g, *_: (s, 0, 0))],
            out_specs=[wide(rows), pl.BlockSpec((1, 1, heads, rows), lambda s, g, *_: (s, g, 0, 0))],
            scratch_shapes=[
                pltpu.VMEM((heads, BLOCK, LANES), jnp.bfloat16),
                pltpu.VMEM((heads, BLOCK), jnp.float32),
                pltpu.VMEM((heads, BLOCK), jnp.float32),
                pltpu.VMEM((LANES, BLOCK), jnp.float32),
            ],
        ),
        out_shape=[
            jax.ShapeDtypeStruct((sequences, rows, model), jnp.bfloat16),
            jax.ShapeDtypeStruct((sequences, groups, heads, rows), jnp.float32),
        ],
        name="attend",
    )(first, head_scale, query, *keys, *values, start)


def attend_back_kernel(pieces, hops, heads, width, factor, first_ref, scale_ref, q_ref, *refs):
    keys, values = refs[:pieces], refs[pieces : 2 * pieces]
    start_ref, lse_ref, out_ref, grad_ref = refs[2 * pieces : 2 * pieces + 4]
    dq_ref = refs[2 * pieces + 4]
    dkeys = refs[2 * pieces + 5 : 3 * pieces + 5]
    dvalues = refs[3 * pieces + 5 : 4 * pieces + 5]
    qh_ref, gh_ref, delta_ref, p_ref, ds_ref, dq_acc, dk_acc, dv_acc = refs[4 * pieces + 5 :]
    sequence, group = pl.program_id(0), pl.program_id(1)
    rows = q_ref.shape[1]
    query_blocks = rows // BLOCK
    for qi in range(query_blocks):
        here = slice(qi * BLOCK, (qi + 1) * BLOCK)
        q_block = q_ref[0, here, :] * factor
        grad = grad_ref[0, here, :]
        product = (grad.astype(jnp.float32) * out_ref[0, here, :].astype(jnp.float32)).T
        for head in range(heads):
            lanes = slice(head * width, (head + 1) * width)
            spot = slice(head * BLOCK, (head + 1) * BLOCK)
            qh_ref[qi, spot] = pick_lanes(q_block, head, width)
            gh_ref[qi, spot] = pick_lanes(grad, head, width)
            delta_ref[head : head + 1, here] = jnp.sum(product[lanes], 0, keepdims=True) / scale_ref[group * heads + head]
    dq_acc[...] = jnp.zeros_like(dq_acc)
    for piece, offset, count, place in key_blocks(rows, hops):
        key = keys[piece][0, offset : offset + count, :]
        key_t = key.T
        value = values[piece][0, offset : offset + count, :]
        dk_acc[:count] = jnp.zeros((count, LANES), jnp.float32)
        dv_acc[:count] = jnp.zeros((count, LANES), jnp.float32)
        for qi in range(query_blocks):
            first_query = qi * BLOCK
            if place > first_query:
                continue

            def body():
                here = slice(first_query, first_query + BLOCK)
                start_row = start_ref[0, :, here]
                for head in range(heads):
                    lanes = slice(head * width, (head + 1) * width)
                    spot = slice(head * BLOCK, (head + 1) * BLOCK)
                    scores = dot_nt(key, qh_ref[qi, spot])
                    scores = mask_scores(scores, place, start_row, first_query, place == first_query)
                    weights = jnp.exp(scores - lse_ref[0, 0, head : head + 1, here])
                    dweights = dot_nt(value, gh_ref[qi, spot])
                    dscores = (weights * (dweights - delta_ref[head : head + 1, here])).astype(jnp.bfloat16)
                    p_ref[:count, spot] = weights.astype(jnp.bfloat16)
                    ds_ref[:count, spot] = dscores
                    dq_acc[lanes, here] += dot_nn(key_t[lanes], dscores)
                dv_acc[:count] += dot_nn(p_ref[:count], gh_ref[qi])
                dk_acc[:count] += dot_nn(ds_ref[:count], qh_ref[qi])

            if place == first_query:
                body()
            else:
                pl.when(first_ref[sequence, qi] < place + count)(body)
        dkeys[piece][0, offset : offset + count, :] = dk_acc[:count].astype(jnp.bfloat16)
        dvalues[piece][0, offset : offset + count, :] = dv_acc[:count].astype(jnp.bfloat16)
    for qi in range(query_blocks):
        here = slice(qi * BLOCK, (qi + 1) * BLOCK)
        dq_ref[0, here, :] = (dq_acc[:, here] * factor).T.astype(jnp.bfloat16)


def attend_back(first, head_scale, query, keys, values, start, lse, scaled, grad, hops):
    sequences, rows, model = query.shape
    head_count = head_scale.shape[0]
    width = model // head_count
    heads = LANES // width
    groups = model // LANES
    pieces = len(keys)
    wide = lambda count: pl.BlockSpec((1, count, LANES), lambda s, g, *_: (s, 0, g))
    counts = [k.shape[1] for k in keys]
    most = max([BLOCK] + [c for c in counts if c % BLOCK])
    kernel = functools.partial(attend_back_kernel, pieces, hops, heads, width, width ** (-0.5))
    shape = lambda count: jax.ShapeDtypeStruct((sequences, count, model), jnp.bfloat16)
    results = pl.pallas_call(
        kernel,
        grid_spec=pltpu.PrefetchScalarGridSpec(
            num_scalar_prefetch=2,
            grid=(sequences, groups),
            in_specs=[wide(rows)] + [wide(c) for c in counts] * 2
            + [
                pl.BlockSpec((1, 1, rows), lambda s, g, *_: (s, 0, 0)),
                pl.BlockSpec((1, 1, heads, rows), lambda s, g, *_: (s, g, 0, 0)),
                wide(rows),
                wide(rows),
            ],
            out_specs=[wide(rows)] + [wide(c) for c in counts] * 2,
            scratch_shapes=[
                pltpu.VMEM((rows // BLOCK, heads * BLOCK, LANES), jnp.bfloat16),
                pltpu.VMEM((rows // BLOCK, heads * BLOCK, LANES), jnp.bfloat16),
                pltpu.VMEM((heads, rows), jnp.float32),
                pltpu.VMEM((most, heads * BLOCK), jnp.bfloat16),
                pltpu.VMEM((most, heads * BLOCK), jnp.bfloat16),
                pltpu.VMEM((LANES, rows), jnp.float32),
                pltpu.VMEM((most, LANES), jnp.float32),
                pltpu.VMEM((most, LANES), jnp.float32),
            ],
        ),
        out_shape=[shape(rows)] + [shape(c) for c in counts] * 2,
        name="attend_back",
    )(first, head_scale, query, *keys, *values, start, lse, scaled, grad)
    return results[0], results[1 : 1 + pieces], results[1 + pieces :]


def halo_rows(rows, ranks):
    hops, left = [], DOCUMENT_MAX - 1
    for _ in range(ranks - 1):
        if left <= 0:
            break
        hops.append(min(rows, -(-left // 32) * 32))
        left -= rows
    return hops


def local(
    inputs,
    cotangent,
    segment_ids,
    query_weight,
    key_weight,
    value_weight,
    output_weight,
    up_weight,
    down_weight,
    first_gain,
    first_shift,
    query_bias,
    value_bias,
    head_scale,
    output_bias,
    post_gain,
    post_shift,
    second_gain,
    second_shift,
    up_bias,
    middle_gain,
    middle_shift,
    down_bias,
):
    sequences, rows, model = inputs.shape
    hidden = up_bias.shape[0]
    head_count = head_scale.shape[0]
    ranks = lax.axis_size("seq")
    rank = lax.axis_index("seq")
    hops = halo_rows(rows, ranks)
    upward = [(i, i + 1) for i in range(ranks - 1)]
    downward = [(i + 1, i) for i in range(ranks - 1)]

    halos, moving = [], inputs
    for hop_rows in hops:
        moving = lax.ppermute(moving[:, rows - hop_rows :], "seq", upward)
        halos.append(moving)

    inward = jnp.concatenate([query_weight, key_weight, value_weight], 1)
    inward = lax.all_gather(inward, BOTH, axis=0, tiled=True)
    outward = lax.all_gather(jnp.concatenate([output_weight, up_weight], 1), BOTH, axis=0, tiled=True)
    down_full = lax.all_gather(down_weight, BOTH, axis=0, tiled=True)
    output_full, up_full = outward[:, :model], outward[:, model:]

    own_ids = lax.dynamic_slice_in_dim(segment_ids, rank * rows, rows, 1)
    start = jnp.sum((segment_ids[:, None, :] < own_ids[:, :, None]).astype(jnp.int32), -1) - rank * rows
    first = start[:, ::BLOCK]
    start = start[:, None, :]

    flat = lambda array: array.reshape(-1, array.shape[-1])
    tokens = flat(inputs).astype(jnp.float32)
    hat_one, scale_one = moments(tokens)
    normed = (hat_one * first_gain + first_shift).astype(jnp.bfloat16)
    projected = dot_nn(normed, inward)
    stacked = lambda array: array.reshape(sequences, -1, array.shape[-1])
    query = stacked((projected[:, :model] + query_bias).astype(jnp.bfloat16))
    keys = [stacked(projected[:, model : 2 * model].astype(jnp.bfloat16))]
    values = [stacked((projected[:, 2 * model :] + value_bias).astype(jnp.bfloat16))]
    normed_pieces = [normed]
    for halo in halos:
        hat, _ = moments(flat(halo).astype(jnp.float32))
        piece = (hat * first_gain + first_shift).astype(jnp.bfloat16)
        normed_pieces.append(piece)
        both = dot_nn(piece, inward[:, model:])
        keys.append(stacked(both[:, :model].astype(jnp.bfloat16)))
        values.append(stacked((both[:, model:] + value_bias).astype(jnp.bfloat16)))
    scaled, lse = attend(first, head_scale, query, keys, values, start, hops)

    scaled_low = flat(scaled)
    branch = dot_nn(scaled_low, output_full) + output_bias
    hat_post, scale_post = moments(branch)
    middle = tokens + hat_post * post_gain + post_shift
    hat_two, scale_two = moments(middle)
    second = (hat_two * second_gain + second_shift).astype(jnp.bfloat16)
    upper = dot_nn(second, up_full) + up_bias
    phi = 0.5 * (1.0 + lax.erf(upper * 0.7071067811865476))
    hat_middle, scale_middle = moments(upper * phi)
    mixed = (hat_middle * middle_gain + middle_shift).astype(jnp.bfloat16)
    layer_output = (middle + dot_nn(mixed, down_full) + down_bias).astype(jnp.bfloat16)

    grad_low = flat(cotangent)
    grad_out = grad_low.astype(jnp.float32)
    grad_mixed = dot_nt(grad_low, down_full)
    slope = phi + upper * (0.3989422804014327 * jnp.exp(-0.5 * upper * upper))
    grad_upper = (norm_back(hat_middle, scale_middle, middle_gain, grad_mixed) * slope).astype(jnp.bfloat16)
    grad_second = dot_nt(grad_upper, up_full)
    grad_middle = grad_out + norm_back(hat_two, scale_two, second_gain, grad_second)
    grad_branch = norm_back(hat_post, scale_post, post_gain, grad_middle).astype(jnp.bfloat16)
    grad_scaled = dot_nt(grad_branch, output_full)
    grad_attended = (grad_scaled * jnp.repeat(head_scale, model // head_count)).astype(jnp.bfloat16)
    head_columns = jnp.sum(grad_scaled * scaled_low.astype(jnp.float32), 0)
    head_term = jnp.sum(head_columns.reshape(head_count, -1), -1) / head_scale

    early_vectors = lax.psum(
        jnp.concatenate(
            [
                head_term,
                jnp.sum(grad_branch.astype(jnp.float32), 0),
                jnp.sum(grad_middle * hat_post, 0),
                jnp.sum(grad_middle, 0),
                jnp.sum(grad_second * hat_two, 0),
                jnp.sum(grad_second, 0),
                jnp.sum(grad_upper.astype(jnp.float32), 0),
                jnp.sum(grad_mixed * hat_middle, 0),
                jnp.sum(grad_mixed, 0),
                jnp.sum(grad_out, 0),
            ]
        ),
        BOTH,
    )
    scatter = lambda array: lax.psum_scatter(array, BOTH, scatter_dimension=0, tiled=True)
    down_part = scatter(dot_tn(mixed, grad_low).astype(jnp.bfloat16))
    outward_part = scatter(
        jnp.concatenate([dot_tn(scaled_low, grad_branch), dot_tn(second, grad_upper)], 1).astype(jnp.bfloat16)
    )

    dquery, dkeys, dvalues = attend_back(
        first, head_scale, query, keys, values, start, lse, scaled, stacked(grad_attended), hops
    )
    carried = None
    for hop in reversed(range(len(hops))):
        partial = stacked(
            dot_nt(flat(dkeys[hop + 1]), inward[:, model : 2 * model])
            + dot_nt(flat(dvalues[hop + 1]), inward[:, 2 * model :])
        )
        if carried is not None:
            partial = partial + jnp.pad(carried, ((0, 0), (partial.shape[1] - carried.shape[1], 0), (0, 0)))
        carried = lax.ppermute(partial.astype(jnp.bfloat16), "seq", downward).astype(jnp.float32)
    query_low, key_low, value_low = flat(dquery), flat(dkeys[0]), flat(dvalues[0])
    grad_normed = (
        dot_nt(query_low, inward[:, :model])
        + dot_nt(key_low, inward[:, model : 2 * model])
        + dot_nt(value_low, inward[:, 2 * model :])
    )
    if carried is not None:
        grad_normed = grad_normed + flat(jnp.pad(carried, ((0, 0), (rows - carried.shape[1], 0), (0, 0))))
    input_grad = (grad_middle + norm_back(hat_one, scale_one, first_gain, grad_normed)).astype(jnp.bfloat16)

    value_bias_term = sum(jnp.sum(d.astype(jnp.float32), (0, 1)) for d in dvalues)
    late_vectors = lax.psum(
        jnp.concatenate(
            [
                jnp.sum(grad_normed * hat_one, 0),
                jnp.sum(grad_normed, 0),
                jnp.sum(query_low.astype(jnp.float32), 0),
                value_bias_term,
            ]
        ),
        BOTH,
    )
    key_matrix = sum(dot_tn(n, flat(d)) for n, d in zip(normed_pieces, dkeys))
    value_matrix = sum(dot_tn(n, flat(d)) for n, d in zip(normed_pieces, dvalues))
    inward_part = scatter(
        jnp.concatenate([dot_tn(normed, query_low), key_matrix, value_matrix], 1).astype(jnp.bfloat16)
    )
    inward_part = inward_part.astype(jnp.float32)
    outward_part = outward_part.astype(jnp.float32)
    late = late_vectors.reshape(4, model)
    early = early_vectors[head_count:]
    five = early[: 5 * model].reshape(5, model)
    three = early[5 * model : 5 * model + 3 * hidden].reshape(3, hidden)
    return (
        stacked(layer_output),
        stacked(input_grad),
        inward_part[:, :model],
        inward_part[:, model : 2 * model],
        inward_part[:, 2 * model :],
        outward_part[:, :model],
        outward_part[:, model:],
        down_part.astype(jnp.float32),
        late[0],
        late[1],
        late[2],
        late[3],
        early_vectors[:head_count],
        five[0],
        five[1],
        five[2],
        five[3],
        five[4],
        three[0],
        three[1],
        three[2],
        early[5 * model + 3 * hidden :],
    )


def solution(mesh):
    sharded, matrix = P("dp", "seq", None), P(BOTH, None)
    in_specs = (sharded, sharded, P("dp", None)) + (matrix,) * 6 + (P(),) * 14
    out_specs = (sharded, sharded) + (matrix,) * 6 + (P(),) * 14
    return jax.shard_map(local, mesh=mesh, in_specs=in_specs, out_specs=out_specs, check_vma=False)
```

```python
import functools

import jax
import jax.numpy as jnp
from jax import lax
from jax.experimental import pallas as pl
from jax.experimental.pallas import tpu as pltpu
from jax.sharding import PartitionSpec as P

EPSILON = 1e-05
MASKED = -1e30
DOCUMENT_MAX = 800
BLOCK = 256
LANES = 256
BOTH = ("dp", "seq")


def dot_nn(a, b):
    return lax.dot_general(a, b, (((1,), (0,)), ((), ())), preferred_element_type=jnp.float32)


def dot_nt(a, b):
    return lax.dot_general(a, b, (((1,), (1,)), ((), ())), preferred_element_type=jnp.float32)


def dot_tn(a, b):
    return lax.dot_general(a, b, (((0,), (0,)), ((), ())), preferred_element_type=jnp.float32)


def moments(values):
    row_mean = jnp.mean(values, -1, keepdims=True)
    centred = values - row_mean
    spread = jnp.mean(centred * centred, -1, keepdims=True)
    scale = lax.rsqrt(spread + EPSILON)
    return centred * scale, scale


def norm_back(hat, scale, gain, grad):
    weighted = gain * grad
    first = jnp.mean(weighted, -1, keepdims=True)
    second = jnp.mean(weighted * hat, -1, keepdims=True)
    return scale * (weighted - first - hat * second)


def pick_lanes(block, head, width):
    lane = lax.broadcasted_iota(jnp.int32, block.shape, 1)
    inside = (lane >= head * width) & (lane < (head + 1) * width)
    return jnp.where(inside, block, jnp.zeros_like(block))


def key_blocks(rows, hops):
    blocks = []
    for block in range(rows // BLOCK):
        blocks.append((0, block * BLOCK, BLOCK, block * BLOCK))
    place = 0
    for hop, hop_rows in enumerate(hops):
        place -= hop_rows
        if hop_rows % BLOCK == 0:
            for block in reversed(range(hop_rows // BLOCK)):
                blocks.append((hop + 1, block * BLOCK, BLOCK, place + block * BLOCK))
        else:
            blocks.append((hop + 1, 0, hop_rows, place))
    return blocks


def mask_scores(scores, first_key, start_row, first_query, diagonal):
    place = first_key + lax.broadcasted_iota(jnp.int32, scores.shape, 0)
    ok = place >= start_row
    if diagonal:
        ok = ok & (place <= first_query + lax.broadcasted_iota(jnp.int32, scores.shape, 1))
    return jnp.where(ok, scores, MASKED)


def attend_kernel(pieces, hops, heads, width, factor, first_ref, scale_ref, q_ref, *refs):
    keys, values = refs[:pieces], refs[pieces : 2 * pieces]
    start_ref, out_ref, lse_ref, qh_ref, m_ref, l_ref, acc_ref = refs[2 * pieces :]
    sequence, group = pl.program_id(0), pl.program_id(1)
    rows = q_ref.shape[1]
    blocks = key_blocks(rows, hops)
    for qi in range(rows // BLOCK):
        first_query = qi * BLOCK
        first = first_ref[sequence, qi]
        start_row = start_ref[0, :, first_query : first_query + BLOCK]
        q_block = q_ref[0, first_query : first_query + BLOCK, :] * factor
        for head in range(heads):
            qh_ref[head] = pick_lanes(q_block, head, width)

        def body(piece, offset, count, place, fresh):
            key = keys[piece][0, offset : offset + count, :]
            value_t = values[piece][0, offset : offset + count, :].T
            for head in range(heads):
                scores = dot_nt(key, qh_ref[head])
                scores = mask_scores(scores, place, start_row, first_query, fresh)
                top = jnp.max(scores, 0, keepdims=True)
                lanes = slice(head * width, (head + 1) * width)
                if fresh:
                    weights = jnp.exp(scores - top)
                    l_ref[head : head + 1] = jnp.sum(weights, 0, keepdims=True)
                    acc_ref[lanes] = dot_nn(value_t[lanes], weights.astype(jnp.bfloat16))
                    m_ref[head : head + 1] = top
                else:
                    before = m_ref[head : head + 1]
                    top = jnp.maximum(before, top)
                    fade = jnp.exp(before - top)
                    weights = jnp.exp(scores - top)
                    l_ref[head : head + 1] = l_ref[head : head + 1] * fade + jnp.sum(weights, 0, keepdims=True)
                    acc_ref[lanes] = acc_ref[lanes] * fade + dot_nn(value_t[lanes], weights.astype(jnp.bfloat16))
                    m_ref[head : head + 1] = top

        body(*blocks[qi], True)
        for block in reversed(blocks[:qi]):
            pl.when(first < block[3] + block[2])(functools.partial(body, *block, False))
        for block in blocks[rows // BLOCK :]:
            pl.when(first < block[3] + block[2])(functools.partial(body, *block, False))
        total = l_ref[...]
        lse_ref[0, 0, :, first_query : first_query + BLOCK] = m_ref[...] + jnp.log(total)
        for head in range(heads):
            lanes = slice(head * width, (head + 1) * width)
            acc_ref[lanes] = acc_ref[lanes] * (scale_ref[group * heads + head] / total[head : head + 1])
        out_ref[0, first_query : first_query + BLOCK, :] = acc_ref[...].T.astype(jnp.bfloat16)


def attend(first, head_scale, query, keys, values, start, hops):
    sequences, rows, model = query.shape
    head_count = head_scale.shape[0]
    width = model // head_count
    heads = LANES // width
    groups = model // LANES
    pieces = len(keys)
    wide = lambda count: pl.BlockSpec((1, count, LANES), lambda s, g, *_: (s, 0, g))
    counts = [k.shape[1] for k in keys]
    kernel = functools.partial(attend_kernel, pieces, hops, heads, width, width ** (-0.5))
    return pl.pallas_call(
        kernel,
        grid_spec=pltpu.PrefetchScalarGridSpec(
            num_scalar_prefetch=2,
            grid=(sequences, groups),
            in_specs=[wide(rows)] + [wide(c) for c in counts] * 2
            + [pl.BlockSpec((1, 1, rows), lambda s, g, *_: (s, 0, 0))],
            out_specs=[wide(rows), pl.BlockSpec((1, 1, heads, rows), lambda s, g, *_: (s, g, 0, 0))],
            scratch_shapes=[
                pltpu.VMEM((heads, BLOCK, LANES), jnp.bfloat16),
                pltpu.VMEM((heads, BLOCK), jnp.float32),
                pltpu.VMEM((heads, BLOCK), jnp.float32),
                pltpu.VMEM((LANES, BLOCK), jnp.float32),
            ],
        ),
        out_shape=[
            jax.ShapeDtypeStruct((sequences, rows, model), jnp.bfloat16),
            jax.ShapeDtypeStruct((sequences, groups, heads, rows), jnp.float32),
        ],
        name="attend",
    )(first, head_scale, query, *keys, *values, start)


def attend_back_kernel(pieces, hops, heads, width, factor, first_ref, scale_ref, q_ref, *refs):
    keys, values = refs[:pieces], refs[pieces : 2 * pieces]
    start_ref, lse_ref, out_ref, grad_ref = refs[2 * pieces : 2 * pieces + 4]
    dq_ref = refs[2 * pieces + 4]
    dkeys = refs[2 * pieces + 5 : 3 * pieces + 5]
    dvalues = refs[3 * pieces + 5 : 4 * pieces + 5]
    qh_ref, gh_ref, delta_ref, p_ref, ds_ref, dq_acc, dk_acc, dv_acc = refs[4 * pieces + 5 :]
    sequence, group = pl.program_id(0), pl.program_id(1)
    rows = q_ref.shape[1]
    query_blocks = rows // BLOCK
    for qi in range(query_blocks):
        here = slice(qi * BLOCK, (qi + 1) * BLOCK)
        q_block = q_ref[0, here, :] * factor
        grad = grad_ref[0, here, :]
        product = (grad.astype(jnp.float32) * out_ref[0, here, :].astype(jnp.float32)).T
        for head in range(heads):
            lanes = slice(head * width, (head + 1) * width)
            spot = slice(head * BLOCK, (head + 1) * BLOCK)
            qh_ref[qi, spot] = pick_lanes(q_block, head, width)
            gh_ref[qi, spot] = pick_lanes(grad, head, width)
            delta_ref[head : head + 1, here] = jnp.sum(product[lanes], 0, keepdims=True) / scale_ref[group * heads + head]
    dq_acc[...] = jnp.zeros_like(dq_acc)
    for piece, offset, count, place in key_blocks(rows, hops):
        key = keys[piece][0, offset : offset + count, :]
        key_t = key.T
        value = values[piece][0, offset : offset + count, :]
        dk_acc[:count] = jnp.zeros((count, LANES), jnp.float32)
        dv_acc[:count] = jnp.zeros((count, LANES), jnp.float32)
        for qi in range(query_blocks):
            first_query = qi * BLOCK
            if place > first_query:
                continue

            def body():
                here = slice(first_query, first_query + BLOCK)
                start_row = start_ref[0, :, here]
                for head in range(heads):
                    lanes = slice(head * width, (head + 1) * width)
                    spot = slice(head * BLOCK, (head + 1) * BLOCK)
                    scores = dot_nt(key, qh_ref[qi, spot])
                    scores = mask_scores(scores, place, start_row, first_query, place == first_query)
                    weights = jnp.exp(scores - lse_ref[0, 0, head : head + 1, here])
                    dweights = dot_nt(value, gh_ref[qi, spot])
                    dscores = (weights * (dweights - delta_ref[head : head + 1, here])).astype(jnp.bfloat16)
                    p_ref[:count, spot] = weights.astype(jnp.bfloat16)
                    ds_ref[:count, spot] = dscores
                    dq_acc[lanes, here] += dot_nn(key_t[lanes], dscores)
                dv_acc[:count] += dot_nn(p_ref[:count], gh_ref[qi])
                dk_acc[:count] += dot_nn(ds_ref[:count], qh_ref[qi])

            if place == first_query:
                body()
            else:
                pl.when(first_ref[sequence, qi] < place + count)(body)
        dkeys[piece][0, offset : offset + count, :] = dk_acc[:count].astype(jnp.bfloat16)
        dvalues[piece][0, offset : offset + count, :] = dv_acc[:count].astype(jnp.bfloat16)
    for qi in range(query_blocks):
        here = slice(qi * BLOCK, (qi + 1) * BLOCK)
        dq_ref[0, here, :] = (dq_acc[:, here] * factor).T.astype(jnp.bfloat16)


def attend_back(first, head_scale, query, keys, values, start, lse, scaled, grad, hops):
    sequences, rows, model = query.shape
    head_count = head_scale.shape[0]
    width = model // head_count
    heads = LANES // width
    groups = model // LANES
    pieces = len(keys)
    wide = lambda count: pl.BlockSpec((1, count, LANES), lambda s, g, *_: (s, 0, g))
    counts = [k.shape[1] for k in keys]
    most = max([BLOCK] + [c for c in counts if c % BLOCK])
    kernel = functools.partial(attend_back_kernel, pieces, hops, heads, width, width ** (-0.5))
    shape = lambda count: jax.ShapeDtypeStruct((sequences, count, model), jnp.bfloat16)
    results = pl.pallas_call(
        kernel,
        grid_spec=pltpu.PrefetchScalarGridSpec(
            num_scalar_prefetch=2,
            grid=(sequences, groups),
            in_specs=[wide(rows)] + [wide(c) for c in counts] * 2
            + [
                pl.BlockSpec((1, 1, rows), lambda s, g, *_: (s, 0, 0)),
                pl.BlockSpec((1, 1, heads, rows), lambda s, g, *_: (s, g, 0, 0)),
                wide(rows),
                wide(rows),
            ],
            out_specs=[wide(rows)] + [wide(c) for c in counts] * 2,
            scratch_shapes=[
                pltpu.VMEM((rows // BLOCK, heads * BLOCK, LANES), jnp.bfloat16),
                pltpu.VMEM((rows // BLOCK, heads * BLOCK, LANES), jnp.bfloat16),
                pltpu.VMEM((heads, rows), jnp.float32),
                pltpu.VMEM((most, heads * BLOCK), jnp.bfloat16),
                pltpu.VMEM((most, heads * BLOCK), jnp.bfloat16),
                pltpu.VMEM((LANES, rows), jnp.float32),
                pltpu.VMEM((most, LANES), jnp.float32),
                pltpu.VMEM((most, LANES), jnp.float32),
            ],
        ),
        out_shape=[shape(rows)] + [shape(c) for c in counts] * 2,
        name="attend_back",
    )(first, head_scale, query, *keys, *values, start, lse, scaled, grad)
    return results[0], results[1 : 1 + pieces], results[1 + pieces :]


def halo_rows(rows, ranks):
    hops, left = [], DOCUMENT_MAX - 1
    for _ in range(ranks - 1):
        if left <= 0:
            break
        hops.append(min(rows, -(-left // 32) * 32))
        left -= rows
    return hops


def bits_of(axis):
    return [(axis, bit) for bit in range(lax.axis_size(axis).bit_length() - 1)]


def exchange(array, axis, bit):
    return lax.ppermute(array, axis, [(i, i ^ (1 << bit)) for i in range(lax.axis_size(axis))])


def reduce_rows(array, order):
    left = bits_of("dp")[::-1] + bits_of("seq")[::-1]
    columns = array.shape[-1]
    for axis, bit in order:
        at = left.index((axis, bit))
        left.pop(at)
        split = array.reshape(1 << at, 2, -1, columns)
        mine = (lax.axis_index(axis) >> bit) & 1
        gone = lax.dynamic_index_in_dim(split, 1 - mine, 1, keepdims=False)
        kept = lax.dynamic_index_in_dim(split, mine, 1, keepdims=False)
        came = exchange(gone.reshape(-1, columns), axis, bit).reshape(kept.shape)
        total = kept.astype(jnp.float32) + came.astype(jnp.float32)
        array = total.astype(array.dtype) if left else total
    return array.reshape(-1, columns)


def reduce_all(vector):
    for axis, bit in bits_of("dp") + bits_of("seq"):
        vector = vector + exchange(vector, axis, bit)
    return vector


def local(
    inputs,
    cotangent,
    segment_ids,
    query_weight,
    key_weight,
    value_weight,
    output_weight,
    up_weight,
    down_weight,
    first_gain,
    first_shift,
    query_bias,
    value_bias,
    head_scale,
    output_bias,
    post_gain,
    post_shift,
    second_gain,
    second_shift,
    up_bias,
    middle_gain,
    middle_shift,
    down_bias,
):
    sequences, rows, model = inputs.shape
    hidden = up_bias.shape[0]
    head_count = head_scale.shape[0]
    ranks = lax.axis_size("seq")
    rank = lax.axis_index("seq")
    hops = halo_rows(rows, ranks)
    upward = [(i, i + 1) for i in range(ranks - 1)]
    downward = [(i + 1, i) for i in range(ranks - 1)]

    halos, moving = [], inputs
    for hop_rows in hops:
        moving = lax.ppermute(moving[:, rows - hop_rows :], "seq", upward)
        halos.append(moving)

    inward = jnp.concatenate([query_weight, key_weight, value_weight], 1)
    inward = lax.all_gather(inward, BOTH, axis=0, tiled=True)
    outward = lax.all_gather(jnp.concatenate([output_weight, up_weight], 1), BOTH, axis=0, tiled=True)
    down_full = lax.all_gather(down_weight, BOTH, axis=0, tiled=True)
    output_full, up_full = outward[:, :model], outward[:, model:]

    own_ids = lax.dynamic_slice_in_dim(segment_ids, rank * rows, rows, 1)
    start = jnp.sum((segment_ids[:, None, :] < own_ids[:, :, None]).astype(jnp.int32), -1) - rank * rows
    first = start[:, ::BLOCK]
    start = start[:, None, :]

    flat = lambda array: array.reshape(-1, array.shape[-1])
    tokens = flat(inputs).astype(jnp.float32)
    hat_one, scale_one = moments(tokens)
    normed = (hat_one * first_gain + first_shift).astype(jnp.bfloat16)
    projected = dot_nn(normed, inward)
    stacked = lambda array: array.reshape(sequences, -1, array.shape[-1])
    query = stacked((projected[:, :model] + query_bias).astype(jnp.bfloat16))
    keys = [stacked(projected[:, model : 2 * model].astype(jnp.bfloat16))]
    values = [stacked((projected[:, 2 * model :] + value_bias).astype(jnp.bfloat16))]
    normed_pieces = [normed]
    for halo in halos:
        hat, _ = moments(flat(halo).astype(jnp.float32))
        piece = (hat * first_gain + first_shift).astype(jnp.bfloat16)
        normed_pieces.append(piece)
        both = dot_nn(piece, inward[:, model:])
        keys.append(stacked(both[:, :model].astype(jnp.bfloat16)))
        values.append(stacked((both[:, model:] + value_bias).astype(jnp.bfloat16)))
    scaled, lse = attend(first, head_scale, query, keys, values, start, hops)

    scaled_low = flat(scaled)
    branch = dot_nn(scaled_low, output_full) + output_bias
    hat_post, scale_post = moments(branch)
    middle = tokens + hat_post * post_gain + post_shift
    hat_two, scale_two = moments(middle)
    second = (hat_two * second_gain + second_shift).astype(jnp.bfloat16)
    upper = dot_nn(second, up_full) + up_bias
    phi = 0.5 * (1.0 + lax.erf(upper * 0.7071067811865476))
    hat_middle, scale_middle = moments(upper * phi)
    mixed = (hat_middle * middle_gain + middle_shift).astype(jnp.bfloat16)
    layer_output = (middle + dot_nn(mixed, down_full) + down_bias).astype(jnp.bfloat16)

    grad_low = flat(cotangent)
    grad_out = grad_low.astype(jnp.float32)
    grad_mixed = dot_nt(grad_low, down_full)
    slope = phi + upper * (0.3989422804014327 * jnp.exp(-0.5 * upper * upper))
    grad_upper = (norm_back(hat_middle, scale_middle, middle_gain, grad_mixed) * slope).astype(jnp.bfloat16)
    grad_second = dot_nt(grad_upper, up_full)
    grad_middle = grad_out + norm_back(hat_two, scale_two, second_gain, grad_second)
    grad_branch = norm_back(hat_post, scale_post, post_gain, grad_middle).astype(jnp.bfloat16)
    grad_scaled = dot_nt(grad_branch, output_full)
    grad_attended = (grad_scaled * jnp.repeat(head_scale, model // head_count)).astype(jnp.bfloat16)
    head_columns = jnp.sum(grad_scaled * scaled_low.astype(jnp.float32), 0)
    head_term = jnp.sum(head_columns.reshape(head_count, -1), -1) / head_scale

    early_vectors = reduce_all(
        jnp.concatenate(
            [
                head_term,
                jnp.sum(grad_branch.astype(jnp.float32), 0),
                jnp.sum(grad_middle * hat_post, 0),
                jnp.sum(grad_middle, 0),
                jnp.sum(grad_second * hat_two, 0),
                jnp.sum(grad_second, 0),
                jnp.sum(grad_upper.astype(jnp.float32), 0),
                jnp.sum(grad_mixed * hat_middle, 0),
                jnp.sum(grad_mixed, 0),
                jnp.sum(grad_out, 0),
            ]
        )
    )
    core, *planes = bits_of("dp")
    one_way = [core, *reversed(planes), *bits_of("seq")]
    other_way = [core, *planes, *bits_of("seq")]
    down_part = reduce_rows(dot_tn(mixed, grad_low).astype(jnp.bfloat16), one_way)
    outward_part = reduce_rows(
        jnp.concatenate([dot_tn(scaled_low, grad_branch), dot_tn(second, grad_upper)], 1).astype(jnp.bfloat16),
        other_way,
    )

    dquery, dkeys, dvalues = attend_back(
        first, head_scale, query, keys, values, start, lse, scaled, stacked(grad_attended), hops
    )
    carried = None
    for hop in reversed(range(len(hops))):
        partial = stacked(
            dot_nt(flat(dkeys[hop + 1]), inward[:, model : 2 * model])
            + dot_nt(flat(dvalues[hop + 1]), inward[:, 2 * model :])
        )
        if carried is not None:
            partial = partial + jnp.pad(carried, ((0, 0), (partial.shape[1] - carried.shape[1], 0), (0, 0)))
        carried = lax.ppermute(partial.astype(jnp.bfloat16), "seq", downward).astype(jnp.float32)
    query_low, key_low, value_low = flat(dquery), flat(dkeys[0]), flat(dvalues[0])
    grad_normed = (
        dot_nt(query_low, inward[:, :model])
        + dot_nt(key_low, inward[:, model : 2 * model])
        + dot_nt(value_low, inward[:, 2 * model :])
    )
    if carried is not None:
        grad_normed = grad_normed + flat(jnp.pad(carried, ((0, 0), (rows - carried.shape[1], 0), (0, 0))))
    input_grad = (grad_middle + norm_back(hat_one, scale_one, first_gain, grad_normed)).astype(jnp.bfloat16)

    value_bias_term = sum(jnp.sum(d.astype(jnp.float32), (0, 1)) for d in dvalues)
    late_vectors = reduce_all(
        jnp.concatenate(
            [
                jnp.sum(grad_normed * hat_one, 0),
                jnp.sum(grad_normed, 0),
                jnp.sum(query_low.astype(jnp.float32), 0),
                value_bias_term,
            ]
        )
    )
    key_matrix = sum(dot_tn(n, flat(d)) for n, d in zip(normed_pieces, dkeys))
    value_matrix = sum(dot_tn(n, flat(d)) for n, d in zip(normed_pieces, dvalues))
    inward_grad = jnp.concatenate([dot_tn(normed, query_low), key_matrix, value_matrix], 1).astype(jnp.bfloat16)
    half = inward_grad.shape[1] // 2
    inward_part = jnp.concatenate(
        [reduce_rows(inward_grad[:, :half], one_way), reduce_rows(inward_grad[:, half:], other_way)], 1
    )
    late = late_vectors.reshape(4, model)
    early = early_vectors[head_count:]
    five = early[: 5 * model].reshape(5, model)
    three = early[5 * model : 5 * model + 3 * hidden].reshape(3, hidden)
    return (
        stacked(layer_output),
        stacked(input_grad),
        inward_part[:, :model],
        inward_part[:, model : 2 * model],
        inward_part[:, 2 * model :],
        outward_part[:, :model],
        outward_part[:, model:],
        down_part,
        late[0],
        late[1],
        late[2],
        late[3],
        early_vectors[:head_count],
        five[0],
        five[1],
        five[2],
        five[3],
        five[4],
        three[0],
        three[1],
        three[2],
        early[5 * model + 3 * hidden :],
    )


def solution(mesh):
    sharded, matrix = P("dp", "seq", None), P(BOTH, None)
    in_specs = (sharded, sharded, P("dp", None)) + (matrix,) * 6 + (P(),) * 14
    out_specs = (sharded, sharded) + (matrix,) * 6 + (P(),) * 14
    return jax.shard_map(local, mesh=mesh, in_specs=in_specs, out_specs=out_specs, check_vma=False)
```

```python
import functools

import jax
import jax.numpy as jnp
from jax import lax
from jax.experimental import pallas as pl
from jax.experimental.pallas import tpu as pltpu
from jax.sharding import PartitionSpec as P

EPSILON = 1e-05
MASKED = -1e30
DOCUMENT_MAX = 800
BLOCK = 256
LANES = 256
BOTH = ("dp", "seq")


def dot_nn(a, b):
    return lax.dot_general(a, b, (((1,), (0,)), ((), ())), preferred_element_type=jnp.float32)


def dot_nt(a, b):
    return lax.dot_general(a, b, (((1,), (1,)), ((), ())), preferred_element_type=jnp.float32)


def dot_tn(a, b):
    return lax.dot_general(a, b, (((0,), (0,)), ((), ())), preferred_element_type=jnp.float32)


def moments(values):
    row_mean = jnp.mean(values, -1, keepdims=True)
    centred = values - row_mean
    spread = jnp.mean(centred * centred, -1, keepdims=True)
    scale = lax.rsqrt(spread + EPSILON)
    return centred * scale, scale


def norm_back(hat, scale, gain, grad):
    weighted = gain * grad
    first = jnp.mean(weighted, -1, keepdims=True)
    second = jnp.mean(weighted * hat, -1, keepdims=True)
    return scale * (weighted - first - hat * second)


def pick_lanes(block, head, width):
    lane = lax.broadcasted_iota(jnp.int32, block.shape, 1)
    inside = (lane >= head * width) & (lane < (head + 1) * width)
    return jnp.where(inside, block, jnp.zeros_like(block))


def key_blocks(rows, hops):
    blocks = []
    for block in range(rows // BLOCK):
        blocks.append((0, block * BLOCK, BLOCK, block * BLOCK))
    place = 0
    for hop, hop_rows in enumerate(hops):
        place -= hop_rows
        if hop_rows % BLOCK == 0:
            for block in reversed(range(hop_rows // BLOCK)):
                blocks.append((hop + 1, block * BLOCK, BLOCK, place + block * BLOCK))
        else:
            blocks.append((hop + 1, 0, hop_rows, place))
    return blocks


def mask_scores(scores, first_key, start_row, first_query, diagonal):
    place = first_key + lax.broadcasted_iota(jnp.int32, scores.shape, 0)
    ok = place >= start_row
    if diagonal:
        ok = ok & (place <= first_query + lax.broadcasted_iota(jnp.int32, scores.shape, 1))
    return jnp.where(ok, scores, MASKED)


def attend_kernel(pieces, hops, heads, width, factor, first_ref, scale_ref, q_ref, *refs):
    keys, values = refs[:pieces], refs[pieces : 2 * pieces]
    start_ref, out_ref, lse_ref, qh_ref, m_ref, l_ref, acc_ref = refs[2 * pieces :]
    sequence, group = pl.program_id(0), pl.program_id(1)
    rows = q_ref.shape[1]
    blocks = key_blocks(rows, hops)
    for qi in range(rows // BLOCK):
        first_query = qi * BLOCK
        first = first_ref[sequence, qi]
        start_row = start_ref[0, :, first_query : first_query + BLOCK]
        q_block = q_ref[0, first_query : first_query + BLOCK, :] * factor
        for head in range(heads):
            qh_ref[head] = pick_lanes(q_block, head, width)

        def body(piece, offset, count, place, fresh):
            key = keys[piece][0, offset : offset + count, :]
            value_t = values[piece][0, offset : offset + count, :].T
            for head in range(heads):
                scores = dot_nt(key, qh_ref[head])
                scores = mask_scores(scores, place, start_row, first_query, fresh)
                top = jnp.max(scores, 0, keepdims=True)
                lanes = slice(head * width, (head + 1) * width)
                if fresh:
                    weights = jnp.exp(scores - top)
                    l_ref[head : head + 1] = jnp.sum(weights, 0, keepdims=True)
                    acc_ref[lanes] = dot_nn(value_t[lanes], weights.astype(jnp.bfloat16))
                    m_ref[head : head + 1] = top
                else:
                    before = m_ref[head : head + 1]
                    top = jnp.maximum(before, top)
                    fade = jnp.exp(before - top)
                    weights = jnp.exp(scores - top)
                    l_ref[head : head + 1] = l_ref[head : head + 1] * fade + jnp.sum(weights, 0, keepdims=True)
                    acc_ref[lanes] = acc_ref[lanes] * fade + dot_nn(value_t[lanes], weights.astype(jnp.bfloat16))
                    m_ref[head : head + 1] = top

        body(*blocks[qi], True)
        for block in reversed(blocks[:qi]):
            pl.when(first < block[3] + block[2])(functools.partial(body, *block, False))
        for block in blocks[rows // BLOCK :]:
            pl.when(first < block[3] + block[2])(functools.partial(body, *block, False))
        total = l_ref[...]
        lse_ref[0, 0, :, first_query : first_query + BLOCK] = m_ref[...] + jnp.log(total)
        for head in range(heads):
            lanes = slice(head * width, (head + 1) * width)
            acc_ref[lanes] = acc_ref[lanes] * (scale_ref[group * heads + head] / total[head : head + 1])
        out_ref[0, first_query : first_query + BLOCK, :] = acc_ref[...].T.astype(jnp.bfloat16)


def attend(first, head_scale, query, keys, values, start, hops):
    sequences, rows, model = query.shape
    head_count = head_scale.shape[0]
    width = model // head_count
    heads = LANES // width
    groups = model // LANES
    pieces = len(keys)
    wide = lambda count: pl.BlockSpec((1, count, LANES), lambda s, g, *_: (s, 0, g))
    counts = [k.shape[1] for k in keys]
    kernel = functools.partial(attend_kernel, pieces, hops, heads, width, width ** (-0.5))
    return pl.pallas_call(
        kernel,
        grid_spec=pltpu.PrefetchScalarGridSpec(
            num_scalar_prefetch=2,
            grid=(sequences, groups),
            in_specs=[wide(rows)] + [wide(c) for c in counts] * 2
            + [pl.BlockSpec((1, 1, rows), lambda s, g, *_: (s, 0, 0))],
            out_specs=[wide(rows), pl.BlockSpec((1, 1, heads, rows), lambda s, g, *_: (s, g, 0, 0))],
            scratch_shapes=[
                pltpu.VMEM((heads, BLOCK, LANES), jnp.bfloat16),
                pltpu.VMEM((heads, BLOCK), jnp.float32),
                pltpu.VMEM((heads, BLOCK), jnp.float32),
                pltpu.VMEM((LANES, BLOCK), jnp.float32),
            ],
        ),
        out_shape=[
            jax.ShapeDtypeStruct((sequences, rows, model), jnp.bfloat16),
            jax.ShapeDtypeStruct((sequences, groups, heads, rows), jnp.float32),
        ],
        name="attend",
    )(first, head_scale, query, *keys, *values, start)


def attend_back_kernel(pieces, hops, heads, width, factor, first_ref, scale_ref, q_ref, *refs):
    keys, values = refs[:pieces], refs[pieces : 2 * pieces]
    start_ref, lse_ref, out_ref, grad_ref = refs[2 * pieces : 2 * pieces + 4]
    dq_ref = refs[2 * pieces + 4]
    dkeys = refs[2 * pieces + 5 : 3 * pieces + 5]
    dvalues = refs[3 * pieces + 5 : 4 * pieces + 5]
    qh_ref, gh_ref, delta_ref, p_ref, ds_ref, dq_acc, dk_acc, dv_acc = refs[4 * pieces + 5 :]
    sequence, group = pl.program_id(0), pl.program_id(1)
    rows = q_ref.shape[1]
    query_blocks = rows // BLOCK
    for qi in range(query_blocks):
        here = slice(qi * BLOCK, (qi + 1) * BLOCK)
        q_block = q_ref[0, here, :] * factor
        grad = grad_ref[0, here, :]
        product = (grad.astype(jnp.float32) * out_ref[0, here, :].astype(jnp.float32)).T
        for head in range(heads):
            lanes = slice(head * width, (head + 1) * width)
            spot = slice(head * BLOCK, (head + 1) * BLOCK)
            qh_ref[qi, spot] = pick_lanes(q_block, head, width)
            gh_ref[qi, spot] = pick_lanes(grad, head, width)
            delta_ref[head : head + 1, here] = jnp.sum(product[lanes], 0, keepdims=True) / scale_ref[group * heads + head]
    dq_acc[...] = jnp.zeros_like(dq_acc)
    for piece, offset, count, place in key_blocks(rows, hops):
        key = keys[piece][0, offset : offset + count, :]
        key_t = key.T
        value = values[piece][0, offset : offset + count, :]
        dk_acc[:count] = jnp.zeros((count, LANES), jnp.float32)
        dv_acc[:count] = jnp.zeros((count, LANES), jnp.float32)
        for qi in range(query_blocks):
            first_query = qi * BLOCK
            if place > first_query:
                continue

            def body():
                here = slice(first_query, first_query + BLOCK)
                start_row = start_ref[0, :, here]
                for head in range(heads):
                    lanes = slice(head * width, (head + 1) * width)
                    spot = slice(head * BLOCK, (head + 1) * BLOCK)
                    scores = dot_nt(key, qh_ref[qi, spot])
                    scores = mask_scores(scores, place, start_row, first_query, place == first_query)
                    weights = jnp.exp(scores - lse_ref[0, 0, head : head + 1, here])
                    dweights = dot_nt(value, gh_ref[qi, spot])
                    dscores = (weights * (dweights - delta_ref[head : head + 1, here])).astype(jnp.bfloat16)
                    p_ref[:count, spot] = weights.astype(jnp.bfloat16)
                    ds_ref[:count, spot] = dscores
                    dq_acc[lanes, here] += dot_nn(key_t[lanes], dscores)
                dv_acc[:count] += dot_nn(p_ref[:count], gh_ref[qi])
                dk_acc[:count] += dot_nn(ds_ref[:count], qh_ref[qi])

            if place == first_query:
                body()
            else:
                pl.when(first_ref[sequence, qi] < place + count)(body)
        dkeys[piece][0, offset : offset + count, :] = dk_acc[:count].astype(jnp.bfloat16)
        dvalues[piece][0, offset : offset + count, :] = dv_acc[:count].astype(jnp.bfloat16)
    for qi in range(query_blocks):
        here = slice(qi * BLOCK, (qi + 1) * BLOCK)
        dq_ref[0, here, :] = (dq_acc[:, here] * factor).T.astype(jnp.bfloat16)


def attend_back(first, head_scale, query, keys, values, start, lse, scaled, grad, hops):
    sequences, rows, model = query.shape
    head_count = head_scale.shape[0]
    width = model // head_count
    heads = LANES // width
    groups = model // LANES
    pieces = len(keys)
    wide = lambda count: pl.BlockSpec((1, count, LANES), lambda s, g, *_: (s, 0, g))
    counts = [k.shape[1] for k in keys]
    most = max([BLOCK] + [c for c in counts if c % BLOCK])
    kernel = functools.partial(attend_back_kernel, pieces, hops, heads, width, width ** (-0.5))
    shape = lambda count: jax.ShapeDtypeStruct((sequences, count, model), jnp.bfloat16)
    results = pl.pallas_call(
        kernel,
        grid_spec=pltpu.PrefetchScalarGridSpec(
            num_scalar_prefetch=2,
            grid=(sequences, groups),
            in_specs=[wide(rows)] + [wide(c) for c in counts] * 2
            + [
                pl.BlockSpec((1, 1, rows), lambda s, g, *_: (s, 0, 0)),
                pl.BlockSpec((1, 1, heads, rows), lambda s, g, *_: (s, g, 0, 0)),
                wide(rows),
                wide(rows),
            ],
            out_specs=[wide(rows)] + [wide(c) for c in counts] * 2,
            scratch_shapes=[
                pltpu.VMEM((rows // BLOCK, heads * BLOCK, LANES), jnp.bfloat16),
                pltpu.VMEM((rows // BLOCK, heads * BLOCK, LANES), jnp.bfloat16),
                pltpu.VMEM((heads, rows), jnp.float32),
                pltpu.VMEM((most, heads * BLOCK), jnp.bfloat16),
                pltpu.VMEM((most, heads * BLOCK), jnp.bfloat16),
                pltpu.VMEM((LANES, rows), jnp.float32),
                pltpu.VMEM((most, LANES), jnp.float32),
                pltpu.VMEM((most, LANES), jnp.float32),
            ],
        ),
        out_shape=[shape(rows)] + [shape(c) for c in counts] * 2,
        name="attend_back",
    )(first, head_scale, query, *keys, *values, start, lse, scaled, grad)
    return results[0], results[1 : 1 + pieces], results[1 + pieces :]


def halo_rows(rows, ranks):
    hops, left = [], DOCUMENT_MAX - 1
    for _ in range(ranks - 1):
        if left <= 0:
            break
        hops.append(min(rows, -(-left // 32) * 32))
        left -= rows
    return hops


def bits_of(axis):
    return [(axis, bit) for bit in range(lax.axis_size(axis).bit_length() - 1)]


def exchange(array, axis, bit):
    return lax.ppermute(array, axis, [(i, i ^ (1 << bit)) for i in range(lax.axis_size(axis))])


def together(*values):
    return lax.optimization_barrier(values)


def pick_columns(array, place, ours):
    axis, bit = place
    order = bits_of("dp")[::-1] + bits_of("seq")[::-1]
    mine = (lax.axis_index(axis) >> bit) & 1
    split = array.reshape(array.shape[0], 1 << order.index(place), 2, -1)
    picked = lax.dynamic_index_in_dim(split, mine if ours else 1 - mine, 2, keepdims=False)
    return picked.reshape(array.shape[0], -1)


own_columns = functools.partial(pick_columns, ours=True)
other_columns = functools.partial(pick_columns, ours=False)


class RowSum:
    def __init__(self, order):
        self.order = list(order)
        self.left = bits_of("dp")[::-1] + bits_of("seq")[::-1]
        self.came = self.kept = self.total = None

    def begin(self, sent):
        axis, bit = self.order.pop(0)
        self.left.remove((axis, bit))
        self.came = exchange(sent, axis, bit)

    def end_step(self, *chain):
        came, *chain = together(self.came, *chain)
        self.total = self.kept.astype(jnp.float32) + came.astype(jnp.float32)
        return chain

    def begin_step(self, *chain):
        axis, bit = self.order.pop(0)
        at = self.left.index((axis, bit))
        self.left.pop(at)
        total = self.total.astype(jnp.bfloat16)
        columns = total.shape[-1]
        split = total.reshape(1 << at, 2, -1, columns)
        mine = (lax.axis_index(axis) >> bit) & 1
        gone = lax.dynamic_index_in_dim(split, 1 - mine, 1, keepdims=False).reshape(-1, columns)
        kept = lax.dynamic_index_in_dim(split, mine, 1, keepdims=False).reshape(-1, columns)
        gone, self.kept, *chain = together(gone, kept, *chain)
        self.came = exchange(gone, axis, bit)
        return chain

    def advance(self, *chain):
        return self.begin_step(*self.end_step(*chain))


def reduce_all(vector):
    for axis, bit in bits_of("dp") + bits_of("seq"):
        vector = vector + exchange(vector, axis, bit)
    return vector


def local(
    inputs,
    cotangent,
    segment_ids,
    query_weight,
    key_weight,
    value_weight,
    output_weight,
    up_weight,
    down_weight,
    first_gain,
    first_shift,
    query_bias,
    value_bias,
    head_scale,
    output_bias,
    post_gain,
    post_shift,
    second_gain,
    second_shift,
    up_bias,
    middle_gain,
    middle_shift,
    down_bias,
):
    sequences, rows, model = inputs.shape
    hidden = up_bias.shape[0]
    head_count = head_scale.shape[0]
    ranks = lax.axis_size("seq")
    rank = lax.axis_index("seq")
    hops = halo_rows(rows, ranks)
    upward = [(i, i + 1) for i in range(ranks - 1)]
    downward = [(i + 1, i) for i in range(ranks - 1)]

    halos = []
    if hops:
        onward = hops[1] if len(hops) > 1 else hops[0]
        shift = lambda array: lax.ppermute(array, "seq", upward)
        moving = shift(inputs[:, rows - onward :])
        nearest = moving
        if onward < hops[0]:
            rest, moving = together(inputs[:, rows - hops[0] : rows - onward], moving)
            nearest = jnp.concatenate([shift(rest), moving], 1)
        halos.append(nearest)
        for hop_rows in hops[1:]:
            moving = shift(moving[:, moving.shape[1] - hop_rows :])
            halos.append(moving)

    inward = jnp.concatenate([query_weight, key_weight, value_weight], 1)
    inward = lax.all_gather(inward, BOTH, axis=0, tiled=True)
    outward = lax.all_gather(jnp.concatenate([output_weight, up_weight], 1), BOTH, axis=0, tiled=True)
    down_full = lax.all_gather(down_weight, BOTH, axis=0, tiled=True)
    output_full, up_full = outward[:, :model], outward[:, model:]

    own_ids = lax.dynamic_slice_in_dim(segment_ids, rank * rows, rows, 1)
    start = jnp.sum((segment_ids[:, None, :] < own_ids[:, :, None]).astype(jnp.int32), -1) - rank * rows
    first = start[:, ::BLOCK]
    start = start[:, None, :]

    flat = lambda array: array.reshape(-1, array.shape[-1])
    tokens = flat(inputs).astype(jnp.float32)
    hat_one, scale_one = moments(tokens)
    normed = (hat_one * first_gain + first_shift).astype(jnp.bfloat16)
    projected = dot_nn(normed, inward)
    stacked = lambda array: array.reshape(sequences, -1, array.shape[-1])
    query = stacked((projected[:, :model] + query_bias).astype(jnp.bfloat16))
    keys = [stacked(projected[:, model : 2 * model].astype(jnp.bfloat16))]
    values = [stacked((projected[:, 2 * model :] + value_bias).astype(jnp.bfloat16))]
    normed_pieces, hats = [normed], [hat_one]
    for halo in halos:
        hat, _ = moments(flat(halo).astype(jnp.float32))
        piece = (hat * first_gain + first_shift).astype(jnp.bfloat16)
        normed_pieces.append(piece)
        hats.append(hat)
        both = dot_nn(piece, inward[:, model:])
        keys.append(stacked(both[:, :model].astype(jnp.bfloat16)))
        values.append(stacked((both[:, model:] + value_bias).astype(jnp.bfloat16)))
    scaled, lse = attend(first, head_scale, query, keys, values, start, hops)

    scaled_low = flat(scaled)
    branch = dot_nn(scaled_low, output_full) + output_bias
    hat_post, scale_post = moments(branch)
    middle = tokens + hat_post * post_gain + post_shift
    hat_two, scale_two = moments(middle)
    second = (hat_two * second_gain + second_shift).astype(jnp.bfloat16)
    upper = dot_nn(second, up_full) + up_bias
    phi = 0.5 * (1.0 + lax.erf(upper * 0.7071067811865476))
    hat_middle, scale_middle = moments(upper * phi)
    mixed = (hat_middle * middle_gain + middle_shift).astype(jnp.bfloat16)
    grad_low = flat(cotangent)
    grad_out = grad_low.astype(jnp.float32)
    core, *planes = bits_of("dp")
    one_way = [core, *reversed(planes), *bits_of("seq")]
    other_way = [core, *planes, *bits_of("seq")]

    down_sum, up_sum = RowSum(one_way), RowSum(other_way)
    sent = dot_tn(other_columns(mixed, core), grad_low).astype(jnp.bfloat16)
    down_sum.begin(sent)
    down_sum.kept = dot_tn(own_columns(mixed, core), grad_low)
    (late_low,) = down_sum.advance(grad_low)

    layer_output = (middle + dot_nn(mixed, down_full) + down_bias).astype(jnp.bfloat16)
    grad_mixed = dot_nt(late_low, down_full)
    slope = phi + upper * (0.3989422804014327 * jnp.exp(-0.5 * upper * upper))
    grad_upper = (norm_back(hat_middle, scale_middle, middle_gain, grad_mixed) * slope).astype(jnp.bfloat16)
    (grad_upper,) = down_sum.advance(grad_upper)
    sent = dot_tn(other_columns(second, core), grad_upper).astype(jnp.bfloat16)
    sent, grad_upper = together(sent, grad_upper)
    up_sum.begin(sent)
    grad_second = dot_nt(grad_upper, up_full)
    grad_middle = grad_out + norm_back(hat_two, scale_two, second_gain, grad_second)
    grad_branch = norm_back(hat_post, scale_post, post_gain, grad_middle).astype(jnp.bfloat16)
    up_sum.kept = dot_tn(own_columns(second, core), grad_upper)
    (grad_branch,) = up_sum.advance(grad_branch)
    grad_scaled = dot_nt(grad_branch, output_full)
    grad_attended = (grad_scaled * jnp.repeat(head_scale, model // head_count)).astype(jnp.bfloat16)
    (grad_attended,) = down_sum.advance(grad_attended)
    head_columns = jnp.sum(grad_scaled * scaled_low.astype(jnp.float32), 0)
    head_term = jnp.sum(head_columns.reshape(head_count, -1), -1) / head_scale

    dquery, dkeys, dvalues = attend_back(
        first, head_scale, query, keys, values, start, lse, scaled, stacked(grad_attended), hops
    )
    partials = [
        dot_nt(flat(dkeys[hop + 1]), inward[:, model : 2 * model])
        + dot_nt(flat(dvalues[hop + 1]), inward[:, 2 * model :])
        for hop in range(len(hops))
    ]
    lower = lambda array: lax.ppermute(array, "seq", downward)
    query_low, key_low, value_low = flat(dquery), flat(dkeys[0]), flat(dvalues[0])
    carried = None
    if hops:
        going = stacked(partials[-1]).astype(jnp.bfloat16)
        going, query_low = together(going, query_low)
        carried = lower(going)
    query_low, key_low, value_low = down_sum.advance(query_low, key_low, value_low)
    query_low, key_low, value_low = up_sum.advance(query_low, key_low, value_low)

    inward_sums = RowSum(one_way), RowSum(other_way)
    halo_normed = normed_pieces[1:]
    halo_pairs = [(flat(k), flat(v)) for k, v in zip(dkeys[1:], dvalues[1:])]

    def four(pick):
        mine = pick(normed, core)
        key_part, value_part = dot_tn(mine, key_low), dot_tn(mine, value_low)
        for piece, (dkey, dvalue) in zip(halo_normed, halo_pairs):
            picked = pick(piece, core)
            key_part, value_part = key_part + dot_tn(picked, dkey), value_part + dot_tn(picked, dvalue)
        return dot_tn(mine, query_low), key_part, value_part, dot_tn(pick(scaled_low, core), grad_branch)

    sent = jnp.concatenate([part.astype(jnp.bfloat16) for part in four(other_columns)], 1)
    came = exchange(sent, *core)
    own = (
        dot_nt(query_low, inward[:, :model])
        + dot_nt(key_low, inward[:, model : 2 * model])
        + dot_nt(value_low, inward[:, 2 * model :])
    )
    for hop in reversed(range(len(hops) - 1)):
        carried, own = together(carried, own)
        partial = stacked(partials[hop])
        going = partial + jnp.pad(
            carried.astype(jnp.float32), ((0, 0), (partial.shape[1] - carried.shape[1], 0), (0, 0))
        )
        going, own = together(going.astype(jnp.bfloat16), own)
        carried = lower(going)
    mine = four(own_columns)
    for index, row_sum in enumerate(inward_sums):
        row_sum.order.pop(0)
        row_sum.left.remove(core)
        row_sum.came = came[:, 2 * index * model : 2 * (index + 1) * model]
        row_sum.kept = jnp.concatenate(mine[2 * index : 2 * (index + 1)], 1)

    vectors = reduce_all(
        jnp.concatenate(
            [
                head_term,
                jnp.sum(grad_branch.astype(jnp.float32), 0),
                jnp.sum(grad_middle * hat_post, 0),
                jnp.sum(grad_middle, 0),
                jnp.sum(grad_second * hat_two, 0),
                jnp.sum(grad_second, 0),
                jnp.sum(grad_out, 0),
                jnp.sum(own * hat_one, 0) + sum(jnp.sum(p * h, 0) for p, h in zip(partials, hats[1:])),
                jnp.sum(own, 0) + sum(jnp.sum(p, 0) for p in partials),
                jnp.sum(query_low.astype(jnp.float32), 0),
                sum(jnp.sum(d.astype(jnp.float32), (0, 1)) for d in dvalues),
                jnp.sum(grad_upper.astype(jnp.float32), 0),
                jnp.sum(grad_mixed * hat_middle, 0),
                jnp.sum(grad_mixed, 0),
            ]
        )
    )
    for row_sum in (down_sum, up_sum, *inward_sums):
        while row_sum.order:
            row_sum.advance()
        row_sum.end_step()

    grad_normed = own
    if hops:
        grad_normed = own + flat(jnp.pad(carried.astype(jnp.float32), ((0, 0), (rows - carried.shape[1], 0), (0, 0))))
    input_grad = (grad_middle + norm_back(hat_one, scale_one, first_gain, grad_normed)).astype(jnp.bfloat16)

    query_key, value_output = (row_sum.total for row_sum in inward_sums)
    rest = vectors[head_count:]
    narrow = rest[: 10 * model].reshape(10, model)
    broad = rest[10 * model :].reshape(3, hidden)
    return (
        stacked(layer_output),
        stacked(input_grad),
        query_key[:, :model],
        query_key[:, model:],
        value_output[:, :model],
        value_output[:, model:],
        up_sum.total,
        down_sum.total,
        narrow[6],
        narrow[7],
        narrow[8],
        narrow[9],
        vectors[:head_count],
        narrow[0],
        narrow[1],
        narrow[2],
        narrow[3],
        narrow[4],
        broad[0],
        broad[1],
        broad[2],
        narrow[5],
    )


def solution(mesh):
    sharded, matrix = P("dp", "seq", None), P(BOTH, None)
    in_specs = (sharded, sharded, P("dp", None)) + (matrix,) * 6 + (P(),) * 14
    out_specs = (sharded, sharded) + (matrix,) * 6 + (P(),) * 14
    return jax.shard_map(local, mesh=mesh, in_specs=in_specs, out_specs=out_specs, check_vma=False)
```

```python
import functools

import jax
import jax.numpy as jnp
from jax import lax
from jax.experimental import pallas as pl
from jax.experimental.pallas import tpu as pltpu
from jax.sharding import PartitionSpec as P

EPSILON = 1e-05
MASKED = -1e30
DOCUMENT_MAX = 800
BLOCK = 256
LANES = 256
BOTH = ("dp", "seq")


def dot_nn(a, b):
    return lax.dot_general(a, b, (((1,), (0,)), ((), ())), preferred_element_type=jnp.float32)


def dot_nt(a, b):
    return lax.dot_general(a, b, (((1,), (1,)), ((), ())), preferred_element_type=jnp.float32)


def dot_tn(a, b):
    return lax.dot_general(a, b, (((0,), (0,)), ((), ())), preferred_element_type=jnp.float32)


def moments(values):
    row_mean = jnp.mean(values, -1, keepdims=True)
    centred = values - row_mean
    spread = jnp.mean(centred * centred, -1, keepdims=True)
    scale = lax.rsqrt(spread + EPSILON)
    return centred * scale, scale


def norm_back(hat, scale, gain, grad):
    weighted = gain * grad
    first = jnp.mean(weighted, -1, keepdims=True)
    second = jnp.mean(weighted * hat, -1, keepdims=True)
    return scale * (weighted - first - hat * second)


def pick_lanes(block, head, width):
    lane = lax.broadcasted_iota(jnp.int32, block.shape, 1)
    inside = (lane >= head * width) & (lane < (head + 1) * width)
    return jnp.where(inside, block, jnp.zeros_like(block))


def key_blocks(rows, hops):
    blocks = []
    for block in range(rows // BLOCK):
        blocks.append((0, block * BLOCK, BLOCK, block * BLOCK))
    place = 0
    for hop, hop_rows in enumerate(hops):
        place -= hop_rows
        if hop_rows % BLOCK == 0:
            for block in reversed(range(hop_rows // BLOCK)):
                blocks.append((hop + 1, block * BLOCK, BLOCK, place + block * BLOCK))
        else:
            blocks.append((hop + 1, 0, hop_rows, place))
    return blocks


def mask_scores(scores, first_key, start_row, first_query, diagonal):
    place = first_key + lax.broadcasted_iota(jnp.int32, scores.shape, 0)
    ok = place >= start_row
    if diagonal:
        ok = ok & (place <= first_query + lax.broadcasted_iota(jnp.int32, scores.shape, 1))
    return jnp.where(ok, scores, MASKED)


def attend_kernel(pieces, hops, heads, width, factor, first_ref, scale_ref, q_ref, *refs):
    keys, values = refs[:pieces], refs[pieces : 2 * pieces]
    start_ref, out_ref, lse_ref, qh_ref, m_ref, l_ref, acc_ref = refs[2 * pieces :]
    sequence, group = pl.program_id(0), pl.program_id(1)
    rows = q_ref.shape[1]
    blocks = key_blocks(rows, hops)
    for qi in range(rows // BLOCK):
        first_query = qi * BLOCK
        first = first_ref[sequence, qi]
        start_row = start_ref[0, :, first_query : first_query + BLOCK]
        q_block = q_ref[0, first_query : first_query + BLOCK, :] * factor
        for head in range(heads):
            qh_ref[head] = pick_lanes(q_block, head, width)

        def body(piece, offset, count, place, fresh):
            key = keys[piece][0, offset : offset + count, :]
            value_t = values[piece][0, offset : offset + count, :].T
            for head in range(heads):
                scores = dot_nt(key, qh_ref[head])
                scores = mask_scores(scores, place, start_row, first_query, fresh)
                top = jnp.max(scores, 0, keepdims=True)
                lanes = slice(head * width, (head + 1) * width)
                if fresh:
                    weights = jnp.exp(scores - top)
                    l_ref[head : head + 1] = jnp.sum(weights, 0, keepdims=True)
                    acc_ref[lanes] = dot_nn(value_t[lanes], weights.astype(jnp.bfloat16))
                    m_ref[head : head + 1] = top
                else:
                    before = m_ref[head : head + 1]
                    top = jnp.maximum(before, top)
                    fade = jnp.exp(before - top)
                    weights = jnp.exp(scores - top)
                    l_ref[head : head + 1] = l_ref[head : head + 1] * fade + jnp.sum(weights, 0, keepdims=True)
                    acc_ref[lanes] = acc_ref[lanes] * fade + dot_nn(value_t[lanes], weights.astype(jnp.bfloat16))
                    m_ref[head : head + 1] = top

        body(*blocks[qi], True)
        for block in reversed(blocks[:qi]):
            pl.when(first < block[3] + block[2])(functools.partial(body, *block, False))
        for block in blocks[rows // BLOCK :]:
            pl.when(first < block[3] + block[2])(functools.partial(body, *block, False))
        total = l_ref[...]
        lse_ref[0, 0, :, first_query : first_query + BLOCK] = m_ref[...] + jnp.log(total)
        for head in range(heads):
            lanes = slice(head * width, (head + 1) * width)
            acc_ref[lanes] = acc_ref[lanes] * (scale_ref[group * heads + head] / total[head : head + 1])
        out_ref[0, first_query : first_query + BLOCK, :] = acc_ref[...].T.astype(jnp.bfloat16)


def attend(first, head_scale, query, keys, values, start, hops):
    sequences, rows, model = query.shape
    head_count = head_scale.shape[0]
    width = model // head_count
    heads = LANES // width
    groups = model // LANES
    pieces = len(keys)
    wide = lambda count: pl.BlockSpec((1, count, LANES), lambda s, g, *_: (s, 0, g))
    counts = [k.shape[1] for k in keys]
    kernel = functools.partial(attend_kernel, pieces, hops, heads, width, width ** (-0.5))
    return pl.pallas_call(
        kernel,
        grid_spec=pltpu.PrefetchScalarGridSpec(
            num_scalar_prefetch=2,
            grid=(sequences, groups),
            in_specs=[wide(rows)] + [wide(c) for c in counts] * 2
            + [pl.BlockSpec((1, 1, rows), lambda s, g, *_: (s, 0, 0))],
            out_specs=[wide(rows), pl.BlockSpec((1, 1, heads, rows), lambda s, g, *_: (s, g, 0, 0))],
            scratch_shapes=[
                pltpu.VMEM((heads, BLOCK, LANES), jnp.bfloat16),
                pltpu.VMEM((heads, BLOCK), jnp.float32),
                pltpu.VMEM((heads, BLOCK), jnp.float32),
                pltpu.VMEM((LANES, BLOCK), jnp.float32),
            ],
        ),
        out_shape=[
            jax.ShapeDtypeStruct((sequences, rows, model), jnp.bfloat16),
            jax.ShapeDtypeStruct((sequences, groups, heads, rows), jnp.float32),
        ],
        name="attend",
    )(first, head_scale, query, *keys, *values, start)


def attend_back_kernel(pieces, hops, heads, width, factor, first_ref, scale_ref, q_ref, *refs):
    keys, values = refs[:pieces], refs[pieces : 2 * pieces]
    start_ref, lse_ref, out_ref, grad_ref = refs[2 * pieces : 2 * pieces + 4]
    dq_ref = refs[2 * pieces + 4]
    dkeys = refs[2 * pieces + 5 : 3 * pieces + 5]
    dvalues = refs[3 * pieces + 5 : 4 * pieces + 5]
    qh_ref, gh_ref, delta_ref, p_ref, ds_ref, dq_acc, dk_acc, dv_acc = refs[4 * pieces + 5 :]
    sequence, group = pl.program_id(0), pl.program_id(1)
    rows = q_ref.shape[1]
    query_blocks = rows // BLOCK
    for qi in range(query_blocks):
        here = slice(qi * BLOCK, (qi + 1) * BLOCK)
        q_block = q_ref[0, here, :] * factor
        grad = grad_ref[0, here, :]
        product = (grad.astype(jnp.float32) * out_ref[0, here, :].astype(jnp.float32)).T
        for head in range(heads):
            lanes = slice(head * width, (head + 1) * width)
            spot = slice(head * BLOCK, (head + 1) * BLOCK)
            qh_ref[qi, spot] = pick_lanes(q_block, head, width)
            gh_ref[qi, spot] = pick_lanes(grad, head, width)
            delta_ref[head : head + 1, here] = jnp.sum(product[lanes], 0, keepdims=True) / scale_ref[group * heads + head]
    dq_acc[...] = jnp.zeros_like(dq_acc)
    for piece, offset, count, place in key_blocks(rows, hops):
        key = keys[piece][0, offset : offset + count, :]
        key_t = key.T
        value = values[piece][0, offset : offset + count, :]
        dk_acc[:count] = jnp.zeros((count, LANES), jnp.float32)
        dv_acc[:count] = jnp.zeros((count, LANES), jnp.float32)
        for qi in range(query_blocks):
            first_query = qi * BLOCK
            if place > first_query:
                continue

            def body():
                here = slice(first_query, first_query + BLOCK)
                start_row = start_ref[0, :, here]
                for head in range(heads):
                    lanes = slice(head * width, (head + 1) * width)
                    spot = slice(head * BLOCK, (head + 1) * BLOCK)
                    scores = dot_nt(key, qh_ref[qi, spot])
                    scores = mask_scores(scores, place, start_row, first_query, place == first_query)
                    weights = jnp.exp(scores - lse_ref[0, 0, head : head + 1, here])
                    dweights = dot_nt(value, gh_ref[qi, spot])
                    dscores = (weights * (dweights - delta_ref[head : head + 1, here])).astype(jnp.bfloat16)
                    p_ref[:count, spot] = weights.astype(jnp.bfloat16)
                    ds_ref[:count, spot] = dscores
                    dq_acc[lanes, here] += dot_nn(key_t[lanes], dscores)
                dv_acc[:count] += dot_nn(p_ref[:count], gh_ref[qi])
                dk_acc[:count] += dot_nn(ds_ref[:count], qh_ref[qi])

            if place == first_query:
                body()
            else:
                pl.when(first_ref[sequence, qi] < place + count)(body)
        dkeys[piece][0, offset : offset + count, :] = dk_acc[:count].astype(jnp.bfloat16)
        dvalues[piece][0, offset : offset + count, :] = dv_acc[:count].astype(jnp.bfloat16)
    for qi in range(query_blocks):
        here = slice(qi * BLOCK, (qi + 1) * BLOCK)
        dq_ref[0, here, :] = (dq_acc[:, here] * factor).T.astype(jnp.bfloat16)


def attend_back(first, head_scale, query, keys, values, start, lse, scaled, grad, hops):
    sequences, rows, model = query.shape
    head_count = head_scale.shape[0]
    width = model // head_count
    heads = LANES // width
    groups = model // LANES
    pieces = len(keys)
    wide = lambda count: pl.BlockSpec((1, count, LANES), lambda s, g, *_: (s, 0, g))
    counts = [k.shape[1] for k in keys]
    most = max([BLOCK] + [c for c in counts if c % BLOCK])
    kernel = functools.partial(attend_back_kernel, pieces, hops, heads, width, width ** (-0.5))
    shape = lambda count: jax.ShapeDtypeStruct((sequences, count, model), jnp.bfloat16)
    results = pl.pallas_call(
        kernel,
        grid_spec=pltpu.PrefetchScalarGridSpec(
            num_scalar_prefetch=2,
            grid=(sequences, groups),
            in_specs=[wide(rows)] + [wide(c) for c in counts] * 2
            + [
                pl.BlockSpec((1, 1, rows), lambda s, g, *_: (s, 0, 0)),
                pl.BlockSpec((1, 1, heads, rows), lambda s, g, *_: (s, g, 0, 0)),
                wide(rows),
                wide(rows),
            ],
            out_specs=[wide(rows)] + [wide(c) for c in counts] * 2,
            scratch_shapes=[
                pltpu.VMEM((rows // BLOCK, heads * BLOCK, LANES), jnp.bfloat16),
                pltpu.VMEM((rows // BLOCK, heads * BLOCK, LANES), jnp.bfloat16),
                pltpu.VMEM((heads, rows), jnp.float32),
                pltpu.VMEM((most, heads * BLOCK), jnp.bfloat16),
                pltpu.VMEM((most, heads * BLOCK), jnp.bfloat16),
                pltpu.VMEM((LANES, rows), jnp.float32),
                pltpu.VMEM((most, LANES), jnp.float32),
                pltpu.VMEM((most, LANES), jnp.float32),
            ],
        ),
        out_shape=[shape(rows)] + [shape(c) for c in counts] * 2,
        name="attend_back",
    )(first, head_scale, query, *keys, *values, start, lse, scaled, grad)
    return results[0], results[1 : 1 + pieces], results[1 + pieces :]


def halo_rows(rows, ranks):
    hops, left = [], DOCUMENT_MAX - 1
    for _ in range(ranks - 1):
        if left <= 0:
            break
        hops.append(min(rows, -(-left // 32) * 32))
        left -= rows
    return hops


def bits_of(axis):
    return [(axis, bit) for bit in range(lax.axis_size(axis).bit_length() - 1)]


def exchange(array, axis, bit):
    return lax.ppermute(array, axis, [(i, i ^ (1 << bit)) for i in range(lax.axis_size(axis))])


def together(*values):
    return lax.optimization_barrier(values)


def pick_kernel(mine_ref, array_ref, other_ref, own_ref):
    width = own_ref.shape[1]
    halves = array_ref[:, :width], array_ref[:, width:]
    for index in range(2):
        @pl.when(mine_ref[0] == index)
        def _():
            own_ref[...] = halves[index]
            other_ref[...] = halves[1 - index]


def pick_columns(array, place):
    axis, bit = place
    order = bits_of("dp")[::-1] + bits_of("seq")[::-1]
    mine = (lax.axis_index(axis) >> bit) & 1
    tokens, columns = array.shape
    above = 1 << order.index(place)
    width = columns // above // 2
    if width % 128:
        split = array.reshape(tokens, above, 2, width)
        take = lambda index: lax.dynamic_index_in_dim(split, index, 2, keepdims=False).reshape(tokens, -1)
        return take(1 - mine), take(mine)
    half = jax.ShapeDtypeStruct((tokens, columns // 2), array.dtype)
    return pl.pallas_call(
        pick_kernel,
        grid_spec=pltpu.PrefetchScalarGridSpec(
            num_scalar_prefetch=1,
            grid=(above,),
            in_specs=[pl.BlockSpec((tokens, 2 * width), lambda block, _: (0, block))],
            out_specs=[pl.BlockSpec((tokens, width), lambda block, _: (0, block))] * 2,
        ),
        out_shape=[half, half],
        name="pick",
    )(mine.reshape(1), array)


class Sequence:
    def __init__(self, token):
        self.token = token

    def __call__(self, *values):
        *values, self.token = together(*values, self.token)
        return values[0] if len(values) == 1 else values


class RowSum:
    def __init__(self, order):
        self.order = list(order)
        self.left = bits_of("dp")[::-1] + bits_of("seq")[::-1]
        self.came = self.kept = self.total = None

    def begin(self, came):
        self.left.remove(self.order.pop(0))
        self.came = came

    def step(self, sequence):
        came, self.kept = sequence(self.came, self.kept)
        total = self.kept.astype(jnp.float32) + came.astype(jnp.float32)
        if not self.order:
            self.total = sequence(total)
            return
        axis, bit = self.order.pop(0)
        at = self.left.index((axis, bit))
        self.left.pop(at)
        total = total.astype(jnp.bfloat16)
        columns = total.shape[-1]
        split = total.reshape(1 << at, 2, -1, columns)
        mine = (lax.axis_index(axis) >> bit) & 1
        gone = lax.dynamic_index_in_dim(split, 1 - mine, 1, keepdims=False).reshape(-1, columns)
        kept = lax.dynamic_index_in_dim(split, mine, 1, keepdims=False).reshape(-1, columns)
        gone, self.kept = sequence(gone, kept)
        self.came = exchange(gone, axis, bit)


def local(
    inputs,
    cotangent,
    segment_ids,
    query_weight,
    key_weight,
    value_weight,
    output_weight,
    up_weight,
    down_weight,
    first_gain,
    first_shift,
    query_bias,
    value_bias,
    head_scale,
    output_bias,
    post_gain,
    post_shift,
    second_gain,
    second_shift,
    up_bias,
    middle_gain,
    middle_shift,
    down_bias,
):
    sequences, rows, model = inputs.shape
    hidden = up_bias.shape[0]
    head_count = head_scale.shape[0]
    ranks = lax.axis_size("seq")
    rank = lax.axis_index("seq")
    hops = halo_rows(rows, ranks)
    upward = [(i, i + 1) for i in range(ranks - 1)]
    downward = [(i + 1, i) for i in range(ranks - 1)]

    halos = []
    if hops:
        onward = hops[1] if len(hops) > 1 else hops[0]
        shift = lambda array: lax.ppermute(array, "seq", upward)
        moving = shift(inputs[:, rows - onward :])
        nearest = moving
        if onward < hops[0]:
            rest, moving = together(inputs[:, rows - hops[0] : rows - onward], moving)
            nearest = jnp.concatenate([shift(rest), moving], 1)
        halos.append(nearest)
        for hop_rows in hops[1:]:
            moving = shift(moving[:, moving.shape[1] - hop_rows :])
            halos.append(moving)

    inward = jnp.concatenate([query_weight, key_weight, value_weight], 1)
    inward = lax.all_gather(inward, BOTH, axis=0, tiled=True)
    outward = lax.all_gather(jnp.concatenate([output_weight, up_weight], 1), BOTH, axis=0, tiled=True)
    down_full = lax.all_gather(down_weight, BOTH, axis=0, tiled=True)
    output_full, up_full = outward[:, :model], outward[:, model:]

    own_ids = lax.dynamic_slice_in_dim(segment_ids, rank * rows, rows, 1)
    start = jnp.sum((segment_ids[:, None, :] < own_ids[:, :, None]).astype(jnp.int32), -1) - rank * rows
    first = start[:, ::BLOCK]
    start = start[:, None, :]

    flat = lambda array: array.reshape(-1, array.shape[-1])
    tokens = flat(inputs).astype(jnp.float32)
    hat_one, scale_one = moments(tokens)
    normed = (hat_one * first_gain + first_shift).astype(jnp.bfloat16)
    projected = dot_nn(normed, inward)
    stacked = lambda array: array.reshape(sequences, -1, array.shape[-1])
    query = stacked((projected[:, :model] + query_bias).astype(jnp.bfloat16))
    keys = [stacked(projected[:, model : 2 * model].astype(jnp.bfloat16))]
    values = [stacked((projected[:, 2 * model :] + value_bias).astype(jnp.bfloat16))]
    normed_pieces, hats = [normed], [hat_one]
    for halo in halos:
        hat, _ = moments(flat(halo).astype(jnp.float32))
        piece = (hat * first_gain + first_shift).astype(jnp.bfloat16)
        normed_pieces.append(piece)
        hats.append(hat)
        both = dot_nn(piece, inward[:, model:])
        keys.append(stacked(both[:, :model].astype(jnp.bfloat16)))
        values.append(stacked((both[:, model:] + value_bias).astype(jnp.bfloat16)))
    scaled, lse = attend(first, head_scale, query, keys, values, start, hops)

    scaled_low = flat(scaled)
    branch = dot_nn(scaled_low, output_full) + output_bias
    hat_post, scale_post = moments(branch)
    middle = tokens + hat_post * post_gain + post_shift
    hat_two, scale_two = moments(middle)
    second = (hat_two * second_gain + second_shift).astype(jnp.bfloat16)
    upper = dot_nn(second, up_full) + up_bias
    phi = 0.5 * (1.0 + lax.erf(upper * 0.7071067811865476))
    hat_middle, scale_middle = moments(upper * phi)
    mixed = (hat_middle * middle_gain + middle_shift).astype(jnp.bfloat16)
    grad_low = flat(cotangent)
    grad_out = grad_low.astype(jnp.float32)
    core, *planes = bits_of("dp")
    one_way = [core, *reversed(planes), *bits_of("seq")]
    other_way = [core, *planes, *bits_of("seq")]

    down_sum, up_sum = RowSum(one_way), RowSum(other_way)
    sums = query_key_sum, value_output_sum = RowSum(one_way), RowSum(other_way)
    sequence = Sequence(jnp.zeros((8, 128), jnp.float32))
    other_mixed, own_mixed = pick_columns(mixed, core)
    sent, own_mixed, low = sequence(dot_tn(other_mixed, grad_low).astype(jnp.bfloat16), own_mixed, grad_low)
    down_sum.begin(exchange(sent, *core))
    down_sum.kept = dot_tn(own_mixed, low)
    down_sum.step(sequence)

    low = sequence(low)
    grad_mixed = dot_nt(low, down_full)
    slope = phi + upper * (0.3989422804014327 * jnp.exp(-0.5 * upper * upper))
    grad_upper = (norm_back(hat_middle, scale_middle, middle_gain, grad_mixed) * slope).astype(jnp.bfloat16)
    other_second, own_second = pick_columns(second, core)
    grad_upper = sequence(grad_upper)
    down_sum.step(sequence)
    sent = dot_tn(other_second, sequence(grad_upper)).astype(jnp.bfloat16)
    sent, grad_upper = sequence(sent, grad_upper)
    up_sum.begin(exchange(sent, *core))
    up_sum.kept = dot_tn(own_second, grad_upper)
    up_sum.step(sequence)
    grad_upper = sequence(grad_upper)
    grad_second = dot_nt(grad_upper, up_full)
    grad_middle = grad_out + norm_back(hat_two, scale_two, second_gain, grad_second)
    grad_branch = norm_back(hat_post, scale_post, post_gain, grad_middle).astype(jnp.bfloat16)
    grad_branch = sequence(grad_branch)
    down_sum.step(sequence)
    grad_branch = sequence(grad_branch)
    grad_scaled = dot_nt(grad_branch, output_full)
    grad_attended = (grad_scaled * jnp.repeat(head_scale, model // head_count)).astype(jnp.bfloat16)
    head_columns = jnp.sum(grad_scaled * scaled_low.astype(jnp.float32), 0)
    head_term = jnp.sum(head_columns.reshape(head_count, -1), -1) / head_scale
    grad_attended = sequence(grad_attended)

    dquery, dkeys, dvalues = attend_back(
        first, head_scale, query, keys, values, start, lse, scaled, stacked(grad_attended), hops
    )
    dkeys, dvalues = [flat(d) for d in dkeys], [flat(d) for d in dvalues]
    query_low = sequence(flat(dquery))
    back = lambda dkey, dvalue: dot_nt(dkey, inward[:, model : 2 * model]) + dot_nt(dvalue, inward[:, 2 * model :])
    lower = lambda array: lax.ppermute(array, "seq", downward)
    partials = [None] * len(hops)
    carried = None
    if hops:
        partials[-1] = back(dkeys[-1], dvalues[-1])
        carried = lower(sequence(stacked(partials[-1]).astype(jnp.bfloat16)))
    down_sum.step(sequence)
    up_sum.step(sequence)

    picked = [pick_columns(piece, core) for piece in normed_pieces]
    picked_scaled = pick_columns(scaled_low, core)
    query_low, grad_branch, dkeys[0], dvalues[0] = sequence(query_low, grad_branch, dkeys[0], dvalues[0])

    def four(side):
        return (
            dot_tn(picked[0][side], query_low),
            sum(dot_tn(p[side], d) for p, d in zip(picked, dkeys)),
            sum(dot_tn(p[side], d) for p, d in zip(picked, dvalues)),
            dot_tn(picked_scaled[side], grad_branch),
        )

    sent = sequence(jnp.concatenate([part.astype(jnp.bfloat16) for part in four(0)], 1))
    came = exchange(sent, *core)
    query_low, grad_branch, dkeys[0], dvalues[0] = sequence(query_low, grad_branch, dkeys[0], dvalues[0])
    mine = four(1)
    for hop in range(len(hops) - 1):
        partials[hop] = back(*sequence(dkeys[hop + 1], dvalues[hop + 1]))
    for index, row_sum in enumerate(sums):
        columns = slice(2 * index * model, 2 * (index + 1) * model)
        row_sum.begin(came[:, columns])
        row_sum.kept = jnp.concatenate(mine[2 * index : 2 * (index + 1)], 1)
        row_sum.step(sequence)
    for hop in reversed(range(len(hops) - 1)):
        carried, partial = sequence(carried, partials[hop])
        partial = stacked(partial)
        missing = partial.shape[1] - carried.shape[1]
        going = partial + jnp.pad(carried.astype(jnp.float32), ((0, 0), (missing, 0), (0, 0)))
        carried = lower(sequence(going.astype(jnp.bfloat16)))
    down_sum.step(sequence)

    query_low, dkeys[0], dvalues[0] = sequence(query_low, dkeys[0], dvalues[0])
    own = (
        dot_nt(query_low, inward[:, :model])
        + dot_nt(dkeys[0], inward[:, model : 2 * model])
        + dot_nt(dvalues[0], inward[:, 2 * model :])
    )
    own = sequence(own)
    for row_sum in sums:
        row_sum.step(sequence)
    own = sequence(own)
    vector = jnp.concatenate(
        [
            head_term,
            jnp.sum(grad_branch.astype(jnp.float32), 0),
            jnp.sum(grad_middle * hat_post, 0),
            jnp.sum(grad_middle, 0),
            jnp.sum(grad_second * hat_two, 0),
            jnp.sum(grad_second, 0),
            jnp.sum(grad_out, 0),
            jnp.sum(own * hat_one, 0) + sum(jnp.sum(p * h, 0) for p, h in zip(partials, hats[1:])),
            jnp.sum(own, 0) + sum(jnp.sum(p, 0) for p in partials),
            jnp.sum(query_low.astype(jnp.float32), 0),
            sum(jnp.sum(d.astype(jnp.float32), 0) for d in dvalues),
            jnp.sum(grad_upper.astype(jnp.float32), 0),
            jnp.sum(grad_mixed * hat_middle, 0),
            jnp.sum(grad_mixed, 0),
        ]
    )
    places = bits_of("dp") + bits_of("seq")

    def sum_vector(vector, count):
        for _ in range(min(count, len(places))):
            vector = sequence(vector + exchange(vector, *places.pop(0)))
        return vector

    vector = sum_vector(sequence(vector), 1)
    up_sum.step(sequence)
    mixed, middle = sequence(mixed, middle)
    layer_output = sequence((middle + dot_nn(mixed, down_full) + down_bias).astype(jnp.bfloat16))
    for row_sum in sums:
        row_sum.step(sequence)
    vector = sum_vector(vector, 2)
    up_sum.step(sequence)
    vector = sum_vector(vector, 1)
    grad_normed = own
    if hops:
        carried, own = sequence(carried, own)
        grad_normed = own + flat(jnp.pad(carried.astype(jnp.float32), ((0, 0), (rows - carried.shape[1], 0), (0, 0))))
    input_grad = (grad_middle + norm_back(hat_one, scale_one, first_gain, grad_normed)).astype(jnp.bfloat16)
    for row_sum in sums:
        row_sum.step(sequence)
    input_grad = sequence(input_grad)
    vector = sum_vector(vector, len(places))
    for row_sum in (up_sum, *sums, down_sum):
        while row_sum.total is None:
            row_sum.step(sequence)
    vectors = vector + sequence.token[0, 0]

    query_key, value_output = query_key_sum.total, value_output_sum.total
    rest = vectors[head_count:]
    narrow = rest[: 10 * model].reshape(10, model)
    broad = rest[10 * model :].reshape(3, hidden)
    return (
        stacked(layer_output),
        stacked(input_grad),
        query_key[:, :model],
        query_key[:, model:],
        value_output[:, :model],
        value_output[:, model:],
        up_sum.total,
        down_sum.total,
        narrow[6],
        narrow[7],
        narrow[8],
        narrow[9],
        vectors[:head_count],
        narrow[0],
        narrow[1],
        narrow[2],
        narrow[3],
        narrow[4],
        broad[0],
        broad[1],
        broad[2],
        narrow[5],
    )


def solution(mesh):
    sharded, matrix = P("dp", "seq", None), P(BOTH, None)
    in_specs = (sharded, sharded, P("dp", None)) + (matrix,) * 6 + (P(),) * 14
    out_specs = (sharded, sharded) + (matrix,) * 6 + (P(),) * 14
    return jax.shard_map(local, mesh=mesh, in_specs=in_specs, out_specs=out_specs, check_vma=False)
```

```python
import functools

import jax
import jax.numpy as jnp
from jax import lax
from jax.experimental import pallas as pl
from jax.experimental.pallas import tpu as pltpu
from jax.sharding import PartitionSpec as P

EPSILON = 1e-05
MASKED = -1e30
DOCUMENT_MAX = 800
BLOCK = 256
LANES = 256
BOTH = ("dp", "seq")


def dot_nn(a, b):
    return lax.dot_general(a, b, (((1,), (0,)), ((), ())), preferred_element_type=jnp.float32)


def dot_nt(a, b):
    return lax.dot_general(a, b, (((1,), (1,)), ((), ())), preferred_element_type=jnp.float32)


def dot_tn(a, b):
    return lax.dot_general(a, b, (((0,), (0,)), ((), ())), preferred_element_type=jnp.float32)


def moments(values):
    row_mean = jnp.mean(values, -1, keepdims=True)
    centred = values - row_mean
    spread = jnp.mean(centred * centred, -1, keepdims=True)
    scale = lax.rsqrt(spread + EPSILON)
    return centred * scale, scale


def norm_back(hat, scale, gain, grad):
    weighted = gain * grad
    first = jnp.mean(weighted, -1, keepdims=True)
    second = jnp.mean(weighted * hat, -1, keepdims=True)
    return scale * (weighted - first - hat * second)


def pick_lanes(block, head, width):
    lane = lax.broadcasted_iota(jnp.int32, block.shape, 1)
    inside = (lane >= head * width) & (lane < (head + 1) * width)
    return jnp.where(inside, block, jnp.zeros_like(block))


def key_blocks(rows, hops):
    blocks = []
    for block in range(rows // BLOCK):
        blocks.append((0, block * BLOCK, BLOCK, block * BLOCK))
    place = 0
    for hop, hop_rows in enumerate(hops):
        place -= hop_rows
        if hop_rows % BLOCK == 0:
            for block in reversed(range(hop_rows // BLOCK)):
                blocks.append((hop + 1, block * BLOCK, BLOCK, place + block * BLOCK))
        else:
            blocks.append((hop + 1, 0, hop_rows, place))
    return blocks


def mask_scores(scores, first_key, start_row, first_query, diagonal):
    place = first_key + lax.broadcasted_iota(jnp.int32, scores.shape, 0)
    ok = place >= start_row
    if diagonal:
        ok = ok & (place <= first_query + lax.broadcasted_iota(jnp.int32, scores.shape, 1))
    return jnp.where(ok, scores, MASKED)


def attend_kernel(pieces, hops, heads, width, factor, first_ref, scale_ref, q_ref, *refs):
    keys, values = refs[:pieces], refs[pieces : 2 * pieces]
    start_ref, out_ref, lse_ref, qh_ref, m_ref, l_ref, acc_ref = refs[2 * pieces :]
    sequence, group = pl.program_id(0), pl.program_id(1)
    rows = q_ref.shape[1]
    blocks = key_blocks(rows, hops)
    for qi in range(rows // BLOCK):
        first_query = qi * BLOCK
        first = first_ref[sequence, qi]
        start_row = start_ref[0, :, first_query : first_query + BLOCK]
        q_block = q_ref[0, first_query : first_query + BLOCK, :] * factor
        for head in range(heads):
            qh_ref[head] = pick_lanes(q_block, head, width)

        def body(piece, offset, count, place, fresh):
            key = keys[piece][0, offset : offset + count, :]
            value_t = values[piece][0, offset : offset + count, :].T
            for head in range(heads):
                scores = dot_nt(key, qh_ref[head])
                scores = mask_scores(scores, place, start_row, first_query, fresh)
                top = jnp.max(scores, 0, keepdims=True)
                lanes = slice(head * width, (head + 1) * width)
                if fresh:
                    weights = jnp.exp(scores - top)
                    l_ref[head : head + 1] = jnp.sum(weights, 0, keepdims=True)
                    acc_ref[lanes] = dot_nn(value_t[lanes], weights.astype(jnp.bfloat16))
                    m_ref[head : head + 1] = top
                else:
                    before = m_ref[head : head + 1]
                    top = jnp.maximum(before, top)
                    fade = jnp.exp(before - top)
                    weights = jnp.exp(scores - top)
                    l_ref[head : head + 1] = l_ref[head : head + 1] * fade + jnp.sum(weights, 0, keepdims=True)
                    acc_ref[lanes] = acc_ref[lanes] * fade + dot_nn(value_t[lanes], weights.astype(jnp.bfloat16))
                    m_ref[head : head + 1] = top

        body(*blocks[qi], True)
        for block in reversed(blocks[:qi]):
            pl.when(first < block[3] + block[2])(functools.partial(body, *block, False))
        for block in blocks[rows // BLOCK :]:
            pl.when(first < block[3] + block[2])(functools.partial(body, *block, False))
        total = l_ref[...]
        lse_ref[0, 0, :, first_query : first_query + BLOCK] = m_ref[...] + jnp.log(total)
        for head in range(heads):
            lanes = slice(head * width, (head + 1) * width)
            acc_ref[lanes] = acc_ref[lanes] * (scale_ref[group * heads + head] / total[head : head + 1])
        out_ref[0, first_query : first_query + BLOCK, :] = acc_ref[...].T.astype(jnp.bfloat16)


def attention_cost(sequences, rows, counts, head_count, model, products):
    pairs = sequences * head_count * rows * sum(counts)
    return pl.CostEstimate(
        flops=2 * products * pairs * LANES,
        bytes_accessed=4 * products * sequences * sum(counts) * model,
        transcendentals=pairs,
    )


def attend(first, head_scale, query, keys, values, start, hops):
    sequences, rows, model = query.shape
    head_count = head_scale.shape[0]
    width = model // head_count
    heads = LANES // width
    groups = model // LANES
    pieces = len(keys)
    wide = lambda count: pl.BlockSpec((1, count, LANES), lambda s, g, *_: (s, 0, g))
    counts = [k.shape[1] for k in keys]
    kernel = functools.partial(attend_kernel, pieces, hops, heads, width, width ** (-0.5))
    return pl.pallas_call(
        kernel,
        grid_spec=pltpu.PrefetchScalarGridSpec(
            num_scalar_prefetch=2,
            grid=(sequences, groups),
            in_specs=[wide(rows)] + [wide(c) for c in counts] * 2
            + [pl.BlockSpec((1, 1, rows), lambda s, g, *_: (s, 0, 0))],
            out_specs=[wide(rows), pl.BlockSpec((1, 1, heads, rows), lambda s, g, *_: (s, g, 0, 0))],
            scratch_shapes=[
                pltpu.VMEM((heads, BLOCK, LANES), jnp.bfloat16),
                pltpu.VMEM((heads, BLOCK), jnp.float32),
                pltpu.VMEM((heads, BLOCK), jnp.float32),
                pltpu.VMEM((LANES, BLOCK), jnp.float32),
            ],
        ),
        out_shape=[
            jax.ShapeDtypeStruct((sequences, rows, model), jnp.bfloat16),
            jax.ShapeDtypeStruct((sequences, groups, heads, rows), jnp.float32),
        ],
        name="attend",
        cost_estimate=attention_cost(sequences, rows, counts, head_count, model, 3),
    )(first, head_scale, query, *keys, *values, start)


def attend_back_kernel(pieces, hops, heads, width, factor, first_ref, scale_ref, q_ref, *refs):
    keys, values = refs[:pieces], refs[pieces : 2 * pieces]
    start_ref, lse_ref, out_ref, grad_ref = refs[2 * pieces : 2 * pieces + 4]
    dq_ref = refs[2 * pieces + 4]
    dkeys = refs[2 * pieces + 5 : 3 * pieces + 5]
    dvalues = refs[3 * pieces + 5 : 4 * pieces + 5]
    qh_ref, gh_ref, delta_ref, p_ref, ds_ref, dq_acc, dk_acc, dv_acc = refs[4 * pieces + 5 :]
    sequence, group = pl.program_id(0), pl.program_id(1)
    rows = q_ref.shape[1]
    query_blocks = rows // BLOCK
    for qi in range(query_blocks):
        here = slice(qi * BLOCK, (qi + 1) * BLOCK)
        q_block = q_ref[0, here, :] * factor
        grad = grad_ref[0, here, :]
        product = (grad.astype(jnp.float32) * out_ref[0, here, :].astype(jnp.float32)).T
        for head in range(heads):
            lanes = slice(head * width, (head + 1) * width)
            spot = slice(head * BLOCK, (head + 1) * BLOCK)
            qh_ref[qi, spot] = pick_lanes(q_block, head, width)
            gh_ref[qi, spot] = pick_lanes(grad, head, width)
            delta_ref[head : head + 1, here] = jnp.sum(product[lanes], 0, keepdims=True) / scale_ref[group * heads + head]
    dq_acc[...] = jnp.zeros_like(dq_acc)
    for piece, offset, count, place in key_blocks(rows, hops):
        key = keys[piece][0, offset : offset + count, :]
        key_t = key.T
        value = values[piece][0, offset : offset + count, :]
        dk_acc[:count] = jnp.zeros((count, LANES), jnp.float32)
        dv_acc[:count] = jnp.zeros((count, LANES), jnp.float32)
        for qi in range(query_blocks):
            first_query = qi * BLOCK
            if place > first_query:
                continue

            def body():
                here = slice(first_query, first_query + BLOCK)
                start_row = start_ref[0, :, here]
                for head in range(heads):
                    lanes = slice(head * width, (head + 1) * width)
                    spot = slice(head * BLOCK, (head + 1) * BLOCK)
                    scores = dot_nt(key, qh_ref[qi, spot])
                    scores = mask_scores(scores, place, start_row, first_query, place == first_query)
                    weights = jnp.exp(scores - lse_ref[0, 0, head : head + 1, here])
                    dweights = dot_nt(value, gh_ref[qi, spot])
                    dscores = (weights * (dweights - delta_ref[head : head + 1, here])).astype(jnp.bfloat16)
                    p_ref[:count, spot] = weights.astype(jnp.bfloat16)
                    ds_ref[:count, spot] = dscores
                    dq_acc[lanes, here] += dot_nn(key_t[lanes], dscores)
                dv_acc[:count] += dot_nn(p_ref[:count], gh_ref[qi])
                dk_acc[:count] += dot_nn(ds_ref[:count], qh_ref[qi])

            if place == first_query:
                body()
            else:
                pl.when(first_ref[sequence, qi] < place + count)(body)
        dkeys[piece][0, offset : offset + count, :] = dk_acc[:count].astype(jnp.bfloat16)
        dvalues[piece][0, offset : offset + count, :] = dv_acc[:count].astype(jnp.bfloat16)
    for qi in range(query_blocks):
        here = slice(qi * BLOCK, (qi + 1) * BLOCK)
        dq_ref[0, here, :] = (dq_acc[:, here] * factor).T.astype(jnp.bfloat16)


def attend_back(first, head_scale, query, keys, values, start, lse, scaled, grad, hops):
    sequences, rows, model = query.shape
    head_count = head_scale.shape[0]
    width = model // head_count
    heads = LANES // width
    groups = model // LANES
    pieces = len(keys)
    wide = lambda count: pl.BlockSpec((1, count, LANES), lambda s, g, *_: (s, 0, g))
    counts = [k.shape[1] for k in keys]
    most = max([BLOCK] + [c for c in counts if c % BLOCK])
    kernel = functools.partial(attend_back_kernel, pieces, hops, heads, width, width ** (-0.5))
    shape = lambda count: jax.ShapeDtypeStruct((sequences, count, model), jnp.bfloat16)
    results = pl.pallas_call(
        kernel,
        grid_spec=pltpu.PrefetchScalarGridSpec(
            num_scalar_prefetch=2,
            grid=(sequences, groups),
            in_specs=[wide(rows)] + [wide(c) for c in counts] * 2
            + [
                pl.BlockSpec((1, 1, rows), lambda s, g, *_: (s, 0, 0)),
                pl.BlockSpec((1, 1, heads, rows), lambda s, g, *_: (s, g, 0, 0)),
                wide(rows),
                wide(rows),
            ],
            out_specs=[wide(rows)] + [wide(c) for c in counts] * 2,
            scratch_shapes=[
                pltpu.VMEM((rows // BLOCK, heads * BLOCK, LANES), jnp.bfloat16),
                pltpu.VMEM((rows // BLOCK, heads * BLOCK, LANES), jnp.bfloat16),
                pltpu.VMEM((heads, rows), jnp.float32),
                pltpu.VMEM((most, heads * BLOCK), jnp.bfloat16),
                pltpu.VMEM((most, heads * BLOCK), jnp.bfloat16),
                pltpu.VMEM((LANES, rows), jnp.float32),
                pltpu.VMEM((most, LANES), jnp.float32),
                pltpu.VMEM((most, LANES), jnp.float32),
            ],
        ),
        out_shape=[shape(rows)] + [shape(c) for c in counts] * 2,
        name="attend_back",
        cost_estimate=attention_cost(sequences, rows, counts, head_count, model, 5),
    )(first, head_scale, query, *keys, *values, start, lse, scaled, grad)
    return results[0], results[1 : 1 + pieces], results[1 + pieces :]


def halo_rows(rows, ranks):
    hops, left = [], DOCUMENT_MAX - 1
    for _ in range(ranks - 1):
        if left <= 0:
            break
        hops.append(min(rows, -(-left // 32) * 32))
        left -= rows
    return hops


def bits_of(axis):
    return [(axis, bit) for bit in range(lax.axis_size(axis).bit_length() - 1)]


def exchange(array, axis, bit):
    return lax.ppermute(array, axis, [(i, i ^ (1 << bit)) for i in range(lax.axis_size(axis))])


def together(*values):
    return lax.optimization_barrier(values)


def pick_kernel(mine_ref, array_ref, other_ref, own_ref):
    width = own_ref.shape[1]
    halves = array_ref[:, :width], array_ref[:, width:]
    for index in range(2):
        @pl.when(mine_ref[0] == index)
        def _():
            own_ref[...] = halves[index]
            other_ref[...] = halves[1 - index]


def pick_columns(array, place):
    axis, bit = place
    order = bits_of("dp")[::-1] + bits_of("seq")[::-1]
    mine = (lax.axis_index(axis) >> bit) & 1
    tokens, columns = array.shape
    above = 1 << order.index(place)
    width = columns // above // 2
    if width % 128:
        split = array.reshape(tokens, above, 2, width)
        take = lambda index: lax.dynamic_index_in_dim(split, index, 2, keepdims=False).reshape(tokens, -1)
        return take(1 - mine), take(mine)
    half = jax.ShapeDtypeStruct((tokens, columns // 2), array.dtype)
    return pl.pallas_call(
        pick_kernel,
        grid_spec=pltpu.PrefetchScalarGridSpec(
            num_scalar_prefetch=1,
            grid=(above,),
            in_specs=[pl.BlockSpec((tokens, 2 * width), lambda block, _: (0, block))],
            out_specs=[pl.BlockSpec((tokens, width), lambda block, _: (0, block))] * 2,
        ),
        out_shape=[half, half],
        name="pick",
        cost_estimate=pl.CostEstimate(flops=0, bytes_accessed=4 * array.size * array.dtype.itemsize, transcendentals=0),
    )(mine.reshape(1), array)


class Sequence:
    def __init__(self, token):
        self.token = token

    def __call__(self, *values):
        *values, self.token = together(*values, self.token)
        return values[0] if len(values) == 1 else values


class RowSum:
    def __init__(self, order):
        self.order = list(order)
        self.left = bits_of("dp")[::-1] + bits_of("seq")[::-1]
        self.came = self.kept = self.total = None

    def begin(self, came):
        self.left.remove(self.order.pop(0))
        self.came = came

    def step(self, sequence):
        if callable(self.kept):
            came, kept = sequence(self.came), self.kept()
        else:
            came, kept = sequence(self.came, self.kept)
        total = kept.astype(jnp.float32) + came.astype(jnp.float32)
        if not self.order:
            self.total = sequence(total)
            return
        axis, bit = self.order.pop(0)
        at = self.left.index((axis, bit))
        self.left.pop(at)
        total = total.astype(jnp.bfloat16)
        columns = total.shape[-1]
        split = total.reshape(1 << at, 2, -1, columns)
        mine = (lax.axis_index(axis) >> bit) & 1
        gone = lax.dynamic_index_in_dim(split, 1 - mine, 1, keepdims=False).reshape(-1, columns)
        kept = lax.dynamic_index_in_dim(split, mine, 1, keepdims=False).reshape(-1, columns)
        gone, self.kept = sequence(gone, kept)
        self.came = exchange(gone, axis, bit)


def local(
    inputs,
    cotangent,
    segment_ids,
    query_weight,
    key_weight,
    value_weight,
    output_weight,
    up_weight,
    down_weight,
    first_gain,
    first_shift,
    query_bias,
    value_bias,
    head_scale,
    output_bias,
    post_gain,
    post_shift,
    second_gain,
    second_shift,
    up_bias,
    middle_gain,
    middle_shift,
    down_bias,
):
    sequences, rows, model = inputs.shape
    hidden = up_bias.shape[0]
    head_count = head_scale.shape[0]
    ranks = lax.axis_size("seq")
    rank = lax.axis_index("seq")
    hops = halo_rows(rows, ranks)
    upward = [(i, i + 1) for i in range(ranks - 1)]
    downward = [(i + 1, i) for i in range(ranks - 1)]

    halos = []
    if hops:
        onward = hops[1] if len(hops) > 1 else hops[0]
        shift = lambda array: lax.ppermute(array, "seq", upward)
        moving = shift(inputs[:, rows - onward :])
        nearest = moving
        if onward < hops[0]:
            rest, moving = together(inputs[:, rows - hops[0] : rows - onward], moving)
            nearest = jnp.concatenate([shift(rest), moving], 1)
        halos.append(nearest)
        for hop_rows in hops[1:]:
            moving = shift(moving[:, moving.shape[1] - hop_rows :])
            halos.append(moving)

    inward = jnp.concatenate([query_weight, key_weight, value_weight], 1)
    inward = lax.all_gather(inward, BOTH, axis=0, tiled=True)
    outward = lax.all_gather(jnp.concatenate([output_weight, up_weight], 1), BOTH, axis=0, tiled=True)
    down_full = lax.all_gather(down_weight, BOTH, axis=0, tiled=True)
    output_full, up_full = outward[:, :model], outward[:, model:]

    own_ids = lax.dynamic_slice_in_dim(segment_ids, rank * rows, rows, 1)
    start = jnp.sum((segment_ids[:, None, :] < own_ids[:, :, None]).astype(jnp.int32), -1) - rank * rows
    first = start[:, ::BLOCK]
    start = start[:, None, :]

    flat = lambda array: array.reshape(-1, array.shape[-1])
    tokens = flat(inputs).astype(jnp.float32)
    hat_one, scale_one = moments(tokens)
    normed = (hat_one * first_gain + first_shift).astype(jnp.bfloat16)
    projected = dot_nn(normed, inward)
    stacked = lambda array: array.reshape(sequences, -1, array.shape[-1])
    query = stacked((projected[:, :model] + query_bias).astype(jnp.bfloat16))
    keys = [stacked(projected[:, model : 2 * model].astype(jnp.bfloat16))]
    values = [stacked((projected[:, 2 * model :] + value_bias).astype(jnp.bfloat16))]
    core, *planes = bits_of("dp")
    normed_pieces, hats, picked = [normed], [hat_one], [pick_columns(normed, core)]
    for halo in halos:
        halo, query, keys[-1], values[-1], picked[-1] = together(halo, query, keys[-1], values[-1], picked[-1])
        hat, _ = moments(flat(halo).astype(jnp.float32))
        piece = (hat * first_gain + first_shift).astype(jnp.bfloat16)
        normed_pieces.append(piece)
        hats.append(hat)
        both = dot_nn(piece, inward[:, model:])
        keys.append(stacked(both[:, :model].astype(jnp.bfloat16)))
        values.append(stacked((both[:, model:] + value_bias).astype(jnp.bfloat16)))
        picked.append(pick_columns(piece, core))
    scaled, lse = attend(first, head_scale, query, keys, values, start, hops)

    scaled_low = flat(scaled)
    branch = dot_nn(scaled_low, output_full) + output_bias
    hat_post, scale_post = moments(branch)
    middle = tokens + hat_post * post_gain + post_shift
    hat_two, scale_two = moments(middle)
    second = (hat_two * second_gain + second_shift).astype(jnp.bfloat16)
    upper = dot_nn(second, up_full) + up_bias
    phi = 0.5 * (1.0 + lax.erf(upper * 0.7071067811865476))
    hat_middle, scale_middle = moments(upper * phi)
    mixed = (hat_middle * middle_gain + middle_shift).astype(jnp.bfloat16)
    grad_low = flat(cotangent)
    grad_out = grad_low.astype(jnp.float32)
    one_way = [core, *reversed(planes), *bits_of("seq")]
    other_way = [core, *planes, *bits_of("seq")]

    down_sum, up_sum = RowSum(one_way), RowSum(other_way)
    sums = query_key_sum, value_output_sum = RowSum(one_way), RowSum(other_way)
    sequence = Sequence(jnp.zeros((8, 128), jnp.float32))
    other_mixed, own_mixed = pick_columns(mixed, core)
    sent, own_mixed, low = sequence(dot_tn(other_mixed, grad_low).astype(jnp.bfloat16), own_mixed, grad_low)
    down_sum.begin(exchange(sent, *core))
    down_sum.kept = lambda: dot_tn(own_mixed, sequence(low))
    down_sum.step(sequence)

    low = sequence(low)
    grad_mixed = dot_nt(low, down_full)
    slope = phi + upper * (0.3989422804014327 * jnp.exp(-0.5 * upper * upper))
    grad_upper = (norm_back(hat_middle, scale_middle, middle_gain, grad_mixed) * slope).astype(jnp.bfloat16)
    other_second, own_second = pick_columns(second, core)
    grad_upper = sequence(grad_upper)
    sent = dot_tn(other_second, grad_upper).astype(jnp.bfloat16)
    sent, grad_upper = sequence(sent, grad_upper)
    up_sum.begin(exchange(sent, *core))
    down_sum.step(sequence)
    up_sum.kept = lambda: dot_tn(own_second, sequence(grad_upper))
    grad_upper = sequence(grad_upper)
    grad_second = sequence(dot_nt(grad_upper, up_full))
    up_sum.step(sequence)
    grad_second = sequence(grad_second)
    grad_middle = grad_out + norm_back(hat_two, scale_two, second_gain, grad_second)
    grad_branch = norm_back(hat_post, scale_post, post_gain, grad_middle).astype(jnp.bfloat16)
    grad_branch = sequence(grad_branch)
    down_sum.step(sequence)
    grad_branch = sequence(grad_branch)
    grad_scaled = dot_nt(grad_branch, output_full)
    grad_attended = (grad_scaled * jnp.repeat(head_scale, model // head_count)).astype(jnp.bfloat16)
    head_columns = jnp.sum(grad_scaled * scaled_low.astype(jnp.float32), 0)
    head_term = jnp.sum(head_columns.reshape(head_count, -1), -1) / head_scale
    grad_attended = sequence(grad_attended)

    dquery, dkeys, dvalues = attend_back(
        first, head_scale, query, keys, values, start, lse, scaled, stacked(grad_attended), hops
    )
    query_low, *pairs = sequence(flat(dquery), *[flat(d) for d in dkeys], *[flat(d) for d in dvalues])
    down_sum.step(sequence)
    up_sum.step(sequence)
    query_low, *pairs = sequence(query_low, *pairs)
    dkeys, dvalues = pairs[: len(keys)], pairs[len(keys) :]
    back = lambda dkey, dvalue: dot_nt(dkey, inward[:, model : 2 * model]) + dot_nt(dvalue, inward[:, 2 * model :])
    lower = lambda array: lax.ppermute(array, "seq", downward)
    partials = [None] * len(hops)
    carried = None
    if hops:
        partials[-1] = back(dkeys[-1], dvalues[-1])
        carried = lower(sequence(stacked(partials[-1]).astype(jnp.bfloat16)))
    for hop in range(len(hops) - 1):
        partials[hop] = back(*sequence(dkeys[hop + 1], dvalues[hop + 1]))
    for hop in reversed(range(len(hops) - 1)):
        carried, partial = sequence(carried, partials[hop])
        partial = stacked(partial)
        missing = partial.shape[1] - carried.shape[1]
        going = partial + jnp.pad(carried.astype(jnp.float32), ((0, 0), (missing, 0), (0, 0)))
        carried = lower(sequence(going.astype(jnp.bfloat16)))

    picked_scaled = pick_columns(scaled_low, core)
    query_low, grad_branch, *pairs = sequence(query_low, grad_branch, *dkeys, *dvalues)
    dkeys, dvalues = pairs[: len(dkeys)], pairs[len(dkeys) :]

    def four(side):
        return (
            dot_tn(picked[0][side], query_low),
            sum(dot_tn(p[side], d) for p, d in zip(picked, dkeys)),
            sum(dot_tn(p[side], d) for p, d in zip(picked, dvalues)),
            dot_tn(picked_scaled[side], grad_branch),
        )

    sent = sequence(jnp.concatenate([part.astype(jnp.bfloat16) for part in four(0)], 1))
    came = exchange(sent, *core)
    query_low, grad_branch, *pairs = sequence(query_low, grad_branch, *dkeys, *dvalues)
    dkeys, dvalues = pairs[: len(dkeys)], pairs[len(dkeys) :]
    for index, row_sum in enumerate(sums):
        columns = slice(2 * index * model, 2 * (index + 1) * model)
        row_sum.begin(came[:, columns])
        row_sum.kept = lambda index=index: jnp.concatenate(four(1)[2 * index : 2 * (index + 1)], 1)
        row_sum.step(sequence)
    down_sum.step(sequence)

    query_low, dkeys[0], dvalues[0] = sequence(query_low, dkeys[0], dvalues[0])
    own = (
        dot_nt(query_low, inward[:, :model])
        + dot_nt(dkeys[0], inward[:, model : 2 * model])
        + dot_nt(dvalues[0], inward[:, 2 * model :])
    )
    own = sequence(own)
    grad_normed = own
    for row_sum in sums:
        row_sum.step(sequence)
    if hops:
        carried, own = sequence(carried, own)
        grad_normed = own + flat(jnp.pad(carried.astype(jnp.float32), ((0, 0), (rows - carried.shape[1], 0), (0, 0))))
    for row_sum in (*sums, up_sum):
        row_sum.step(sequence)
    own = sequence(own)
    vector = jnp.concatenate(
        [
            head_term,
            jnp.sum(grad_branch.astype(jnp.float32), 0),
            jnp.sum(grad_middle * hat_post, 0),
            jnp.sum(grad_middle, 0),
            jnp.sum(grad_second * hat_two, 0),
            jnp.sum(grad_second, 0),
            jnp.sum(grad_out, 0),
            jnp.sum(own * hat_one, 0) + sum(jnp.sum(p * h, 0) for p, h in zip(partials, hats[1:])),
            jnp.sum(own, 0) + sum(jnp.sum(p, 0) for p in partials),
            jnp.sum(query_low.astype(jnp.float32), 0),
            sum(jnp.sum(d.astype(jnp.float32), 0) for d in dvalues),
            jnp.sum(grad_upper.astype(jnp.float32), 0),
            jnp.sum(grad_mixed * hat_middle, 0),
            jnp.sum(grad_mixed, 0),
        ]
    )
    places = bits_of("dp") + bits_of("seq")

    def sum_vector(vector, count):
        for _ in range(min(count, len(places))):
            vector = sequence(vector + exchange(vector, *places.pop(0)))
        return vector

    vector = sequence(vector)
    grad_normed, mixed, middle = sequence(grad_normed, mixed, middle)
    input_grad = (grad_middle + norm_back(hat_one, scale_one, first_gain, grad_normed)).astype(jnp.bfloat16)
    layer_output = (middle + dot_nn(mixed, down_full) + down_bias).astype(jnp.bfloat16)
    input_grad, layer_output = sequence(input_grad, layer_output)
    vector = sum_vector(vector, 1)
    for row_sum in (*sums, up_sum):
        row_sum.step(sequence)
    vector = sum_vector(vector, 2)
    up_sum.step(sequence)
    vector = sum_vector(vector, len(places))
    for row_sum in (up_sum, *sums, down_sum):
        while row_sum.total is None:
            row_sum.step(sequence)
    vectors = vector + sequence.token[0, 0]

    query_key, value_output = query_key_sum.total, value_output_sum.total
    rest = vectors[head_count:]
    narrow = rest[: 10 * model].reshape(10, model)
    broad = rest[10 * model :].reshape(3, hidden)
    return (
        stacked(layer_output),
        stacked(input_grad),
        query_key[:, :model],
        query_key[:, model:],
        value_output[:, :model],
        value_output[:, model:],
        up_sum.total,
        down_sum.total,
        narrow[6],
        narrow[7],
        narrow[8],
        narrow[9],
        vectors[:head_count],
        narrow[0],
        narrow[1],
        narrow[2],
        narrow[3],
        narrow[4],
        broad[0],
        broad[1],
        broad[2],
        narrow[5],
    )


def solution(mesh):
    sharded, matrix = P("dp", "seq", None), P(BOTH, None)
    in_specs = (sharded, sharded, P("dp", None)) + (matrix,) * 6 + (P(),) * 14
    out_specs = (sharded, sharded) + (matrix,) * 6 + (P(),) * 14
    return jax.shard_map(local, mesh=mesh, in_specs=in_specs, out_specs=out_specs, check_vma=False)
```

```python
import functools

import jax
import jax.numpy as jnp
from jax import lax
from jax.experimental import pallas as pl
from jax.experimental.pallas import tpu as pltpu
from jax.sharding import PartitionSpec as P

EPSILON = 1e-05
MASKED = -1e30
DOCUMENT_MAX = 800
BLOCK = 256
LANES = 256
BOTH = ("dp", "seq")


def dot_nn(a, b):
    return lax.dot_general(a, b, (((1,), (0,)), ((), ())), preferred_element_type=jnp.float32)


def dot_nt(a, b):
    return lax.dot_general(a, b, (((1,), (1,)), ((), ())), preferred_element_type=jnp.float32)


def dot_tn(a, b):
    return lax.dot_general(a, b, (((0,), (0,)), ((), ())), preferred_element_type=jnp.float32)


def moments(values):
    row_mean = jnp.mean(values, -1, keepdims=True)
    centred = values - row_mean
    spread = jnp.mean(centred * centred, -1, keepdims=True)
    scale = lax.rsqrt(spread + EPSILON)
    return centred * scale, scale


def norm_back(hat, scale, gain, grad):
    weighted = gain * grad
    first = jnp.mean(weighted, -1, keepdims=True)
    second = jnp.mean(weighted * hat, -1, keepdims=True)
    return scale * (weighted - first - hat * second)


def pick_lanes(block, head, width):
    lane = lax.broadcasted_iota(jnp.int32, block.shape, 1)
    inside = (lane >= head * width) & (lane < (head + 1) * width)
    return jnp.where(inside, block, jnp.zeros_like(block))


def key_blocks(rows, hops):
    blocks = []
    for block in range(rows // BLOCK):
        blocks.append((0, block * BLOCK, BLOCK, block * BLOCK))
    place = 0
    for hop, hop_rows in enumerate(hops):
        place -= hop_rows
        if hop_rows % BLOCK == 0:
            for block in reversed(range(hop_rows // BLOCK)):
                blocks.append((hop + 1, block * BLOCK, BLOCK, place + block * BLOCK))
        else:
            blocks.append((hop + 1, 0, hop_rows, place))
    return blocks


def mask_scores(scores, first_key, start_row, first_query, diagonal):
    place = first_key + lax.broadcasted_iota(jnp.int32, scores.shape, 0)
    ok = place >= start_row
    if diagonal:
        ok = ok & (place <= first_query + lax.broadcasted_iota(jnp.int32, scores.shape, 1))
    return jnp.where(ok, scores, MASKED)


def attend_kernel(pieces, hops, heads, width, factor, first_ref, scale_ref, q_ref, *refs):
    keys, values = refs[:pieces], refs[pieces : 2 * pieces]
    start_ref, out_ref, lse_ref, qh_ref, m_ref, l_ref, acc_ref = refs[2 * pieces :]
    sequence, group = pl.program_id(0), pl.program_id(1)
    rows = q_ref.shape[1]
    blocks = key_blocks(rows, hops)
    for qi in range(rows // BLOCK):
        first_query = qi * BLOCK
        first = first_ref[sequence, qi]
        start_row = start_ref[0, :, first_query : first_query + BLOCK]
        q_block = q_ref[0, first_query : first_query + BLOCK, :] * factor
        for head in range(heads):
            qh_ref[head] = pick_lanes(q_block, head, width)

        def body(piece, offset, count, place, fresh):
            key = keys[piece][0, offset : offset + count, :]
            value_t = values[piece][0, offset : offset + count, :].T
            for head in range(heads):
                scores = dot_nt(key, qh_ref[head])
                scores = mask_scores(scores, place, start_row, first_query, fresh)
                top = jnp.max(scores, 0, keepdims=True)
                lanes = slice(head * width, (head + 1) * width)
                if fresh:
                    weights = jnp.exp(scores - top)
                    l_ref[head : head + 1] = jnp.sum(weights, 0, keepdims=True)
                    acc_ref[lanes] = dot_nn(value_t[lanes], weights.astype(jnp.bfloat16))
                    m_ref[head : head + 1] = top
                else:
                    before = m_ref[head : head + 1]
                    top = jnp.maximum(before, top)
                    fade = jnp.exp(before - top)
                    weights = jnp.exp(scores - top)
                    l_ref[head : head + 1] = l_ref[head : head + 1] * fade + jnp.sum(weights, 0, keepdims=True)
                    acc_ref[lanes] = acc_ref[lanes] * fade + dot_nn(value_t[lanes], weights.astype(jnp.bfloat16))
                    m_ref[head : head + 1] = top

        body(*blocks[qi], True)
        for block in reversed(blocks[:qi]):
            pl.when(first < block[3] + block[2])(functools.partial(body, *block, False))
        for block in blocks[rows // BLOCK :]:
            pl.when(first < block[3] + block[2])(functools.partial(body, *block, False))
        total = l_ref[...]
        lse_ref[0, 0, :, first_query : first_query + BLOCK] = m_ref[...] + jnp.log(total)
        for head in range(heads):
            lanes = slice(head * width, (head + 1) * width)
            acc_ref[lanes] = acc_ref[lanes] * (scale_ref[group * heads + head] / total[head : head + 1])
        out_ref[0, first_query : first_query + BLOCK, :] = acc_ref[...].T.astype(jnp.bfloat16)


def attention_cost(sequences, rows, counts, head_count, model, products):
    pairs = sequences * head_count * rows * sum(counts)
    return pl.CostEstimate(
        flops=2 * products * pairs * LANES,
        bytes_accessed=4 * products * sequences * sum(counts) * model,
        transcendentals=pairs,
    )


def attend(first, head_scale, query, keys, values, start, hops):
    sequences, rows, model = query.shape
    head_count = head_scale.shape[0]
    width = model // head_count
    heads = LANES // width
    groups = model // LANES
    pieces = len(keys)
    wide = lambda count: pl.BlockSpec((1, count, LANES), lambda s, g, *_: (s, 0, g))
    counts = [k.shape[1] for k in keys]
    kernel = functools.partial(attend_kernel, pieces, hops, heads, width, width ** (-0.5))
    return pl.pallas_call(
        kernel,
        grid_spec=pltpu.PrefetchScalarGridSpec(
            num_scalar_prefetch=2,
            grid=(sequences, groups),
            in_specs=[wide(rows)] + [wide(c) for c in counts] * 2
            + [pl.BlockSpec((1, 1, rows), lambda s, g, *_: (s, 0, 0))],
            out_specs=[wide(rows), pl.BlockSpec((1, 1, heads, rows), lambda s, g, *_: (s, g, 0, 0))],
            scratch_shapes=[
                pltpu.VMEM((heads, BLOCK, LANES), jnp.bfloat16),
                pltpu.VMEM((heads, BLOCK), jnp.float32),
                pltpu.VMEM((heads, BLOCK), jnp.float32),
                pltpu.VMEM((LANES, BLOCK), jnp.float32),
            ],
        ),
        out_shape=[
            jax.ShapeDtypeStruct((sequences, rows, model), jnp.bfloat16),
            jax.ShapeDtypeStruct((sequences, groups, heads, rows), jnp.float32),
        ],
        name="attend",
        cost_estimate=attention_cost(sequences, rows, counts, head_count, model, 3),
    )(first, head_scale, query, *keys, *values, start)


def attend_back_kernel(pieces, hops, heads, width, factor, first_ref, scale_ref, q_ref, *refs):
    keys, values = refs[:pieces], refs[pieces : 2 * pieces]
    start_ref, lse_ref, out_ref, grad_ref = refs[2 * pieces : 2 * pieces + 4]
    dq_ref = refs[2 * pieces + 4]
    dkeys = refs[2 * pieces + 5 : 3 * pieces + 5]
    dvalues = refs[3 * pieces + 5 : 4 * pieces + 5]
    qh_ref, gh_ref, delta_ref, p_ref, ds_ref, dq_acc, dk_acc, dv_acc = refs[4 * pieces + 5 :]
    sequence, group = pl.program_id(0), pl.program_id(1)
    rows = q_ref.shape[1]
    query_blocks = rows // BLOCK
    for qi in range(query_blocks):
        here = slice(qi * BLOCK, (qi + 1) * BLOCK)
        q_block = q_ref[0, here, :] * factor
        grad = grad_ref[0, here, :]
        product = (grad.astype(jnp.float32) * out_ref[0, here, :].astype(jnp.float32)).T
        for head in range(heads):
            lanes = slice(head * width, (head + 1) * width)
            spot = slice(head * BLOCK, (head + 1) * BLOCK)
            qh_ref[qi, spot] = pick_lanes(q_block, head, width)
            gh_ref[qi, spot] = pick_lanes(grad, head, width)
            delta_ref[head : head + 1, here] = jnp.sum(product[lanes], 0, keepdims=True) / scale_ref[group * heads + head]
    dq_acc[...] = jnp.zeros_like(dq_acc)
    for piece, offset, count, place in key_blocks(rows, hops):
        key = keys[piece][0, offset : offset + count, :]
        key_t = key.T
        value = values[piece][0, offset : offset + count, :]
        dk_acc[:count] = jnp.zeros((count, LANES), jnp.float32)
        dv_acc[:count] = jnp.zeros((count, LANES), jnp.float32)
        for qi in range(query_blocks):
            first_query = qi * BLOCK
            if place > first_query:
                continue

            def body():
                here = slice(first_query, first_query + BLOCK)
                start_row = start_ref[0, :, here]
                for head in range(heads):
                    lanes = slice(head * width, (head + 1) * width)
                    spot = slice(head * BLOCK, (head + 1) * BLOCK)
                    scores = dot_nt(key, qh_ref[qi, spot])
                    scores = mask_scores(scores, place, start_row, first_query, place == first_query)
                    weights = jnp.exp(scores - lse_ref[0, 0, head : head + 1, here])
                    dweights = dot_nt(value, gh_ref[qi, spot])
                    dscores = (weights * (dweights - delta_ref[head : head + 1, here])).astype(jnp.bfloat16)
                    p_ref[:count, spot] = weights.astype(jnp.bfloat16)
                    ds_ref[:count, spot] = dscores
                    dq_acc[lanes, here] += dot_nn(key_t[lanes], dscores)
                dv_acc[:count] += dot_nn(p_ref[:count], gh_ref[qi])
                dk_acc[:count] += dot_nn(ds_ref[:count], qh_ref[qi])

            if place == first_query:
                body()
            else:
                pl.when(first_ref[sequence, qi] < place + count)(body)
        dkeys[piece][0, offset : offset + count, :] = dk_acc[:count].astype(jnp.bfloat16)
        dvalues[piece][0, offset : offset + count, :] = dv_acc[:count].astype(jnp.bfloat16)
    for qi in range(query_blocks):
        here = slice(qi * BLOCK, (qi + 1) * BLOCK)
        dq_ref[0, here, :] = (dq_acc[:, here] * factor).T.astype(jnp.bfloat16)


def attend_back(first, head_scale, query, keys, values, start, lse, scaled, grad, hops):
    sequences, rows, model = query.shape
    head_count = head_scale.shape[0]
    width = model // head_count
    heads = LANES // width
    groups = model // LANES
    pieces = len(keys)
    wide = lambda count: pl.BlockSpec((1, count, LANES), lambda s, g, *_: (s, 0, g))
    counts = [k.shape[1] for k in keys]
    most = max([BLOCK] + [c for c in counts if c % BLOCK])
    kernel = functools.partial(attend_back_kernel, pieces, hops, heads, width, width ** (-0.5))
    shape = lambda count: jax.ShapeDtypeStruct((sequences, count, model), jnp.bfloat16)
    results = pl.pallas_call(
        kernel,
        grid_spec=pltpu.PrefetchScalarGridSpec(
            num_scalar_prefetch=2,
            grid=(sequences, groups),
            in_specs=[wide(rows)] + [wide(c) for c in counts] * 2
            + [
                pl.BlockSpec((1, 1, rows), lambda s, g, *_: (s, 0, 0)),
                pl.BlockSpec((1, 1, heads, rows), lambda s, g, *_: (s, g, 0, 0)),
                wide(rows),
                wide(rows),
            ],
            out_specs=[wide(rows)] + [wide(c) for c in counts] * 2,
            scratch_shapes=[
                pltpu.VMEM((rows // BLOCK, heads * BLOCK, LANES), jnp.bfloat16),
                pltpu.VMEM((rows // BLOCK, heads * BLOCK, LANES), jnp.bfloat16),
                pltpu.VMEM((heads, rows), jnp.float32),
                pltpu.VMEM((most, heads * BLOCK), jnp.bfloat16),
                pltpu.VMEM((most, heads * BLOCK), jnp.bfloat16),
                pltpu.VMEM((LANES, rows), jnp.float32),
                pltpu.VMEM((most, LANES), jnp.float32),
                pltpu.VMEM((most, LANES), jnp.float32),
            ],
        ),
        out_shape=[shape(rows)] + [shape(c) for c in counts] * 2,
        name="attend_back",
        cost_estimate=attention_cost(sequences, rows, counts, head_count, model, 5),
    )(first, head_scale, query, *keys, *values, start, lse, scaled, grad)
    return results[0], results[1 : 1 + pieces], results[1 + pieces :]


def halo_rows(rows, ranks):
    hops, left = [], DOCUMENT_MAX - 1
    for _ in range(ranks - 1):
        if left <= 0:
            break
        hops.append(min(rows, -(-left // 32) * 32))
        left -= rows
    return hops


def bits_of(axis):
    return [(axis, bit) for bit in range(lax.axis_size(axis).bit_length() - 1)]


def exchange(array, axis, bit):
    return lax.ppermute(array, axis, [(i, i ^ (1 << bit)) for i in range(lax.axis_size(axis))])


def together(*values):
    return lax.optimization_barrier(values)


def pick_kernel(mine_ref, array_ref, other_ref, own_ref):
    width = own_ref.shape[1]
    halves = array_ref[:, :width], array_ref[:, width:]
    for index in range(2):
        @pl.when(mine_ref[0] == index)
        def _():
            own_ref[...] = halves[index]
            other_ref[...] = halves[1 - index]


def pick_columns(array, place):
    axis, bit = place
    order = bits_of("dp")[::-1] + bits_of("seq")[::-1]
    mine = (lax.axis_index(axis) >> bit) & 1
    tokens, columns = array.shape
    above = 1 << order.index(place)
    width = columns // above // 2
    if width % 128:
        split = array.reshape(tokens, above, 2, width)
        take = lambda index: lax.dynamic_index_in_dim(split, index, 2, keepdims=False).reshape(tokens, -1)
        return take(1 - mine), take(mine)
    half = jax.ShapeDtypeStruct((tokens, columns // 2), array.dtype)
    return pl.pallas_call(
        pick_kernel,
        grid_spec=pltpu.PrefetchScalarGridSpec(
            num_scalar_prefetch=1,
            grid=(above,),
            in_specs=[pl.BlockSpec((tokens, 2 * width), lambda block, _: (0, block))],
            out_specs=[pl.BlockSpec((tokens, width), lambda block, _: (0, block))] * 2,
        ),
        out_shape=[half, half],
        name="pick",
        cost_estimate=pl.CostEstimate(flops=0, bytes_accessed=4 * array.size * array.dtype.itemsize, transcendentals=0),
    )(mine.reshape(1), array)


class Sequence:
    def __init__(self, token):
        self.token = token

    def __call__(self, *values):
        *values, self.token = together(*values, self.token)
        return values[0] if len(values) == 1 else values


def lay_rows(total, width, shares):
    total = total.astype(jnp.bfloat16)
    return [total[:, left : left + width].reshape(shares, -1, width) for left in range(0, total.shape[1], width)]


class RowSum:
    def __init__(self, order):
        self.order = list(order)
        self.left = bits_of("dp")[::-1] + bits_of("seq")[::-1]
        self.came = self.kept = self.total = None

    def begin(self, came):
        self.left.remove(self.order.pop(0))
        self.came = came

    def step(self, sequence):
        if callable(self.kept):
            came, kept = sequence(self.came), self.kept()
        else:
            came, kept = sequence(self.came, self.kept)
        total = kept.astype(jnp.float32) + came.astype(jnp.float32)
        if not self.order:
            self.total = total
            return
        self.send(total, sequence)

    def send(self, total, sequence):
        axis, bit = self.order.pop(0)
        at = self.left.index((axis, bit))
        self.left.pop(at)
        total = total.astype(jnp.bfloat16)
        columns = total.shape[-1]
        split = total.reshape(1 << at, 2, -1, columns)
        mine = (lax.axis_index(axis) >> bit) & 1
        gone = lax.dynamic_index_in_dim(split, 1 - mine, 1, keepdims=False).reshape(-1, columns)
        kept = lax.dynamic_index_in_dim(split, mine, 1, keepdims=False).reshape(-1, columns)
        gone, self.kept = sequence(gone, kept)
        self.came = exchange(gone, axis, bit)


def local(
    inputs,
    cotangent,
    segment_ids,
    query_weight,
    key_weight,
    value_weight,
    output_weight,
    up_weight,
    down_weight,
    first_gain,
    first_shift,
    query_bias,
    value_bias,
    head_scale,
    output_bias,
    post_gain,
    post_shift,
    second_gain,
    second_shift,
    up_bias,
    middle_gain,
    middle_shift,
    down_bias,
):
    sequences, rows, model = inputs.shape
    hidden = up_bias.shape[0]
    head_count = head_scale.shape[0]
    ranks = lax.axis_size("seq")
    rank = lax.axis_index("seq")
    hops = halo_rows(rows, ranks)
    upward = [(i, i + 1) for i in range(ranks - 1)]
    downward = [(i + 1, i) for i in range(ranks - 1)]

    halos = []
    if hops:
        onward = hops[1] if len(hops) > 1 else hops[0]
        shift = lambda array: lax.ppermute(array, "seq", upward)
        moving = shift(inputs[:, rows - onward :])
        nearest = moving
        if onward < hops[0]:
            rest, moving = together(inputs[:, rows - hops[0] : rows - onward], moving)
            nearest = jnp.concatenate([shift(rest), moving], 1)
        halos.append(nearest)
        for hop_rows in hops[1:]:
            moving = shift(moving[:, moving.shape[1] - hop_rows :])
            halos.append(moving)

    inward = jnp.concatenate([query_weight, key_weight, value_weight], 1)
    inward = lax.all_gather(inward, BOTH, axis=0, tiled=True)
    outward = lax.all_gather(jnp.concatenate([output_weight, up_weight], 1), BOTH, axis=0, tiled=True)
    down_full = lax.all_gather(down_weight, BOTH, axis=0, tiled=True)
    output_full, up_full = outward[:, :model], outward[:, model:]

    own_ids = lax.dynamic_slice_in_dim(segment_ids, rank * rows, rows, 1)
    start = jnp.sum((segment_ids[:, None, :] < own_ids[:, :, None]).astype(jnp.int32), -1) - rank * rows
    first = start[:, ::BLOCK]
    start = start[:, None, :]

    flat = lambda array: array.reshape(-1, array.shape[-1])
    tokens = flat(inputs).astype(jnp.float32)
    hat_one, scale_one = moments(tokens)
    normed = (hat_one * first_gain + first_shift).astype(jnp.bfloat16)
    projected = dot_nn(normed, inward)
    stacked = lambda array: array.reshape(sequences, -1, array.shape[-1])
    query = stacked((projected[:, :model] + query_bias).astype(jnp.bfloat16))
    keys = [stacked(projected[:, model : 2 * model].astype(jnp.bfloat16))]
    values = [stacked((projected[:, 2 * model :] + value_bias).astype(jnp.bfloat16))]
    core, *planes = bits_of("dp")
    normed_pieces, hats, picked = [normed], [hat_one], [pick_columns(normed, core)]
    for halo in halos:
        halo, query, keys[-1], values[-1], picked[-1] = together(halo, query, keys[-1], values[-1], picked[-1])
        hat, _ = moments(flat(halo).astype(jnp.float32))
        piece = (hat * first_gain + first_shift).astype(jnp.bfloat16)
        normed_pieces.append(piece)
        hats.append(hat)
        both = dot_nn(piece, inward[:, model:])
        keys.append(stacked(both[:, :model].astype(jnp.bfloat16)))
        values.append(stacked((both[:, model:] + value_bias).astype(jnp.bfloat16)))
        picked.append(pick_columns(piece, core))
    scaled, lse = attend(first, head_scale, query, keys, values, start, hops)

    scaled_low = flat(scaled)
    branch = dot_nn(scaled_low, output_full) + output_bias
    hat_post, scale_post = moments(branch)
    middle = tokens + hat_post * post_gain + post_shift
    hat_two, scale_two = moments(middle)
    second = (hat_two * second_gain + second_shift).astype(jnp.bfloat16)
    upper = dot_nn(second, up_full) + up_bias
    phi = 0.5 * (1.0 + lax.erf(upper * 0.7071067811865476))
    hat_middle, scale_middle = moments(upper * phi)
    mixed = (hat_middle * middle_gain + middle_shift).astype(jnp.bfloat16)
    grad_low = flat(cotangent)
    grad_out = grad_low.astype(jnp.float32)
    one_way, other_way = [core, *reversed(planes)], [core, *planes]

    down_sum, up_sum = RowSum(one_way), RowSum(other_way)
    sums = query_key_sum, value_output_sum = RowSum(one_way), RowSum(other_way)
    sequence = Sequence(jnp.zeros((8, 128), jnp.float32))
    other_mixed, own_mixed = pick_columns(mixed, core)
    sent, own_mixed, low = sequence(dot_tn(other_mixed, grad_low).astype(jnp.bfloat16), own_mixed, grad_low)
    down_sum.begin(exchange(sent, *core))
    down_sum.kept = lambda: dot_tn(own_mixed, sequence(low))
    down_sum.step(sequence)

    low = sequence(low)
    grad_mixed = dot_nt(low, down_full)
    slope = phi + upper * (0.3989422804014327 * jnp.exp(-0.5 * upper * upper))
    grad_upper = (norm_back(hat_middle, scale_middle, middle_gain, grad_mixed) * slope).astype(jnp.bfloat16)
    other_second, own_second = pick_columns(second, core)
    grad_upper = sequence(grad_upper)
    sent = dot_tn(other_second, grad_upper).astype(jnp.bfloat16)
    sent, grad_upper = sequence(sent, grad_upper)
    up_sum.begin(exchange(sent, *core))
    up_sum.kept = lambda: dot_tn(own_second, sequence(grad_upper))
    grad_upper = sequence(grad_upper)
    grad_second = sequence(dot_nt(grad_upper, up_full))
    up_sum.step(sequence)
    grad_second = sequence(grad_second)
    grad_middle = grad_out + norm_back(hat_two, scale_two, second_gain, grad_second)
    grad_branch = norm_back(hat_post, scale_post, post_gain, grad_middle).astype(jnp.bfloat16)
    grad_branch = sequence(grad_branch)
    grad_scaled = dot_nt(grad_branch, output_full)
    grad_attended = (grad_scaled * jnp.repeat(head_scale, model // head_count)).astype(jnp.bfloat16)
    head_columns = jnp.sum(grad_scaled * scaled_low.astype(jnp.float32), 0)
    head_term = jnp.sum(head_columns.reshape(head_count, -1), -1) / head_scale
    grad_attended = sequence(grad_attended)

    dquery, dkeys, dvalues = attend_back(
        first, head_scale, query, keys, values, start, lse, scaled, stacked(grad_attended), hops
    )
    query_low, *pairs = sequence(flat(dquery), *[flat(d) for d in dkeys], *[flat(d) for d in dvalues])
    down_sum.step(sequence)
    up_sum.step(sequence)
    query_low, *pairs = sequence(query_low, *pairs)
    dkeys, dvalues = pairs[: len(keys)], pairs[len(keys) :]
    back = lambda dkey, dvalue: dot_nt(dkey, inward[:, model : 2 * model]) + dot_nt(dvalue, inward[:, 2 * model :])
    lower = lambda array: lax.ppermute(array, "seq", downward)
    partials = [None] * len(hops)
    carried = None
    if hops:
        partials[-1] = back(dkeys[-1], dvalues[-1])
        carried = lower(sequence(stacked(partials[-1]).astype(jnp.bfloat16)))
    for hop in range(len(hops) - 1):
        partials[hop] = back(*sequence(dkeys[hop + 1], dvalues[hop + 1]))
    for hop in reversed(range(len(hops) - 1)):
        carried, partial = sequence(carried, partials[hop])
        partial = stacked(partial)
        missing = partial.shape[1] - carried.shape[1]
        going = partial + jnp.pad(carried.astype(jnp.float32), ((0, 0), (missing, 0), (0, 0)))
        carried = lower(sequence(going.astype(jnp.bfloat16)))

    picked_scaled = pick_columns(scaled_low, core)
    query_low, grad_branch, *pairs = sequence(query_low, grad_branch, *dkeys, *dvalues)
    dkeys, dvalues = pairs[: len(dkeys)], pairs[len(dkeys) :]

    def four(side):
        return (
            dot_tn(picked[0][side], query_low),
            sum(dot_tn(p[side], d) for p, d in zip(picked, dkeys)),
            sum(dot_tn(p[side], d) for p, d in zip(picked, dvalues)),
            dot_tn(picked_scaled[side], grad_branch),
        )

    sent = sequence(jnp.concatenate([part.astype(jnp.bfloat16) for part in four(0)], 1))
    came = exchange(sent, *core)

    def join(row_sums, width):
        for row_sum in row_sums:
            while row_sum.total is None:
                row_sum.step(sequence)
        joint = RowSum(bits_of("seq"))
        joint.left = bits_of("seq")[::-1]
        pieces = [piece for row_sum in row_sums for piece in lay_rows(row_sum.total, width, ranks)]
        joint.send(jnp.concatenate(pieces, 1).reshape(-1, width), sequence)
        return joint

    outer = join([down_sum, up_sum], model)
    query_low, grad_branch, *pairs = sequence(query_low, grad_branch, *dkeys, *dvalues)
    dkeys, dvalues = pairs[: len(dkeys)], pairs[len(dkeys) :]
    for index, row_sum in enumerate(sums):
        columns = slice(2 * index * model, 2 * (index + 1) * model)
        row_sum.begin(came[:, columns])
        row_sum.kept = lambda index=index: jnp.concatenate(four(1)[2 * index : 2 * (index + 1)], 1)
        row_sum.step(sequence)

    query_low, dkeys[0], dvalues[0] = sequence(query_low, dkeys[0], dvalues[0])
    own = (
        dot_nt(query_low, inward[:, :model])
        + dot_nt(dkeys[0], inward[:, model : 2 * model])
        + dot_nt(dvalues[0], inward[:, 2 * model :])
    )
    own = sequence(own)
    for row_sum in sums:
        row_sum.step(sequence)
    outer.step(sequence)
    own = sequence(own)
    vector = jnp.concatenate(
        [
            head_term,
            jnp.sum(grad_branch.astype(jnp.float32), 0),
            jnp.sum(grad_middle * hat_post, 0),
            jnp.sum(grad_middle, 0),
            jnp.sum(grad_second * hat_two, 0),
            jnp.sum(grad_second, 0),
            jnp.sum(grad_out, 0),
            jnp.sum(own * hat_one, 0) + sum(jnp.sum(p * h, 0) for p, h in zip(partials, hats[1:])),
            jnp.sum(own, 0) + sum(jnp.sum(p, 0) for p in partials),
            jnp.sum(query_low.astype(jnp.float32), 0),
            sum(jnp.sum(d.astype(jnp.float32), 0) for d in dvalues),
            jnp.sum(grad_upper.astype(jnp.float32), 0),
            jnp.sum(grad_mixed * hat_middle, 0),
            jnp.sum(grad_mixed, 0),
        ]
    )
    places = bits_of("dp") + bits_of("seq")
    vector = sequence(vector)
    vector_came = exchange(vector, *places.pop(0))

    def add_vector(vector, vector_came):
        if vector_came is not None:
            vector = sequence(vector + vector_came)
            vector_came = exchange(vector, *places.pop(0)) if places else None
        return vector, vector_came

    grad_normed = own
    if hops:
        carried, own = sequence(carried, own)
        grad_normed = own + flat(jnp.pad(carried.astype(jnp.float32), ((0, 0), (rows - carried.shape[1], 0), (0, 0))))
    vector, vector_came = add_vector(vector, vector_came)
    inner = join(sums, 2 * model)
    vector, vector_came = add_vector(vector, vector_came)
    grad_normed, mixed, middle = sequence(grad_normed, mixed, middle)
    input_grad = (grad_middle + norm_back(hat_one, scale_one, first_gain, grad_normed)).astype(jnp.bfloat16)
    input_grad = sequence(input_grad)
    vector, vector_came = add_vector(vector, vector_came)
    mixed, middle = sequence(mixed, middle)
    layer_output = (middle + dot_nn(mixed, down_full) + down_bias).astype(jnp.bfloat16)
    layer_output = sequence(layer_output)
    inner.step(sequence)
    while vector_came is not None:
        vector, vector_came = add_vector(vector, vector_came)
    for joint in (outer, inner):
        while joint.total is None:
            joint.step(sequence)
    vectors = vector + sequence.token[0, 0]

    share = down_weight.shape[0]
    down_total, outer_total = outer.total[:share], outer.total[share:]
    up_total = jnp.concatenate(jnp.split(outer_total, hidden // model), 1)
    query_key, value_output = jnp.split(inner.total, 2)
    rest = vectors[head_count:]
    narrow = rest[: 10 * model].reshape(10, model)
    broad = rest[10 * model :].reshape(3, hidden)
    return (
        stacked(layer_output),
        stacked(input_grad),
        query_key[:, :model],
        query_key[:, model:],
        value_output[:, :model],
        value_output[:, model:],
        up_total,
        down_total,
        narrow[6],
        narrow[7],
        narrow[8],
        narrow[9],
        vectors[:head_count],
        narrow[0],
        narrow[1],
        narrow[2],
        narrow[3],
        narrow[4],
        broad[0],
        broad[1],
        broad[2],
        narrow[5],
    )


def solution(mesh):
    sharded, matrix = P("dp", "seq", None), P(BOTH, None)
    in_specs = (sharded, sharded, P("dp", None)) + (matrix,) * 6 + (P(),) * 14
    out_specs = (sharded, sharded) + (matrix,) * 6 + (P(),) * 14
    return jax.shard_map(local, mesh=mesh, in_specs=in_specs, out_specs=out_specs, check_vma=False)
```

```python
import functools

import jax
import jax.numpy as jnp
from jax import lax
from jax.experimental import pallas as pl
from jax.experimental.pallas import tpu as pltpu
from jax.sharding import PartitionSpec as P

EPSILON = 1e-05
MASKED = -1e30
DOCUMENT_MAX = 800
BLOCK = 256
LANES = 256
BOTH = ("dp", "seq")


def dot_nn(a, b):
    return lax.dot_general(a, b, (((1,), (0,)), ((), ())), preferred_element_type=jnp.float32)


def dot_nt(a, b):
    return lax.dot_general(a, b, (((1,), (1,)), ((), ())), preferred_element_type=jnp.float32)


def dot_tn(a, b):
    return lax.dot_general(a, b, (((0,), (0,)), ((), ())), preferred_element_type=jnp.float32)


def moments(values):
    row_mean = jnp.mean(values, -1, keepdims=True)
    centred = values - row_mean
    spread = jnp.mean(centred * centred, -1, keepdims=True)
    scale = lax.rsqrt(spread + EPSILON)
    return centred * scale, scale


def norm_back(hat, scale, gain, grad):
    weighted = gain * grad
    first = jnp.mean(weighted, -1, keepdims=True)
    second = jnp.mean(weighted * hat, -1, keepdims=True)
    return scale * (weighted - first - hat * second)


def pick_lanes(block, head, width):
    lane = lax.broadcasted_iota(jnp.int32, block.shape, 1)
    inside = (lane >= head * width) & (lane < (head + 1) * width)
    return jnp.where(inside, block, jnp.zeros_like(block))


def key_blocks(rows, hops):
    blocks = []
    for block in range(rows // BLOCK):
        blocks.append((0, block * BLOCK, BLOCK, block * BLOCK))
    place = 0
    for hop, hop_rows in enumerate(hops):
        place -= hop_rows
        if hop_rows % BLOCK == 0:
            for block in reversed(range(hop_rows // BLOCK)):
                blocks.append((hop + 1, block * BLOCK, BLOCK, place + block * BLOCK))
        else:
            blocks.append((hop + 1, 0, hop_rows, place))
    return blocks


def mask_scores(scores, first_key, start_row, first_query, diagonal):
    place = first_key + lax.broadcasted_iota(jnp.int32, scores.shape, 0)
    ok = place >= start_row
    if diagonal:
        ok = ok & (place <= first_query + lax.broadcasted_iota(jnp.int32, scores.shape, 1))
    return jnp.where(ok, scores, MASKED)


def attend_kernel(pieces, hops, heads, width, factor, first_ref, scale_ref, q_ref, *refs):
    keys, values = refs[:pieces], refs[pieces : 2 * pieces]
    start_ref, out_ref, lse_ref, qh_ref, m_ref, l_ref, acc_ref = refs[2 * pieces :]
    sequence, group = pl.program_id(0), pl.program_id(1)
    rows = q_ref.shape[1]
    blocks = key_blocks(rows, hops)
    for qi in range(rows // BLOCK):
        first_query = qi * BLOCK
        first = first_ref[sequence, qi]
        start_row = start_ref[0, :, first_query : first_query + BLOCK]
        q_block = q_ref[0, first_query : first_query + BLOCK, :] * factor
        for head in range(heads):
            qh_ref[head] = pick_lanes(q_block, head, width)

        def body(piece, offset, count, place, fresh):
            key = keys[piece][0, offset : offset + count, :]
            value_t = values[piece][0, offset : offset + count, :].T
            for head in range(heads):
                scores = dot_nt(key, qh_ref[head])
                scores = mask_scores(scores, place, start_row, first_query, fresh)
                top = jnp.max(scores, 0, keepdims=True)
                lanes = slice(head * width, (head + 1) * width)
                if fresh:
                    weights = jnp.exp(scores - top)
                    l_ref[head : head + 1] = jnp.sum(weights, 0, keepdims=True)
                    acc_ref[lanes] = dot_nn(value_t[lanes], weights.astype(jnp.bfloat16))
                    m_ref[head : head + 1] = top
                else:
                    before = m_ref[head : head + 1]
                    top = jnp.maximum(before, top)
                    fade = jnp.exp(before - top)
                    weights = jnp.exp(scores - top)
                    l_ref[head : head + 1] = l_ref[head : head + 1] * fade + jnp.sum(weights, 0, keepdims=True)
                    acc_ref[lanes] = acc_ref[lanes] * fade + dot_nn(value_t[lanes], weights.astype(jnp.bfloat16))
                    m_ref[head : head + 1] = top

        body(*blocks[qi], True)
        for block in reversed(blocks[:qi]):
            pl.when(first < block[3] + block[2])(functools.partial(body, *block, False))
        for block in blocks[rows // BLOCK :]:
            pl.when(first < block[3] + block[2])(functools.partial(body, *block, False))
        total = l_ref[...]
        lse_ref[0, 0, :, first_query : first_query + BLOCK] = m_ref[...] + jnp.log(total)
        for head in range(heads):
            lanes = slice(head * width, (head + 1) * width)
            acc_ref[lanes] = acc_ref[lanes] * (scale_ref[group * heads + head] / total[head : head + 1])
        out_ref[0, first_query : first_query + BLOCK, :] = acc_ref[...].T.astype(jnp.bfloat16)


def attention_cost(sequences, rows, counts, head_count, model, products):
    pairs = sequences * head_count * rows * sum(counts)
    return pl.CostEstimate(
        flops=2 * products * pairs * LANES,
        bytes_accessed=4 * products * sequences * sum(counts) * model,
        transcendentals=pairs,
    )


def attend(first, head_scale, query, keys, values, start, hops):
    sequences, rows, model = query.shape
    head_count = head_scale.shape[0]
    width = model // head_count
    heads = LANES // width
    groups = model // LANES
    pieces = len(keys)
    wide = lambda count: pl.BlockSpec((1, count, LANES), lambda s, g, *_: (s, 0, g))
    counts = [k.shape[1] for k in keys]
    kernel = functools.partial(attend_kernel, pieces, hops, heads, width, width ** (-0.5))
    return pl.pallas_call(
        kernel,
        grid_spec=pltpu.PrefetchScalarGridSpec(
            num_scalar_prefetch=2,
            grid=(sequences, groups),
            in_specs=[wide(rows)] + [wide(c) for c in counts] * 2
            + [pl.BlockSpec((1, 1, rows), lambda s, g, *_: (s, 0, 0))],
            out_specs=[wide(rows), pl.BlockSpec((1, 1, heads, rows), lambda s, g, *_: (s, g, 0, 0))],
            scratch_shapes=[
                pltpu.VMEM((heads, BLOCK, LANES), jnp.bfloat16),
                pltpu.VMEM((heads, BLOCK), jnp.float32),
                pltpu.VMEM((heads, BLOCK), jnp.float32),
                pltpu.VMEM((LANES, BLOCK), jnp.float32),
            ],
        ),
        out_shape=[
            jax.ShapeDtypeStruct((sequences, rows, model), jnp.bfloat16),
            jax.ShapeDtypeStruct((sequences, groups, heads, rows), jnp.float32),
        ],
        name="attend",
        cost_estimate=attention_cost(sequences, rows, counts, head_count, model, 3),
    )(first, head_scale, query, *keys, *values, start)


def attend_back_kernel(pieces, hops, heads, width, factor, first_ref, scale_ref, q_ref, *refs):
    keys, values = refs[:pieces], refs[pieces : 2 * pieces]
    start_ref, lse_ref, out_ref, grad_ref = refs[2 * pieces : 2 * pieces + 4]
    dq_ref = refs[2 * pieces + 4]
    dkeys = refs[2 * pieces + 5 : 3 * pieces + 5]
    dvalues = refs[3 * pieces + 5 : 4 * pieces + 5]
    qh_ref, gh_ref, delta_ref, p_ref, ds_ref, dq_acc, dk_acc, dv_acc = refs[4 * pieces + 5 :]
    sequence, group = pl.program_id(0), pl.program_id(1)
    rows = q_ref.shape[1]
    query_blocks = rows // BLOCK
    for qi in range(query_blocks):
        here = slice(qi * BLOCK, (qi + 1) * BLOCK)
        q_block = q_ref[0, here, :] * factor
        grad = grad_ref[0, here, :]
        product = (grad.astype(jnp.float32) * out_ref[0, here, :].astype(jnp.float32)).T
        for head in range(heads):
            lanes = slice(head * width, (head + 1) * width)
            spot = slice(head * BLOCK, (head + 1) * BLOCK)
            qh_ref[qi, spot] = pick_lanes(q_block, head, width)
            gh_ref[qi, spot] = pick_lanes(grad, head, width)
            delta_ref[head : head + 1, here] = jnp.sum(product[lanes], 0, keepdims=True) / scale_ref[group * heads + head]
    dq_acc[...] = jnp.zeros_like(dq_acc)
    for piece, offset, count, place in key_blocks(rows, hops):
        key = keys[piece][0, offset : offset + count, :]
        key_t = key.T
        value = values[piece][0, offset : offset + count, :]
        dk_acc[:count] = jnp.zeros((count, LANES), jnp.float32)
        dv_acc[:count] = jnp.zeros((count, LANES), jnp.float32)
        for qi in range(query_blocks):
            first_query = qi * BLOCK
            if place > first_query:
                continue

            def body():
                here = slice(first_query, first_query + BLOCK)
                start_row = start_ref[0, :, here]
                for head in range(heads):
                    lanes = slice(head * width, (head + 1) * width)
                    spot = slice(head * BLOCK, (head + 1) * BLOCK)
                    scores = dot_nt(key, qh_ref[qi, spot])
                    scores = mask_scores(scores, place, start_row, first_query, place == first_query)
                    weights = jnp.exp(scores - lse_ref[0, 0, head : head + 1, here])
                    dweights = dot_nt(value, gh_ref[qi, spot])
                    dscores = (weights * (dweights - delta_ref[head : head + 1, here])).astype(jnp.bfloat16)
                    p_ref[:count, spot] = weights.astype(jnp.bfloat16)
                    ds_ref[:count, spot] = dscores
                    dq_acc[lanes, here] += dot_nn(key_t[lanes], dscores)
                dv_acc[:count] += dot_nn(p_ref[:count], gh_ref[qi])
                dk_acc[:count] += dot_nn(ds_ref[:count], qh_ref[qi])

            if place == first_query:
                body()
            else:
                pl.when(first_ref[sequence, qi] < place + count)(body)
        dkeys[piece][0, offset : offset + count, :] = dk_acc[:count].astype(jnp.bfloat16)
        dvalues[piece][0, offset : offset + count, :] = dv_acc[:count].astype(jnp.bfloat16)
    for qi in range(query_blocks):
        here = slice(qi * BLOCK, (qi + 1) * BLOCK)
        dq_ref[0, here, :] = (dq_acc[:, here] * factor).T.astype(jnp.bfloat16)


def attend_back(first, head_scale, query, keys, values, start, lse, scaled, grad, hops):
    sequences, rows, model = query.shape
    head_count = head_scale.shape[0]
    width = model // head_count
    heads = LANES // width
    groups = model // LANES
    pieces = len(keys)
    wide = lambda count: pl.BlockSpec((1, count, LANES), lambda s, g, *_: (s, 0, g))
    counts = [k.shape[1] for k in keys]
    most = max([BLOCK] + [c for c in counts if c % BLOCK])
    kernel = functools.partial(attend_back_kernel, pieces, hops, heads, width, width ** (-0.5))
    shape = lambda count: jax.ShapeDtypeStruct((sequences, count, model), jnp.bfloat16)
    results = pl.pallas_call(
        kernel,
        grid_spec=pltpu.PrefetchScalarGridSpec(
            num_scalar_prefetch=2,
            grid=(sequences, groups),
            in_specs=[wide(rows)] + [wide(c) for c in counts] * 2
            + [
                pl.BlockSpec((1, 1, rows), lambda s, g, *_: (s, 0, 0)),
                pl.BlockSpec((1, 1, heads, rows), lambda s, g, *_: (s, g, 0, 0)),
                wide(rows),
                wide(rows),
            ],
            out_specs=[wide(rows)] + [wide(c) for c in counts] * 2,
            scratch_shapes=[
                pltpu.VMEM((rows // BLOCK, heads * BLOCK, LANES), jnp.bfloat16),
                pltpu.VMEM((rows // BLOCK, heads * BLOCK, LANES), jnp.bfloat16),
                pltpu.VMEM((heads, rows), jnp.float32),
                pltpu.VMEM((most, heads * BLOCK), jnp.bfloat16),
                pltpu.VMEM((most, heads * BLOCK), jnp.bfloat16),
                pltpu.VMEM((LANES, rows), jnp.float32),
                pltpu.VMEM((most, LANES), jnp.float32),
                pltpu.VMEM((most, LANES), jnp.float32),
            ],
        ),
        out_shape=[shape(rows)] + [shape(c) for c in counts] * 2,
        name="attend_back",
        cost_estimate=attention_cost(sequences, rows, counts, head_count, model, 5),
    )(first, head_scale, query, *keys, *values, start, lse, scaled, grad)
    return results[0], results[1 : 1 + pieces], results[1 + pieces :]


def halo_rows(rows, ranks):
    hops, left = [], DOCUMENT_MAX - 1
    for _ in range(ranks - 1):
        if left <= 0:
            break
        hops.append(min(rows, -(-left // 32) * 32))
        left -= rows
    return hops


def bits_of(axis):
    return [(axis, bit) for bit in range(lax.axis_size(axis).bit_length() - 1)]


def exchange(array, axis, bit):
    return lax.ppermute(array, axis, [(i, i ^ (1 << bit)) for i in range(lax.axis_size(axis))])


def together(*values):
    return lax.optimization_barrier(values)


def pick_kernel(mine_ref, array_ref, other_ref, own_ref):
    width = own_ref.shape[1]
    halves = array_ref[:, :width], array_ref[:, width:]
    for index in range(2):
        @pl.when(mine_ref[0] == index)
        def _():
            own_ref[...] = halves[index]
            other_ref[...] = halves[1 - index]


def pick_columns(array, place):
    axis, bit = place
    order = bits_of("dp")[::-1] + bits_of("seq")[::-1]
    mine = (lax.axis_index(axis) >> bit) & 1
    tokens, columns = array.shape
    above = 1 << order.index(place)
    width = columns // above // 2
    if width % 128:
        split = array.reshape(tokens, above, 2, width)
        take = lambda index: lax.dynamic_index_in_dim(split, index, 2, keepdims=False).reshape(tokens, -1)
        return take(1 - mine), take(mine)
    half = jax.ShapeDtypeStruct((tokens, columns // 2), array.dtype)
    return pl.pallas_call(
        pick_kernel,
        grid_spec=pltpu.PrefetchScalarGridSpec(
            num_scalar_prefetch=1,
            grid=(above,),
            in_specs=[pl.BlockSpec((tokens, 2 * width), lambda block, _: (0, block))],
            out_specs=[pl.BlockSpec((tokens, width), lambda block, _: (0, block))] * 2,
        ),
        out_shape=[half, half],
        name="pick",
        cost_estimate=pl.CostEstimate(flops=0, bytes_accessed=4 * array.size * array.dtype.itemsize, transcendentals=0),
    )(mine.reshape(1), array)


class Sequence:
    def __init__(self, token):
        self.token = token

    def __call__(self, *values):
        *values, self.token = together(*values, self.token)
        return values[0] if len(values) == 1 else values


def lay_rows(total, width, shares):
    total = total.astype(jnp.bfloat16)
    return [total[:, left : left + width].reshape(shares, -1, width) for left in range(0, total.shape[1], width)]


class RowSum:
    def __init__(self, order):
        self.order = list(order)
        self.left = bits_of("dp")[::-1] + bits_of("seq")[::-1]
        self.came = self.kept = self.total = None

    def begin(self, came):
        self.left.remove(self.order.pop(0))
        self.came = came

    def step(self, sequence):
        came, kept = sequence(self.came), self.kept()
        total = kept.astype(jnp.float32) + came.reshape(kept.shape).astype(jnp.float32)
        total = total.reshape(-1, total.shape[-1])
        if not self.order:
            self.total = total
            return
        self.send(total, sequence)

    def send(self, total, sequence):
        axis, bit = self.order.pop(0)
        at = self.left.index((axis, bit))
        self.left.pop(at)
        total = total.astype(jnp.bfloat16)
        columns = total.shape[-1]
        split = total.reshape(1 << at, 2, -1, columns)
        mine = (lax.axis_index(axis) >> bit) & 1
        take = lambda rows, index: lax.dynamic_index_in_dim(rows, index, 1, keepdims=False)
        gone, split = sequence(take(split, 1 - mine).reshape(-1, columns), split)
        self.kept = lambda: take(split, mine)
        self.came = exchange(gone, axis, bit)


def local(
    inputs,
    cotangent,
    segment_ids,
    query_weight,
    key_weight,
    value_weight,
    output_weight,
    up_weight,
    down_weight,
    first_gain,
    first_shift,
    query_bias,
    value_bias,
    head_scale,
    output_bias,
    post_gain,
    post_shift,
    second_gain,
    second_shift,
    up_bias,
    middle_gain,
    middle_shift,
    down_bias,
):
    sequences, rows, model = inputs.shape
    hidden = up_bias.shape[0]
    head_count = head_scale.shape[0]
    ranks = lax.axis_size("seq")
    rank = lax.axis_index("seq")
    hops = halo_rows(rows, ranks)
    upward = [(i, i + 1) for i in range(ranks - 1)]
    downward = [(i + 1, i) for i in range(ranks - 1)]

    halos = []
    if hops:
        onward = hops[1] if len(hops) > 1 else hops[0]
        shift = lambda array: lax.ppermute(array, "seq", upward)
        moving = shift(inputs[:, rows - onward :])
        nearest = moving
        if onward < hops[0]:
            rest, moving = together(inputs[:, rows - hops[0] : rows - onward], moving)
            nearest = jnp.concatenate([shift(rest), moving], 1)
        halos.append(nearest)
        for hop_rows in hops[1:]:
            moving = shift(moving[:, moving.shape[1] - hop_rows :])
            halos.append(moving)

    inward = jnp.concatenate([query_weight, key_weight, value_weight], 1)
    inward = lax.all_gather(inward, BOTH, axis=0, tiled=True)
    outward = lax.all_gather(jnp.concatenate([output_weight, up_weight], 1), BOTH, axis=0, tiled=True)
    down_full = lax.all_gather(down_weight, BOTH, axis=0, tiled=True)
    output_full, up_full = outward[:, :model], outward[:, model:]

    own_ids = lax.dynamic_slice_in_dim(segment_ids, rank * rows, rows, 1)
    start = jnp.sum((segment_ids[:, None, :] < own_ids[:, :, None]).astype(jnp.int32), -1) - rank * rows
    first = start[:, ::BLOCK]
    start = start[:, None, :]

    flat = lambda array: array.reshape(-1, array.shape[-1])
    tokens = flat(inputs).astype(jnp.float32)
    hat_one, scale_one = moments(tokens)
    normed = (hat_one * first_gain + first_shift).astype(jnp.bfloat16)
    projected = dot_nn(normed, inward)
    stacked = lambda array: array.reshape(sequences, -1, array.shape[-1])
    query = stacked((projected[:, :model] + query_bias).astype(jnp.bfloat16))
    keys = [stacked(projected[:, model : 2 * model].astype(jnp.bfloat16))]
    values = [stacked((projected[:, 2 * model :] + value_bias).astype(jnp.bfloat16))]
    core, *planes = bits_of("dp")
    normed_pieces, hats = [normed], [hat_one]
    for halo in halos:
        halo, query, keys[-1], values[-1] = together(halo, query, keys[-1], values[-1])
        hat, _ = moments(flat(halo).astype(jnp.float32))
        piece = (hat * first_gain + first_shift).astype(jnp.bfloat16)
        normed_pieces.append(piece)
        hats.append(hat)
        both = dot_nn(piece, inward[:, model:])
        keys.append(stacked(both[:, :model].astype(jnp.bfloat16)))
        values.append(stacked((both[:, model:] + value_bias).astype(jnp.bfloat16)))
    scaled, lse = attend(first, head_scale, query, keys, values, start, hops)

    scaled_low, *normed_pieces = together(flat(scaled), *normed_pieces)
    picked = [pick_columns(piece, core) for piece in normed_pieces]
    branch = dot_nn(scaled_low, output_full) + output_bias
    hat_post, scale_post = moments(branch)
    middle = tokens + hat_post * post_gain + post_shift
    hat_two, scale_two = moments(middle)
    second = (hat_two * second_gain + second_shift).astype(jnp.bfloat16)
    upper = dot_nn(second, up_full) + up_bias
    phi = 0.5 * (1.0 + lax.erf(upper * 0.7071067811865476))
    bent = upper * phi
    bent_mean = jnp.mean(bent, -1, keepdims=True)
    bent_spread = jnp.maximum(jnp.mean(bent * bent, -1, keepdims=True) - bent_mean * bent_mean, 0.0)
    scale_middle = lax.rsqrt(bent_spread + EPSILON)
    hat_middle = (bent - bent_mean) * scale_middle
    mixed = (hat_middle * middle_gain + middle_shift).astype(jnp.bfloat16)
    grad_low = flat(cotangent)
    grad_out = grad_low.astype(jnp.float32)
    one_way, other_way = [core, *reversed(planes)], [core, *planes]

    down_sum, up_sum = RowSum(one_way), RowSum(other_way)
    sums = query_key_sum, value_output_sum = RowSum(one_way), RowSum(other_way)
    sequence = Sequence(jnp.zeros((8, 128), jnp.float32))
    down_sum.send(dot_tn(mixed, grad_low), sequence)

    low = sequence(grad_low)
    grad_mixed = dot_nt(low, down_full)
    slope = phi + upper * (0.3989422804014327 * jnp.exp(-0.5 * upper * upper))
    grad_upper = (norm_back(hat_middle, scale_middle, middle_gain, grad_mixed) * slope).astype(jnp.bfloat16)
    grad_upper = sequence(grad_upper)
    down_sum.step(sequence)
    up_sum.send(dot_tn(second, sequence(grad_upper)), sequence)
    grad_upper = sequence(grad_upper)
    grad_second = sequence(dot_nt(grad_upper, up_full))
    up_sum.step(sequence)
    grad_second = sequence(grad_second)
    grad_middle = grad_out + norm_back(hat_two, scale_two, second_gain, grad_second)
    grad_branch = norm_back(hat_post, scale_post, post_gain, grad_middle).astype(jnp.bfloat16)
    grad_branch = sequence(grad_branch)
    grad_scaled = dot_nt(grad_branch, output_full)
    grad_attended = (grad_scaled * jnp.repeat(head_scale, model // head_count)).astype(jnp.bfloat16)
    head_columns = jnp.sum(grad_scaled * scaled_low.astype(jnp.float32), 0)
    head_term = jnp.sum(head_columns.reshape(head_count, -1), -1) / head_scale
    grad_attended = sequence(grad_attended)

    dquery, dkeys, dvalues = attend_back(
        first, head_scale, query, keys, values, start, lse, scaled, stacked(grad_attended), hops
    )
    query_low, *pairs = sequence(flat(dquery), *[flat(d) for d in dkeys], *[flat(d) for d in dvalues])
    down_sum.step(sequence)
    up_sum.step(sequence)
    query_low, *pairs = sequence(query_low, *pairs)
    dkeys, dvalues = pairs[: len(keys)], pairs[len(keys) :]
    back = lambda dkey, dvalue: dot_nt(dkey, inward[:, model : 2 * model]) + dot_nt(dvalue, inward[:, 2 * model :])
    lower = lambda array: lax.ppermute(array, "seq", downward)
    partials = [None] * len(hops)
    carried = None
    if hops:
        partials[-1] = back(dkeys[-1], dvalues[-1])
        carried = lower(sequence(stacked(partials[-1]).astype(jnp.bfloat16)))
    for hop in range(len(hops) - 1):
        partials[hop] = back(*sequence(dkeys[hop + 1], dvalues[hop + 1]))
    for hop in reversed(range(len(hops) - 1)):
        carried, partial = sequence(carried, partials[hop])
        partial = stacked(partial)
        missing = partial.shape[1] - carried.shape[1]
        going = partial + jnp.pad(carried.astype(jnp.float32), ((0, 0), (missing, 0), (0, 0)))
        carried = lower(sequence(going.astype(jnp.bfloat16)))

    picked_scaled = pick_columns(scaled_low, core)
    query_low, grad_branch, *pairs = sequence(query_low, grad_branch, *dkeys, *dvalues)
    dkeys, dvalues = pairs[: len(dkeys)], pairs[len(dkeys) :]

    def four(side):
        return (
            dot_tn(picked[0][side], query_low),
            sum(dot_tn(p[side], d) for p, d in zip(picked, dkeys)),
            sum(dot_tn(p[side], d) for p, d in zip(picked, dvalues)),
            dot_tn(picked_scaled[side], grad_branch),
        )

    sent = sequence(jnp.concatenate([part.astype(jnp.bfloat16) for part in four(0)], 1))
    came = exchange(sent, *core)

    def join(row_sums, width):
        for row_sum in row_sums:
            while row_sum.total is None:
                row_sum.step(sequence)
        joint = RowSum(bits_of("seq"))
        joint.left = bits_of("seq")[::-1]
        pieces = [piece for row_sum in row_sums for piece in lay_rows(row_sum.total, width, ranks)]
        joint.send(jnp.concatenate(pieces, 1).reshape(-1, width), sequence)
        return joint

    outer = join([down_sum, up_sum], model)
    query_low, grad_branch, *pairs = sequence(query_low, grad_branch, *dkeys, *dvalues)
    dkeys, dvalues = pairs[: len(dkeys)], pairs[len(dkeys) :]
    for index, row_sum in enumerate(sums):
        columns = slice(2 * index * model, 2 * (index + 1) * model)
        row_sum.begin(came[:, columns])
        row_sum.kept = lambda index=index: jnp.concatenate(four(1)[2 * index : 2 * (index + 1)], 1)
        row_sum.step(sequence)

    query_low, dkeys[0], dvalues[0] = sequence(query_low, dkeys[0], dvalues[0])
    own = (
        dot_nt(query_low, inward[:, :model])
        + dot_nt(dkeys[0], inward[:, model : 2 * model])
        + dot_nt(dvalues[0], inward[:, 2 * model :])
    )
    own = sequence(own)
    for row_sum in sums:
        row_sum.step(sequence)
    outer.step(sequence)
    own = sequence(own)
    vector = jnp.concatenate(
        [
            head_term,
            jnp.sum(grad_branch.astype(jnp.float32), 0),
            jnp.sum(grad_middle * hat_post, 0),
            jnp.sum(grad_middle, 0),
            jnp.sum(grad_second * hat_two, 0),
            jnp.sum(grad_second, 0),
            jnp.sum(grad_out, 0),
            jnp.sum(own * hat_one, 0) + sum(jnp.sum(p * h, 0) for p, h in zip(partials, hats[1:])),
            jnp.sum(own, 0) + sum(jnp.sum(p, 0) for p in partials),
            jnp.sum(query_low.astype(jnp.float32), 0),
            sum(jnp.sum(d.astype(jnp.float32), 0) for d in dvalues),
            jnp.sum(grad_upper.astype(jnp.float32), 0),
            jnp.sum(grad_mixed * hat_middle, 0),
            jnp.sum(grad_mixed, 0),
        ]
    )
    places = bits_of("seq") + bits_of("dp")
    vector = sequence(vector)
    vector_came = exchange(vector, *places.pop(0))

    def add_vector(vector, vector_came):
        if vector_came is not None:
            vector = sequence(vector + vector_came)
            vector_came = exchange(vector, *places.pop(0)) if places else None
        return vector, vector_came

    grad_normed = own
    if hops:
        carried, own = sequence(carried, own)
        grad_normed = own + flat(jnp.pad(carried.astype(jnp.float32), ((0, 0), (rows - carried.shape[1], 0), (0, 0))))
    vector, vector_came = add_vector(vector, vector_came)
    inner = join(sums, 2 * model)
    vector, vector_came = add_vector(vector, vector_came)
    grad_normed, mixed, middle = sequence(grad_normed, mixed, middle)
    input_grad = (grad_middle + norm_back(hat_one, scale_one, first_gain, grad_normed)).astype(jnp.bfloat16)
    input_grad = sequence(input_grad)
    vector, vector_came = add_vector(vector, vector_came)
    mixed, middle = sequence(mixed, middle)
    layer_output = (middle + dot_nn(mixed, down_full) + down_bias).astype(jnp.bfloat16)
    layer_output = sequence(layer_output)
    inner.step(sequence)
    while vector_came is not None:
        vector, vector_came = add_vector(vector, vector_came)
    for joint in (outer, inner):
        while joint.total is None:
            joint.step(sequence)
    vectors = vector + sequence.token[0, 0]

    share = down_weight.shape[0]
    down_total, outer_total = outer.total[:share], outer.total[share:]
    up_total = jnp.concatenate(jnp.split(outer_total, hidden // model), 1)
    query_key, value_output = jnp.split(inner.total, 2)
    rest = vectors[head_count:]
    narrow = rest[: 10 * model].reshape(10, model)
    broad = rest[10 * model :].reshape(3, hidden)
    return (
        stacked(layer_output),
        stacked(input_grad),
        query_key[:, :model],
        query_key[:, model:],
        value_output[:, :model],
        value_output[:, model:],
        up_total,
        down_total,
        narrow[6],
        narrow[7],
        narrow[8],
        narrow[9],
        vectors[:head_count],
        narrow[0],
        narrow[1],
        narrow[2],
        narrow[3],
        narrow[4],
        broad[0],
        broad[1],
        broad[2],
        narrow[5],
    )


def solution(mesh):
    sharded, matrix = P("dp", "seq", None), P(BOTH, None)
    in_specs = (sharded, sharded, P("dp", None)) + (matrix,) * 6 + (P(),) * 14
    out_specs = (sharded, sharded) + (matrix,) * 6 + (P(),) * 14
    return jax.shard_map(local, mesh=mesh, in_specs=in_specs, out_specs=out_specs, check_vma=False)
```

```python
import functools

import jax
import jax.numpy as jnp
from jax import lax
from jax.experimental import pallas as pl
from jax.experimental.pallas import tpu as pltpu
from jax.sharding import PartitionSpec as P

EPSILON = 1e-05
MASKED = -1e30
DOCUMENT_MAX = 800
BLOCK = 256
LANES = 256
BOTH = ("dp", "seq")


def dot_nn(a, b):
    return lax.dot_general(a, b, (((1,), (0,)), ((), ())), preferred_element_type=jnp.float32)


def dot_nt(a, b):
    return lax.dot_general(a, b, (((1,), (1,)), ((), ())), preferred_element_type=jnp.float32)


def dot_tn(a, b):
    return lax.dot_general(a, b, (((0,), (0,)), ((), ())), preferred_element_type=jnp.float32)


def moments(values):
    row_mean = jnp.mean(values, -1, keepdims=True)
    centred = values - row_mean
    spread = jnp.mean(centred * centred, -1, keepdims=True)
    scale = lax.rsqrt(spread + EPSILON)
    return centred * scale, scale


def norm_back(hat, scale, gain, grad):
    weighted = gain * grad
    first = jnp.mean(weighted, -1, keepdims=True)
    second = jnp.mean(weighted * hat, -1, keepdims=True)
    return scale * (weighted - first - hat * second)


def pick_lanes(block, head, width):
    lane = lax.broadcasted_iota(jnp.int32, block.shape, 1)
    inside = (lane >= head * width) & (lane < (head + 1) * width)
    return jnp.where(inside, block, jnp.zeros_like(block))


def key_blocks(rows, hops):
    blocks = []
    for block in range(rows // BLOCK):
        blocks.append((0, block * BLOCK, BLOCK, block * BLOCK))
    place = 0
    for hop, hop_rows in enumerate(hops):
        place -= hop_rows
        if hop_rows % BLOCK == 0:
            for block in reversed(range(hop_rows // BLOCK)):
                blocks.append((hop + 1, block * BLOCK, BLOCK, place + block * BLOCK))
        else:
            blocks.append((hop + 1, 0, hop_rows, place))
    return blocks


def mask_scores(scores, first_key, start_row, first_query, diagonal):
    place = first_key + lax.broadcasted_iota(jnp.int32, scores.shape, 0)
    ok = place >= start_row
    if diagonal:
        ok = ok & (place <= first_query + lax.broadcasted_iota(jnp.int32, scores.shape, 1))
    return jnp.where(ok, scores, MASKED)


def attend_kernel(pieces, hops, heads, width, factor, first_ref, scale_ref, q_ref, *refs):
    keys, values = refs[:pieces], refs[pieces : 2 * pieces]
    start_ref, out_ref, lse_ref, qh_ref, m_ref, l_ref, acc_ref = refs[2 * pieces :]
    sequence, group = pl.program_id(0), pl.program_id(1)
    rows = q_ref.shape[1]
    blocks = key_blocks(rows, hops)
    for qi in range(rows // BLOCK):
        first_query = qi * BLOCK
        first = first_ref[sequence, qi]
        start_row = start_ref[0, :, first_query : first_query + BLOCK]
        q_block = q_ref[0, first_query : first_query + BLOCK, :] * factor
        for head in range(heads):
            qh_ref[head] = pick_lanes(q_block, head, width)

        def body(piece, offset, count, place, fresh):
            key = keys[piece][0, offset : offset + count, :]
            value_t = values[piece][0, offset : offset + count, :].T
            for head in range(heads):
                scores = dot_nt(key, qh_ref[head])
                scores = mask_scores(scores, place, start_row, first_query, fresh)
                top = jnp.max(scores, 0, keepdims=True)
                lanes = slice(head * width, (head + 1) * width)
                if fresh:
                    weights = jnp.exp(scores - top)
                    l_ref[head : head + 1] = jnp.sum(weights, 0, keepdims=True)
                    acc_ref[lanes] = dot_nn(value_t[lanes], weights.astype(jnp.bfloat16))
                    m_ref[head : head + 1] = top
                else:
                    before = m_ref[head : head + 1]
                    top = jnp.maximum(before, top)
                    fade = jnp.exp(before - top)
                    weights = jnp.exp(scores - top)
                    l_ref[head : head + 1] = l_ref[head : head + 1] * fade + jnp.sum(weights, 0, keepdims=True)
                    acc_ref[lanes] = acc_ref[lanes] * fade + dot_nn(value_t[lanes], weights.astype(jnp.bfloat16))
                    m_ref[head : head + 1] = top

        body(*blocks[qi], True)
        for block in reversed(blocks[:qi]):
            pl.when(first < block[3] + block[2])(functools.partial(body, *block, False))
        for block in blocks[rows // BLOCK :]:
            pl.when(first < block[3] + block[2])(functools.partial(body, *block, False))
        total = l_ref[...]
        lse_ref[0, 0, :, first_query : first_query + BLOCK] = m_ref[...] + jnp.log(total)
        for head in range(heads):
            lanes = slice(head * width, (head + 1) * width)
            acc_ref[lanes] = acc_ref[lanes] * (scale_ref[group * heads + head] / total[head : head + 1])
        out_ref[0, first_query : first_query + BLOCK, :] = acc_ref[...].T.astype(jnp.bfloat16)


def attention_cost(sequences, rows, counts, head_count, model, products):
    pairs = sequences * head_count * rows * sum(counts)
    return pl.CostEstimate(
        flops=2 * products * pairs * LANES,
        bytes_accessed=4 * products * sequences * sum(counts) * model,
        transcendentals=pairs,
    )


def attend(first, head_scale, query, keys, values, start, hops):
    sequences, rows, model = query.shape
    head_count = head_scale.shape[0]
    width = model // head_count
    heads = LANES // width
    groups = model // LANES
    pieces = len(keys)
    wide = lambda count: pl.BlockSpec((1, count, LANES), lambda s, g, *_: (s, 0, g))
    counts = [k.shape[1] for k in keys]
    kernel = functools.partial(attend_kernel, pieces, hops, heads, width, width ** (-0.5))
    return pl.pallas_call(
        kernel,
        grid_spec=pltpu.PrefetchScalarGridSpec(
            num_scalar_prefetch=2,
            grid=(sequences, groups),
            in_specs=[wide(rows)] + [wide(c) for c in counts] * 2
            + [pl.BlockSpec((1, 1, rows), lambda s, g, *_: (s, 0, 0))],
            out_specs=[wide(rows), pl.BlockSpec((1, 1, heads, rows), lambda s, g, *_: (s, g, 0, 0))],
            scratch_shapes=[
                pltpu.VMEM((heads, BLOCK, LANES), jnp.bfloat16),
                pltpu.VMEM((heads, BLOCK), jnp.float32),
                pltpu.VMEM((heads, BLOCK), jnp.float32),
                pltpu.VMEM((LANES, BLOCK), jnp.float32),
            ],
        ),
        out_shape=[
            jax.ShapeDtypeStruct((sequences, rows, model), jnp.bfloat16),
            jax.ShapeDtypeStruct((sequences, groups, heads, rows), jnp.float32),
        ],
        name="attend",
        cost_estimate=attention_cost(sequences, rows, counts, head_count, model, 3),
    )(first, head_scale, query, *keys, *values, start)


def attend_back_kernel(pieces, hops, heads, width, factor, first_ref, scale_ref, q_ref, *refs):
    keys, values = refs[:pieces], refs[pieces : 2 * pieces]
    start_ref, lse_ref, out_ref, grad_ref = refs[2 * pieces : 2 * pieces + 4]
    dq_ref = refs[2 * pieces + 4]
    dkeys = refs[2 * pieces + 5 : 3 * pieces + 5]
    dvalues = refs[3 * pieces + 5 : 4 * pieces + 5]
    qh_ref, gh_ref, delta_ref, p_ref, ds_ref, dq_acc, dk_acc, dv_acc = refs[4 * pieces + 5 :]
    sequence, group = pl.program_id(0), pl.program_id(1)
    rows = q_ref.shape[1]
    query_blocks = rows // BLOCK
    for qi in range(query_blocks):
        here = slice(qi * BLOCK, (qi + 1) * BLOCK)
        q_block = q_ref[0, here, :] * factor
        grad = grad_ref[0, here, :]
        product = (grad.astype(jnp.float32) * out_ref[0, here, :].astype(jnp.float32)).T
        for head in range(heads):
            lanes = slice(head * width, (head + 1) * width)
            spot = slice(head * BLOCK, (head + 1) * BLOCK)
            qh_ref[qi, spot] = pick_lanes(q_block, head, width)
            gh_ref[qi, spot] = pick_lanes(grad, head, width)
            delta_ref[head : head + 1, here] = jnp.sum(product[lanes], 0, keepdims=True) / scale_ref[group * heads + head]
    dq_acc[...] = jnp.zeros_like(dq_acc)
    for piece, offset, count, place in key_blocks(rows, hops):
        key = keys[piece][0, offset : offset + count, :]
        key_t = key.T
        value = values[piece][0, offset : offset + count, :]
        dk_acc[:count] = jnp.zeros((count, LANES), jnp.float32)
        dv_acc[:count] = jnp.zeros((count, LANES), jnp.float32)
        for qi in range(query_blocks):
            first_query = qi * BLOCK
            if place > first_query:
                continue

            def body():
                here = slice(first_query, first_query + BLOCK)
                start_row = start_ref[0, :, here]
                for head in range(heads):
                    lanes = slice(head * width, (head + 1) * width)
                    spot = slice(head * BLOCK, (head + 1) * BLOCK)
                    scores = dot_nt(key, qh_ref[qi, spot])
                    scores = mask_scores(scores, place, start_row, first_query, place == first_query)
                    weights = jnp.exp(scores - lse_ref[0, 0, head : head + 1, here])
                    dweights = dot_nt(value, gh_ref[qi, spot])
                    dscores = (weights * (dweights - delta_ref[head : head + 1, here])).astype(jnp.bfloat16)
                    p_ref[:count, spot] = weights.astype(jnp.bfloat16)
                    ds_ref[:count, spot] = dscores
                    dq_acc[lanes, here] += dot_nn(key_t[lanes], dscores)
                dv_acc[:count] += dot_nn(p_ref[:count], gh_ref[qi])
                dk_acc[:count] += dot_nn(ds_ref[:count], qh_ref[qi])

            if place == first_query:
                body()
            else:
                pl.when(first_ref[sequence, qi] < place + count)(body)
        dkeys[piece][0, offset : offset + count, :] = dk_acc[:count].astype(jnp.bfloat16)
        dvalues[piece][0, offset : offset + count, :] = dv_acc[:count].astype(jnp.bfloat16)
    for qi in range(query_blocks):
        here = slice(qi * BLOCK, (qi + 1) * BLOCK)
        dq_ref[0, here, :] = (dq_acc[:, here] * factor).T.astype(jnp.bfloat16)


def attend_back(first, head_scale, query, keys, values, start, lse, scaled, grad, hops):
    sequences, rows, model = query.shape
    head_count = head_scale.shape[0]
    width = model // head_count
    heads = LANES // width
    groups = model // LANES
    pieces = len(keys)
    wide = lambda count: pl.BlockSpec((1, count, LANES), lambda s, g, *_: (s, 0, g))
    counts = [k.shape[1] for k in keys]
    most = max([BLOCK] + [c for c in counts if c % BLOCK])
    kernel = functools.partial(attend_back_kernel, pieces, hops, heads, width, width ** (-0.5))
    shape = lambda count: jax.ShapeDtypeStruct((sequences, count, model), jnp.bfloat16)
    results = pl.pallas_call(
        kernel,
        grid_spec=pltpu.PrefetchScalarGridSpec(
            num_scalar_prefetch=2,
            grid=(sequences, groups),
            in_specs=[wide(rows)] + [wide(c) for c in counts] * 2
            + [
                pl.BlockSpec((1, 1, rows), lambda s, g, *_: (s, 0, 0)),
                pl.BlockSpec((1, 1, heads, rows), lambda s, g, *_: (s, g, 0, 0)),
                wide(rows),
                wide(rows),
            ],
            out_specs=[wide(rows)] + [wide(c) for c in counts] * 2,
            scratch_shapes=[
                pltpu.VMEM((rows // BLOCK, heads * BLOCK, LANES), jnp.bfloat16),
                pltpu.VMEM((rows // BLOCK, heads * BLOCK, LANES), jnp.bfloat16),
                pltpu.VMEM((heads, rows), jnp.float32),
                pltpu.VMEM((most, heads * BLOCK), jnp.bfloat16),
                pltpu.VMEM((most, heads * BLOCK), jnp.bfloat16),
                pltpu.VMEM((LANES, rows), jnp.float32),
                pltpu.VMEM((most, LANES), jnp.float32),
                pltpu.VMEM((most, LANES), jnp.float32),
            ],
        ),
        out_shape=[shape(rows)] + [shape(c) for c in counts] * 2,
        name="attend_back",
        cost_estimate=attention_cost(sequences, rows, counts, head_count, model, 5),
    )(first, head_scale, query, *keys, *values, start, lse, scaled, grad)
    return results[0], results[1 : 1 + pieces], results[1 + pieces :]


def halo_rows(rows, ranks):
    hops, left = [], DOCUMENT_MAX - 1
    for _ in range(ranks - 1):
        if left <= 0:
            break
        hops.append(min(rows, -(-left // 32) * 32))
        left -= rows
    return hops


def bits_of(axis):
    return [(axis, bit) for bit in range(lax.axis_size(axis).bit_length() - 1)]


def exchange(array, axis, bit):
    return lax.ppermute(array, axis, [(i, i ^ (1 << bit)) for i in range(lax.axis_size(axis))])


def together(*values):
    return lax.optimization_barrier(values)


def pick_kernel(mine_ref, array_ref, other_ref, own_ref):
    width = own_ref.shape[1]
    halves = array_ref[:, :width], array_ref[:, width:]
    for index in range(2):
        @pl.when(mine_ref[0] == index)
        def _():
            own_ref[...] = halves[index]
            other_ref[...] = halves[1 - index]


def pick_columns(array, place):
    axis, bit = place
    order = bits_of("dp")[::-1] + bits_of("seq")[::-1]
    mine = (lax.axis_index(axis) >> bit) & 1
    tokens, columns = array.shape
    above = 1 << order.index(place)
    width = columns // above // 2
    if width % 128:
        split = array.reshape(tokens, above, 2, width)
        take = lambda index: lax.dynamic_index_in_dim(split, index, 2, keepdims=False).reshape(tokens, -1)
        return take(1 - mine), take(mine)
    half = jax.ShapeDtypeStruct((tokens, columns // 2), array.dtype)
    return pl.pallas_call(
        pick_kernel,
        grid_spec=pltpu.PrefetchScalarGridSpec(
            num_scalar_prefetch=1,
            grid=(above,),
            in_specs=[pl.BlockSpec((tokens, 2 * width), lambda block, _: (0, block))],
            out_specs=[pl.BlockSpec((tokens, width), lambda block, _: (0, block))] * 2,
        ),
        out_shape=[half, half],
        name="pick",
        cost_estimate=pl.CostEstimate(flops=0, bytes_accessed=4 * array.size * array.dtype.itemsize, transcendentals=0),
    )(mine.reshape(1), array)


class Sequence:
    def __init__(self, token):
        self.token = token

    def __call__(self, *values):
        *values, self.token = together(*values, self.token)
        return values[0] if len(values) == 1 else values


def lay_rows(total, width, shares):
    total = total.astype(jnp.bfloat16)
    return [total[:, left : left + width].reshape(shares, -1, width) for left in range(0, total.shape[1], width)]


class RowSum:
    def __init__(self, order):
        self.order = list(order)
        self.left = bits_of("dp")[::-1] + bits_of("seq")[::-1]
        self.came = self.kept = self.total = None

    def begin(self, came):
        self.left.remove(self.order.pop(0))
        self.came = came

    def step(self, sequence):
        came, kept = sequence(self.came), self.kept()
        total = kept.astype(jnp.float32) + came.reshape(kept.shape).astype(jnp.float32)
        total = total.reshape(-1, total.shape[-1])
        if not self.order:
            self.total = total
            return
        self.send(total, sequence)

    def send(self, total, sequence):
        axis, bit = self.order.pop(0)
        at = self.left.index((axis, bit))
        self.left.pop(at)
        total = total.astype(jnp.bfloat16)
        columns = total.shape[-1]
        split = total.reshape(1 << at, 2, -1, columns)
        mine = (lax.axis_index(axis) >> bit) & 1
        take = lambda rows, index: lax.dynamic_index_in_dim(rows, index, 1, keepdims=False)
        gone, split = sequence(take(split, 1 - mine).reshape(-1, columns), split)
        self.kept = lambda: take(split, mine)
        self.came = exchange(gone, axis, bit)


def local(
    inputs,
    cotangent,
    segment_ids,
    query_weight,
    key_weight,
    value_weight,
    output_weight,
    up_weight,
    down_weight,
    first_gain,
    first_shift,
    query_bias,
    value_bias,
    head_scale,
    output_bias,
    post_gain,
    post_shift,
    second_gain,
    second_shift,
    up_bias,
    middle_gain,
    middle_shift,
    down_bias,
):
    sequences, rows, model = inputs.shape
    hidden = up_bias.shape[0]
    head_count = head_scale.shape[0]
    ranks = lax.axis_size("seq")
    rank = lax.axis_index("seq")
    hops = halo_rows(rows, ranks)
    upward = [(i, i + 1) for i in range(ranks - 1)]
    downward = [(i + 1, i) for i in range(ranks - 1)]

    halos = []
    if hops:
        onward = hops[1] if len(hops) > 1 else hops[0]
        shift = lambda array: lax.ppermute(array, "seq", upward)
        moving = shift(inputs[:, rows - onward :])
        nearest = moving
        if onward < hops[0]:
            rest, moving = together(inputs[:, rows - hops[0] : rows - onward], moving)
            nearest = jnp.concatenate([shift(rest), moving], 1)
        halos.append(nearest)
        for hop_rows in hops[1:]:
            moving = shift(moving[:, moving.shape[1] - hop_rows :])
            halos.append(moving)

    inward = jnp.concatenate([query_weight, key_weight, value_weight], 1)
    inward = lax.all_gather(inward, BOTH, axis=0, tiled=True)
    outward = lax.all_gather(jnp.concatenate([output_weight, up_weight], 1), BOTH, axis=0, tiled=True)
    down_full = lax.all_gather(down_weight, BOTH, axis=0, tiled=True)
    output_full, up_full = outward[:, :model], outward[:, model:]

    own_ids = lax.dynamic_slice_in_dim(segment_ids, rank * rows, rows, 1)
    start = jnp.sum((segment_ids[:, None, :] < own_ids[:, :, None]).astype(jnp.int32), -1) - rank * rows
    first = start[:, ::BLOCK]
    start = start[:, None, :]

    flat = lambda array: array.reshape(-1, array.shape[-1])
    tokens = flat(inputs).astype(jnp.float32)
    hat_one, scale_one = moments(tokens)
    normed = (hat_one * first_gain + first_shift).astype(jnp.bfloat16)
    projected = dot_nn(normed, inward)
    stacked = lambda array: array.reshape(sequences, -1, array.shape[-1])
    query = stacked((projected[:, :model] + query_bias).astype(jnp.bfloat16))
    keys = [stacked(projected[:, model : 2 * model].astype(jnp.bfloat16))]
    values = [stacked((projected[:, 2 * model :] + value_bias).astype(jnp.bfloat16))]
    core, *planes = bits_of("dp")
    normed_pieces, hats = [normed], [hat_one]
    for halo in halos:
        halo, query, keys[-1], values[-1] = together(halo, query, keys[-1], values[-1])
        hat, _ = moments(flat(halo).astype(jnp.float32))
        piece = (hat * first_gain + first_shift).astype(jnp.bfloat16)
        normed_pieces.append(piece)
        hats.append(hat)
        both = dot_nn(piece, inward[:, model:])
        keys.append(stacked(both[:, :model].astype(jnp.bfloat16)))
        values.append(stacked((both[:, model:] + value_bias).astype(jnp.bfloat16)))
    scaled, lse = attend(first, head_scale, query, keys, values, start, hops)

    scaled_low, *normed_pieces = together(flat(scaled), *normed_pieces)
    branch = dot_nn(scaled_low, output_full) + output_bias
    hat_post, scale_post = moments(branch)
    middle = tokens + hat_post * post_gain + post_shift
    hat_two, scale_two = moments(middle)
    second = (hat_two * second_gain + second_shift).astype(jnp.bfloat16)
    upper = dot_nn(second, up_full) + up_bias
    phi = 0.5 * (1.0 + lax.erf(upper * 0.7071067811865476))
    bent = upper * phi
    bent_mean = jnp.mean(bent, -1, keepdims=True)
    bent_spread = jnp.maximum(jnp.mean(bent * bent, -1, keepdims=True) - bent_mean * bent_mean, 0.0)
    scale_middle = lax.rsqrt(bent_spread + EPSILON)
    hat_middle = (bent - bent_mean) * scale_middle
    mixed = (hat_middle * middle_gain + middle_shift).astype(jnp.bfloat16)
    grad_low = flat(cotangent)
    grad_out = grad_low.astype(jnp.float32)
    one_way, other_way = [core, *reversed(planes)], [core, *planes]

    down_sum, up_sum = RowSum(one_way), RowSum(other_way)
    sums = query_key_sum, value_output_sum = RowSum(one_way), RowSum(other_way)
    sequence = Sequence(jnp.zeros((8, 128), jnp.float32))
    down_sum.send(dot_tn(mixed, grad_low), sequence)

    picked = [sequence(*pick_columns(piece, core)) for piece in (*normed_pieces, scaled_low)]
    *picked, picked_scaled = picked

    low = sequence(grad_low)
    grad_mixed = dot_nt(low, down_full)
    slope = phi + upper * (0.3989422804014327 * jnp.exp(-0.5 * upper * upper))
    grad_upper = (norm_back(hat_middle, scale_middle, middle_gain, grad_mixed) * slope).astype(jnp.bfloat16)
    grad_upper = sequence(grad_upper)
    down_sum.step(sequence)
    up_sum.send(dot_tn(second, sequence(grad_upper)), sequence)
    grad_upper = sequence(grad_upper)
    grad_second = sequence(dot_nt(grad_upper, up_full))
    up_sum.step(sequence)
    grad_second = sequence(grad_second)
    grad_middle = grad_out + norm_back(hat_two, scale_two, second_gain, grad_second)
    grad_branch = norm_back(hat_post, scale_post, post_gain, grad_middle).astype(jnp.bfloat16)
    grad_branch = sequence(grad_branch)
    grad_scaled = dot_nt(grad_branch, output_full)
    grad_attended = (grad_scaled * jnp.repeat(head_scale, model // head_count)).astype(jnp.bfloat16)
    head_columns = jnp.sum(grad_scaled * scaled_low.astype(jnp.float32), 0)
    head_term = jnp.sum(head_columns.reshape(head_count, -1), -1) / head_scale
    grad_attended = sequence(grad_attended)

    dquery, dkeys, dvalues = attend_back(
        first, head_scale, query, keys, values, start, lse, scaled, stacked(grad_attended), hops
    )
    query_low, *pairs = sequence(flat(dquery), *[flat(d) for d in dkeys], *[flat(d) for d in dvalues])
    down_sum.step(sequence)
    up_sum.step(sequence)
    query_low, *pairs = sequence(query_low, *pairs)
    dkeys, dvalues = pairs[: len(keys)], pairs[len(keys) :]
    back = lambda dkey, dvalue: dot_nt(dkey, inward[:, model : 2 * model]) + dot_nt(dvalue, inward[:, 2 * model :])
    lower = lambda array: lax.ppermute(array, "seq", downward)
    partials = [None] * len(hops)
    carried = None
    if hops:
        partials[-1] = back(dkeys[-1], dvalues[-1])
        carried = lower(sequence(stacked(partials[-1]).astype(jnp.bfloat16)))
    for hop in range(len(hops) - 1):
        partials[hop] = back(*sequence(dkeys[hop + 1], dvalues[hop + 1]))
    for hop in reversed(range(len(hops) - 1)):
        carried, partial = sequence(carried, partials[hop])
        partial = stacked(partial)
        missing = partial.shape[1] - carried.shape[1]
        going = partial + jnp.pad(carried.astype(jnp.float32), ((0, 0), (missing, 0), (0, 0)))
        carried = lower(sequence(going.astype(jnp.bfloat16)))

    query_low, grad_branch, *pairs = sequence(query_low, grad_branch, *dkeys, *dvalues)
    dkeys, dvalues = pairs[: len(dkeys)], pairs[len(dkeys) :]

    def four(side):
        return (
            dot_tn(picked[0][side], query_low),
            sum(dot_tn(p[side], d) for p, d in zip(picked, dkeys)),
            sum(dot_tn(p[side], d) for p, d in zip(picked, dvalues)),
            dot_tn(picked_scaled[side], grad_branch),
        )

    sent = sequence(jnp.concatenate([part.astype(jnp.bfloat16) for part in four(0)], 1))
    came = exchange(sent, *core)

    def join(row_sums, width):
        for row_sum in row_sums:
            while row_sum.total is None:
                row_sum.step(sequence)
        joint = RowSum(bits_of("seq"))
        joint.left = bits_of("seq")[::-1]
        pieces = [piece for row_sum in row_sums for piece in lay_rows(row_sum.total, width, ranks)]
        joint.send(jnp.concatenate(pieces, 1).reshape(-1, width), sequence)
        return joint

    outer = join([down_sum, up_sum], model)
    query_low, grad_branch, *pairs = sequence(query_low, grad_branch, *dkeys, *dvalues)
    dkeys, dvalues = pairs[: len(dkeys)], pairs[len(dkeys) :]
    for index, row_sum in enumerate(sums):
        columns = slice(2 * index * model, 2 * (index + 1) * model)
        row_sum.begin(came[:, columns])
        row_sum.kept = lambda index=index: jnp.concatenate(four(1)[2 * index : 2 * (index + 1)], 1)
        row_sum.step(sequence)

    query_low, dkeys[0], dvalues[0] = sequence(query_low, dkeys[0], dvalues[0])
    own = (
        dot_nt(query_low, inward[:, :model])
        + dot_nt(dkeys[0], inward[:, model : 2 * model])
        + dot_nt(dvalues[0], inward[:, 2 * model :])
    )
    own = sequence(own)
    for row_sum in sums:
        row_sum.step(sequence)
    outer.step(sequence)
    own = sequence(own)
    vector = jnp.concatenate(
        [
            head_term,
            jnp.sum(grad_branch.astype(jnp.float32), 0),
            jnp.sum(grad_middle * hat_post, 0),
            jnp.sum(grad_middle, 0),
            jnp.sum(grad_second * hat_two, 0),
            jnp.sum(grad_second, 0),
            jnp.sum(grad_out, 0),
            jnp.sum(own * hat_one, 0) + sum(jnp.sum(p * h, 0) for p, h in zip(partials, hats[1:])),
            jnp.sum(own, 0) + sum(jnp.sum(p, 0) for p in partials),
            jnp.sum(query_low.astype(jnp.float32), 0),
            sum(jnp.sum(d.astype(jnp.float32), 0) for d in dvalues),
            jnp.sum(grad_upper.astype(jnp.float32), 0),
            jnp.sum(grad_mixed * hat_middle, 0),
            jnp.sum(grad_mixed, 0),
        ]
    )
    places = bits_of("dp") + bits_of("seq")
    vector = sequence(vector)
    vector_came = exchange(vector, *places.pop(0))

    def add_vector(vector, vector_came):
        if vector_came is not None:
            vector = sequence(vector + vector_came)
            vector_came = exchange(vector, *places.pop(0)) if places else None
        return vector, vector_came

    grad_normed = own
    if hops:
        carried, own = sequence(carried, own)
        grad_normed = own + flat(jnp.pad(carried.astype(jnp.float32), ((0, 0), (rows - carried.shape[1], 0), (0, 0))))
    vector, vector_came = add_vector(vector, vector_came)
    inner = join(sums, 2 * model)
    vector, vector_came = add_vector(vector, vector_came)
    grad_normed, mixed, middle = sequence(grad_normed, mixed, middle)
    input_grad = (grad_middle + norm_back(hat_one, scale_one, first_gain, grad_normed)).astype(jnp.bfloat16)
    input_grad = sequence(input_grad)
    vector, vector_came = add_vector(vector, vector_came)
    mixed, middle = sequence(mixed, middle)
    layer_output = (middle + dot_nn(mixed, down_full) + down_bias).astype(jnp.bfloat16)
    layer_output = sequence(layer_output)
    inner.step(sequence)
    while vector_came is not None:
        vector, vector_came = add_vector(vector, vector_came)
    for joint in (outer, inner):
        while joint.total is None:
            joint.step(sequence)
    vectors = vector + sequence.token[0, 0]

    share = down_weight.shape[0]
    down_total, outer_total = outer.total[:share], outer.total[share:]
    up_total = jnp.concatenate(jnp.split(outer_total, hidden // model), 1)
    query_key, value_output = jnp.split(inner.total, 2)
    rest = vectors[head_count:]
    narrow = rest[: 10 * model].reshape(10, model)
    broad = rest[10 * model :].reshape(3, hidden)
    return (
        stacked(layer_output),
        stacked(input_grad),
        query_key[:, :model],
        query_key[:, model:],
        value_output[:, :model],
        value_output[:, model:],
        up_total,
        down_total,
        narrow[6],
        narrow[7],
        narrow[8],
        narrow[9],
        vectors[:head_count],
        narrow[0],
        narrow[1],
        narrow[2],
        narrow[3],
        narrow[4],
        broad[0],
        broad[1],
        broad[2],
        narrow[5],
    )


def solution(mesh):
    sharded, matrix = P("dp", "seq", None), P(BOTH, None)
    in_specs = (sharded, sharded, P("dp", None)) + (matrix,) * 6 + (P(),) * 14
    out_specs = (sharded, sharded) + (matrix,) * 6 + (P(),) * 14
    return jax.shard_map(local, mesh=mesh, in_specs=in_specs, out_specs=out_specs, check_vma=False)
```
